32 devices in a mesh: dp: 32 (over z, y, x, core).
Axes of the slice: x: 2, y: 2, z: 4, core: 2. Of those that a mesh axis runs over, the one named last changes fastest.
Arguments:
- tokens: bfloat16 [16384, 768], P('dp'), may hold values from -6 to 6
- cotangent: bfloat16 [16384, 768], P('dp'), may hold values from -15 to 15
- seq_lengths: int32 [32, 2], P('dp'), may hold values from 0 to 512, as said below
- random_feat: bfloat16 [12, 64, 64], replicated, may hold values from -4 to 4
- w_qkv: float32 [768, 2304], P('dp'), may hold values from -0.21875 to 0.21875
- b_qkv: float32 [2304], P('dp'), may hold values from -1.5 to 1.5
- w_out: float32 [768, 768], P('dp'), may hold values from -0.875 to 0.875
- b_out: float32 [768], P('dp'), may hold values from -1.5 to 1.5
- ln1_gain: float32 [768], P('dp'), may hold values from 0.25 to 1.75
- ln1_bias: float32 [768], P('dp'), may hold values from -1.5 to 1.5
- w_up: float32 [768, 3072], P('dp'), may hold values from -0.21875 to 0.21875
- b_up: float32 [3072], P('dp'), may hold values from -1.5 to 1.5
- w_down: float32 [3072, 768], P('dp'), may hold values from -0.109375 to 0.109375
- b_down: float32 [768], P('dp'), may hold values from -1.5 to 1.5
- ln2_gain: float32 [768], P('dp'), may hold values from 0.25 to 1.75
- ln2_bias: float32 [768], P('dp'), may hold values from -1.5 to 1.5
- rpe_table: float32 [12288], P('dp'), may hold values from -2.5 to 2.5
Outputs:
- out: bfloat16 [16384, 768], P('dp')
- grad_tokens: float32 [16384, 768], P('dp')
- grad_w_qkv: float32 [768, 2304], P('dp')
- grad_b_qkv: float32 [2304], P('dp')
- grad_w_out: float32 [768, 768], P('dp')
- grad_b_out: float32 [768], P('dp')
- grad_ln1_gain: float32 [768], P('dp')
- grad_ln1_bias: float32 [768], P('dp')
- grad_w_up: float32 [768, 3072], P('dp')
- grad_b_up: float32 [3072], P('dp')
- grad_w_down: float32 [3072, 768], P('dp')
- grad_b_down: float32 [768], P('dp')
- grad_ln2_gain: float32 [768], P('dp')
- grad_ln2_bias: float32 [768], P('dp')
- grad_rpe: float32 [12288], P('dp')
The draws below stay inside these ranges and needn't reach their ends.
Inputs may be any that keep to these rules, and one draw needn't show every extreme that they name: `seq_lengths`: row n gives the lengths of the one or two sequences packed from the start of device n's 512 token slots; a second length of 0 means one sequence; the two lengths sum to 512 or less, and some row holds one sequence of exactly 512.
All inputs are finite; a program needn't handle non-finite values.
Results may differ from the reference program's by a relative error of at most 0.018.
Values may be sent and summed in bfloat16 or wider, within the bound.
A program may use at most 192 MiB of HBM per device.

```python
import jax
import jax.numpy as jnp
from jax import lax

D = 768
H = 12
DH = 64
M = 64
FF = 3072
TOK_DEV = 512
RPE_LEN = 1024
TOKENS = 16384


def draw_cotangent(key, part):
    block_count = TOKENS // TOK_DEV
    owner = (jnp.arange(TOKENS, dtype=jnp.int32) // TOK_DEV).astype(jnp.float32)
    factor = 1.0 + 2.0 * owner / max(block_count - 1, 1)
    base = jnp.clip(jax.random.normal(key, (TOKENS, D), jnp.float32), -5.0, 5.0)
    return (base * factor[:, None]).astype(jnp.bfloat16)


def draw_seq_lengths(key, part):
    block_count = TOKENS // TOK_DEV
    keys = jax.random.split(key, 5)
    places = jnp.arange(block_count, dtype=jnp.int32)
    chosen = jax.random.randint(keys[1], (), 0, block_count)
    single = (jax.random.randint(keys[0], (block_count,), 0, 5) < 2) | (places == chosen)
    whole = TOK_DEV - jax.random.randint(keys[2], (block_count,), 0, TOK_DEV // 8 + 1)
    whole = jnp.where(places == chosen, TOK_DEV, whole)
    first = jax.random.randint(keys[3], (block_count,), TOK_DEV // 4, TOK_DEV // 2 + 1)
    second = jax.random.randint(keys[4], (block_count,), TOK_DEV // 4, TOK_DEV // 2 + 1)
    leading = jnp.where(single, whole, first)
    trailing = jnp.where(single, 0, second)
    return jnp.stack([leading, trailing], axis=1).astype(jnp.int32)


def block_levels(stream_key, dims, shards, smallest, top_value):
    loudness = 1.0
    for dim, shards_of in shards:
        steps = jax.random.uniform(jax.random.fold_in(jax.random.fold_in(stream_key, 6), dim), (shards_of,), jnp.float32, smallest / len(shards), top_value / len(shards))
        loudness = loudness * jnp.repeat(jnp.exp(steps), dims[dim] // shards_of).reshape((-1,) + (1,) * (len(dims) - 1 - dim))
    return loudness


def noise(stream_key, shape, deviation, bound, cuts=(), kind=jnp.bfloat16):
    drawn = deviation * jax.random.normal(stream_key, shape, jnp.float32)
    if cuts:
        drawn = drawn * block_levels(stream_key, shape, cuts, -0.22, 0.18)
    return jnp.clip(drawn, -bound, bound).astype(kind)


def setup_inputs(seed: int = 0) -> dict:
    splits = jax.random.split(jax.random.key(seed), 18)
    return {
        "tokens": noise(splits[0], (TOKENS, D), 1.0, 6.0, ((0, 32),)),
        "cotangent": draw_cotangent(jax.random.fold_in(splits[17], 71), 0),
        "seq_lengths": draw_seq_lengths(jax.random.fold_in(splits[17], 71), 0),
        "random_feat": noise(splits[3], (H, DH, M), 1.0, 4.0),
        "w_qkv": noise(splits[4], (D, 3 * D), D ** -0.5, 0.21875, ((0, 32),), jnp.float32),
        "b_qkv": noise(splits[5], (3 * D,), 0.3, 1.5, ((0, 32),), jnp.float32),
        "w_out": noise(splits[6], (D, D), (D // 16) ** -0.5, 0.875, ((0, 32),), jnp.float32),
        "b_out": noise(splits[7], (D,), 0.3, 1.5, ((0, 32),), jnp.float32),
        "ln1_gain": jnp.clip(1.0 + 0.15 * jax.random.normal(splits[8], (D,), jnp.float32), 0.25, 1.75),
        "ln1_bias": noise(splits[9], (D,), 0.3, 1.5, ((0, 32),), jnp.float32),
        "w_up": noise(splits[10], (D, FF), D ** -0.5, 0.21875, ((0, 32),), jnp.float32),
        "b_up": noise(splits[11], (FF,), 0.3, 1.5, ((0, 32),), jnp.float32),
        "w_down": noise(splits[12], (FF, D), FF ** -0.5, 0.109375, ((0, 32),), jnp.float32),
        "b_down": noise(splits[13], (D,), 0.3, 1.5, ((0, 32),), jnp.float32),
        "ln2_gain": jnp.clip(1.0 + 0.15 * jax.random.normal(splits[14], (D,), jnp.float32), 0.25, 1.75),
        "ln2_bias": noise(splits[15], (D,), 0.3, 1.5, ((0, 32),), jnp.float32),
        "rpe_table": noise(splits[16], (H * RPE_LEN,), 0.5, 2.5, ((0, 32),), jnp.float32),
    }


HIGHEST = lax.Precision.HIGHEST
EPSILON = 1e-05

@jax.custom_vjp
def low(v):
    return lax.optimization_barrier(v.astype(jnp.bfloat16)).astype(jnp.float32)

@jax.custom_vjp
def low_back(v):
    return v

def low_keep(v):
    return (low(v), None)

def low_pass(kept, grad):
    return (grad,)

def back_keep(v):
    return (v, None)

def back_low(kept, grad):
    return (low(grad),)
low.defvjp(low_keep, low_pass)
low_back.defvjp(back_keep, back_low)

def layer_norm(value, gain, offset):
    centred = value - lax.optimization_barrier(jnp.mean(value, axis=-1, keepdims=True))
    inverse = lax.rsqrt(lax.optimization_barrier(jnp.mean(centred * centred, axis=-1, keepdims=True)) + EPSILON)
    return centred * inverse * gain + offset

def feature_map(part, projection):
    scaled = part * DH ** (-0.25)
    mapped = jnp.einsum('thd,hdm->thm', scaled, projection, precision=HIGHEST)
    squared = 0.5 * lax.optimization_barrier(jnp.sum(scaled * scaled, axis=-1, keepdims=True))
    return jnp.exp(mapped - squared) * M ** (-0.5)

def attend_head(elements, segment, offsets):
    query_feat, key_feat, values, table_row = elements
    kernel = low_back(jnp.dot(query_feat, key_feat.T, precision=HIGHEST))
    coefficient = jnp.exp(table_row[offsets])
    same = (segment[:, None] == segment[None, :]).astype(jnp.float32)
    scores = kernel * coefficient * same
    denominator = lax.optimization_barrier(jnp.sum(scores, axis=1))
    numerator = low_back(jnp.dot(low(scores), values, precision=HIGHEST))
    return numerator / denominator[:, None]

def layer(inputs, weights, projection, segment, offsets):
    w_qkv, b_qkv, w_out, b_out, gain_one, bias_one, w_up, b_up, w_down, b_down, gain_two, bias_two, rpe = tuple((low(piece) for piece in weights))
    qkv = low_back(jnp.dot(inputs, w_qkv, precision=HIGHEST)) + b_qkv
    query = qkv[:, :D].reshape(TOK_DEV, H, DH)
    key_part = qkv[:, D:2 * D].reshape(TOK_DEV, H, DH)
    value_part = qkv[:, 2 * D:].reshape(TOK_DEV, H, DH)
    query_feat = low(feature_map(query, projection)).transpose(1, 0, 2)
    key_feat = low(feature_map(key_part, projection)).transpose(1, 0, 2)
    values = low(value_part).transpose(1, 0, 2)
    table = rpe.reshape(H, RPE_LEN)
    head_step = jax.checkpoint(lambda elements: attend_head(elements, segment, offsets))
    context = lax.map(head_step, (query_feat, key_feat, values, table))
    context = context.transpose(1, 0, 2).reshape(TOK_DEV, D)
    attended = low_back(jnp.dot(low(context), w_out, precision=HIGHEST)) + b_out
    normed = layer_norm(inputs + attended, gain_one, bias_one)
    upward = low_back(jnp.dot(low(normed), w_up, precision=HIGHEST)) + b_up
    activated = jax.nn.gelu(upward, approximate=False)
    downward = low_back(jnp.dot(low(activated), w_down, precision=HIGHEST)) + b_down
    return layer_norm(normed + downward, gain_two, bias_two)

def reference(tokens, cotangent, seq_lengths, random_feat, w_qkv, b_qkv, w_out, b_out, ln1_gain, ln1_bias, w_up, b_up, w_down, b_down, ln2_gain, ln2_bias, rpe_table):
    weights = (w_qkv, b_qkv, w_out, b_out, ln1_gain, ln1_bias, w_up, b_up, w_down, b_down, ln2_gain, ln2_bias, rpe_table)
    projection = random_feat.astype(jnp.float32)
    block_count = TOKENS // TOK_DEV
    position = jnp.arange(TOK_DEV, dtype=jnp.int32)
    offsets = (position[:, None] - position[None, :] + RPE_LEN // 2).astype(jnp.int32)

    def visit(running, element):
        block_tokens, block_grad, lengths = element
        first_end = lengths[0]
        second_end = lengths[0] + lengths[1]
        segment = (position >= first_end).astype(jnp.int32) + (position >= second_end).astype(jnp.int32)
        valid = (position < second_end).astype(jnp.float32)

        def forward(inputs, *pieces):
            return layer(inputs, pieces, projection, segment, offsets)
        result, backward = jax.vjp(forward, block_tokens.astype(jnp.float32), *weights)
        grads = backward(block_grad.astype(jnp.float32) * valid[:, None])
        summed = tuple((total + piece for total, piece in zip(running, grads[1:])))
        return (summed, (result.astype(jnp.bfloat16), grads[0]))
    initial = tuple((jnp.zeros(piece.shape, jnp.float32) for piece in weights))
    totals, (results, grad_inputs) = lax.scan(visit, initial, (tokens.reshape(block_count, TOK_DEV, D), cotangent.reshape(block_count, TOK_DEV, D), seq_lengths))
    return (results.reshape(TOKENS, D), grad_inputs.reshape(TOKENS, D), totals[0], totals[1], totals[2], totals[3], totals[4], totals[5], totals[6], totals[7], totals[8], totals[9], totals[10], totals[11], totals[12])
```

```python
import functools

import jax
import jax.numpy as jnp
from jax import lax
from jax.experimental import pallas as pl
from jax.experimental.pallas import tpu as pltpu
from jax.sharding import PartitionSpec as P

EPSILON = 1e-05
F32 = jnp.float32
LOW = jnp.bfloat16
MESH = pl.DeviceIdType.MESH
MIB = 2**20


def mm(first_op, second_op, first_dim=1, second_dim=0):
    return lax.dot_general(
        first_op,
        second_op,
        (((first_dim,), (second_dim,)), ((), ())),
        preferred_element_type=F32,
    )


def mm2(value, weight, weight_dim=0):
    high = value.astype(LOW)
    rest = (value - high.astype(F32)).astype(LOW)
    return mm(high, weight, 1, weight_dim) + mm(rest, weight, 1, weight_dim)


def iota(shape, dim):
    return lax.broadcasted_iota(jnp.int32, shape, dim)


def cols(index, width):
    return pl.ds(pl.multiple_of(index * width, width), width)


def build_tables(seq_ref, feat_ref, mask_ref, block_ref, ones_ref):
    rows = mask_ref.shape[0]
    first_end = seq_ref[0, 0]
    second_end = first_end + seq_ref[0, 1]

    def segment(place):
        return (place >= first_end).astype(jnp.int32) + (place >= second_end).astype(jnp.int32)

    across = segment(iota((128, rows), 1))
    for start in range(0, rows, 128):
        down = segment(iota((128, rows), 0) + start)
        mask_ref[start : start + 128, :] = jnp.where(down == across, 1.0, 0.0)
    head_size = feat_ref.shape[1]
    breadth = ones_ref.shape[0]
    group = breadth // head_size
    bits = head_size.bit_length() - 1
    owner_row = lax.shift_right_logical(iota((breadth, breadth), 0), bits)
    owner_col = lax.shift_right_logical(iota((breadth, breadth), 1), bits)
    same = owner_row == owner_col
    ones_ref[...] = jnp.where(same, 1.0, 0.0).astype(LOW)
    for index in range(feat_ref.shape[0] // group):
        rows_of = []
        for inner in range(group):
            piece = feat_ref[index * group + inner].astype(F32)
            rows_of.append(jnp.concatenate([piece] * group, axis=1))
        full = jnp.concatenate(rows_of, axis=0)
        block_ref[index] = jnp.where(same, full, 0.0).astype(LOW)


def project(tokens_ref, w_ref, vec_ref, scaled_ref, phi_ref, low_ref, block_ref, ones_ref):
    breadth = tokens_ref.shape[1]
    tile = ones_ref.shape[0]
    per_part = breadth // tile
    scale = 64 ** (-0.25)

    def features(step, carry):
        where = cols(step, tile)
        acc = mm(tokens_ref[...], w_ref[:, where]) + vec_ref[0:1, where]
        scaled = acc * scale
        scaled_ref[:, where] = scaled
        block = block_ref[lax.rem(step, per_part)]
        mapped = mm2(scaled, block)
        squared = mm2(scaled * scaled, ones_ref[...])
        phi = jnp.exp(mapped - 0.5 * squared) * 0.125
        phi_ref[:, where] = phi
        low_ref[:, where] = phi.astype(LOW)
        return carry

    lax.fori_loop(0, 2 * per_part, features, 0)

    def plain(step, carry):
        where = cols(step + 2 * per_part, tile)
        acc = mm(tokens_ref[...], w_ref[:, where]) + vec_ref[0:1, where]
        low_ref[:, where] = acc.astype(LOW)
        return carry

    lax.fori_loop(0, per_part, plain, 0)


def coefficients(rpe_ref, head, coef_ref):
    flip = (iota((128, 128), 0) + iota((128, 128), 1) == 127).astype(F32).astype(LOW)
    raw = rpe_ref[pl.ds(pl.multiple_of(head * 8, 8), 8), :].astype(LOW)
    table = jnp.exp(mm(raw, flip))
    wide = jnp.concatenate(
        [jnp.broadcast_to(table[7 - k : 8 - k, :], (128, 128)) for k in range(8)], axis=1
    )
    coef_ref[...] = pltpu.roll(wide, 1024 - 127, axis=1, stride=1, stride_axis=0)


def attend(low_ref, rpe_ref, mask_ref, den_ref, ctx_ref, ctx_low_ref, coef_ref, key_ref):
    rows, breadth = ctx_ref.shape

    def pair_step(pair, carry):
        q_at = cols(pair, 128)
        k_at = pl.ds(pl.multiple_of(pair * 128 + breadth, 128), 128)
        v_at = pl.ds(pl.multiple_of(pair * 128 + 2 * breadth, 128), 128)
        lane = iota((128, 128), 1)
        for side in range(2):
            coefficients(rpe_ref, pair * 2 + side, coef_ref)
            mine = lane >= 64 if side else lane < 64
            keep_half(low_ref, k_at, key_ref, side)
            for block in range(rows // 128):
                at = slice(block * 128, block * 128 + 128)
                kernel = mm(low_ref[at, q_at], key_ref[...], 1, 1)
                lead = 128 * (rows // 128 - 1 - block)
                scores = kernel * (coef_ref[:, lead : lead + rows] * mask_ref[at, :])
                total = jnp.sum(scores, axis=1, keepdims=True)
                context = mm(scores.astype(LOW), low_ref[:, v_at]) * (1.0 / total)
                total = jnp.broadcast_to(total, (128, 128))
                if side == 0:
                    den_ref[at, q_at] = total
                    ctx_ref[at, q_at] = context
                else:
                    den_ref[at, q_at] = jnp.where(mine, total, den_ref[at, q_at])
                    context = jnp.where(mine, context, ctx_ref[at, q_at])
                    ctx_ref[at, q_at] = context
                    ctx_low_ref[at, q_at] = context.astype(LOW)
        return carry

    lax.fori_loop(0, breadth // 128, pair_step, 0)


def keep_half(low_ref, where, out_ref, side):
    rows = low_ref.shape[0]
    lane = iota((rows, 128), 1)
    mine = lane >= 64 if side else lane < 64
    out_ref[...] = jnp.where(mine, low_ref[:, where].astype(F32), 0.0).astype(LOW)


def forward_kernel(
    seq_ref, tokens_ref, feat_ref, w_ref, vec_ref, rpe_ref,
    scaled_ref, phi_ref, low_ref, den_ref, ctx_ref, ctx_low_ref,
    mask_ref, block_ref, ones_ref, coef_ref, key_ref,
):
    build_tables(seq_ref, feat_ref, mask_ref, block_ref, ones_ref)
    project(tokens_ref, w_ref, vec_ref, scaled_ref, phi_ref, low_ref, block_ref, ones_ref)
    attend(low_ref, rpe_ref, mask_ref, den_ref, ctx_ref, ctx_low_ref, coef_ref, key_ref)


def norm(value):
    centred = value - jnp.mean(value, axis=-1, keepdims=True)
    inverse = lax.rsqrt(jnp.mean(centred * centred, axis=-1, keepdims=True) + EPSILON)
    return centred * inverse, inverse


def norm_back(grad, xhat, inverse, gain):
    scaled = grad * gain
    mean = jnp.mean(scaled, axis=-1, keepdims=True)
    along = jnp.mean(scaled * xhat, axis=-1, keepdims=True)
    return inverse * (scaled - mean - xhat * along)


def add_to(ref, row, value):
    ref[row : row + 1, 0 : value.shape[1]] += value


def column_sum(value):
    return jnp.sum(value, axis=0, keepdims=True)


def middle_kernel(
    seq_ref, tokens_ref, cot_ref, ctx_low_ref, vec_ref, w_out_ref, w_up_ref, w_down_ref,
    out_ref, g_hidden_ref, g_ctx_ref, d_out_ref, d_up_ref, d_down_ref, gvec_ref,
    wide_ref, normed_ref, normed_low_ref, xhat_ref, inverse_ref, act_ref, slope_ref, g_sum_ref,
    g_low_ref, g_up_ref, flip_ref,
):
    rows, breadth = tokens_ref.shape
    hidden = w_up_ref.shape[1]
    height, tile = 128, 256
    blocks, tiles = rows // height, breadth // tile
    valid_rows = seq_ref[0, 0] + seq_ref[0, 1]
    gvec_ref[...] = jnp.zeros_like(gvec_ref)
    gain_one, bias_one = vec_ref[3:4, :breadth], vec_ref[4:5, :breadth]
    gain_two, bias_two = vec_ref[6:7, :breadth], vec_ref[7:8, :breadth]

    def rows_at(step):
        return pl.ds(pl.multiple_of(step * height, height), height)

    def loop(count, step):
        def run(index, carry):
            step(index)
            return carry

        lax.fori_loop(0, count, run, 0)

    def attended_step(step):
        where = cols(step, tile)
        wide_ref[:, where] = mm(ctx_low_ref[...], w_out_ref[:, where]) + vec_ref[2:3, where]

    loop(tiles, attended_step)

    def first_norm(step):
        at = rows_at(step)
        xhat, inverse = norm(tokens_ref[at, :].astype(F32) + wide_ref[at, :])
        xhat_ref[at, :] = xhat
        inverse_ref[at, :] = jnp.broadcast_to(inverse, (height, 128))
        normed = xhat * gain_one + bias_one
        normed_ref[at, :] = normed
        normed_low_ref[at, :] = normed.astype(LOW)

    loop(blocks, first_norm)

    def upward_step(step):
        where = cols(step, tile)
        upward = mm(normed_low_ref[...], w_up_ref[:, where]) + vec_ref[1:2, where]
        phi = 0.5 + 0.5 * lax.erf(upward * 0.5**0.5)
        density = jnp.exp(-0.5 * upward * upward) * 0.3989422804014327
        act_ref[:, where] = (upward * phi).astype(LOW)
        slope_ref[:, where] = phi + upward * density

    loop(hidden // tile, upward_step)

    def downward_step(step):
        where = cols(step, tile)
        wide_ref[:, where] = mm(act_ref[...], w_down_ref[:, where]) + vec_ref[5:6, where]

    loop(tiles, downward_step)

    def second_norm(step):
        at = rows_at(step)
        xhat, inverse = norm(normed_ref[at, :] + wide_ref[at, :])
        out_ref[at, :] = (xhat * gain_two + bias_two).astype(LOW)
        place = iota((height, breadth), 0) + step * height
        grad = jnp.where(place < valid_rows, cot_ref[at, :].astype(F32), 0.0)
        add_to(gvec_ref, 6, column_sum(grad * xhat))
        add_to(gvec_ref, 7, column_sum(grad))
        g_sum = norm_back(grad, xhat, inverse, gain_two)
        add_to(gvec_ref, 5, column_sum(g_sum))
        g_sum_ref[at, :] = g_sum
        g_low_ref[at, :] = g_sum.astype(LOW)

    loop(blocks, second_norm)
    flip_ref[...] = jnp.transpose(normed_low_ref[...])

    def down_step(step):
        where = cols(step, tile)
        g_upward = mm(g_low_ref[...], w_down_ref[where, :], 1, 1) * slope_ref[:, where]
        gvec_ref[1:2, where] = column_sum(g_upward)
        g_upward = g_upward.astype(LOW)
        g_up_ref[:, where] = g_upward
        d_down_ref[where, :] = mm(act_ref[:, where], g_low_ref[...], 0, 0).astype(LOW)
        d_up_ref[:, where] = mm(flip_ref[...], g_upward).astype(LOW)

    loop(hidden // tile, down_step)

    def up_back(step):
        where = cols(step, tile)
        wide_ref[:, where] = mm(g_up_ref[...], w_up_ref[where, :], 1, 1) + g_sum_ref[:, where]

    loop(tiles, up_back)

    def first_back(step):
        at = rows_at(step)
        g_normed = wide_ref[at, :]
        xhat = xhat_ref[at, :]
        add_to(gvec_ref, 3, column_sum(g_normed * xhat))
        add_to(gvec_ref, 4, column_sum(g_normed))
        g_hidden = norm_back(g_normed, xhat, inverse_ref[at, 0:1], gain_one)
        add_to(gvec_ref, 2, column_sum(g_hidden))
        g_hidden_ref[at, :] = g_hidden
        g_low_ref[at, :] = g_hidden.astype(LOW)

    loop(blocks, first_back)

    def out_back(step):
        where = cols(step, tile)
        g_ctx_ref[:, where] = mm(g_low_ref[...], w_out_ref[where, :], 1, 1)
        d_out_ref[where, :] = mm(ctx_low_ref[:, where], g_low_ref[...], 0, 0).astype(LOW)

    loop(tiles, out_back)


def diagonals(diag_ref, out_ref, head):
    value = diag_ref[...]
    height = value.shape[0]
    while height > 1:
        height //= 2
        value = value[height:] + pltpu.roll(value[:height], height, axis=1)
    for k in range(8):
        out_ref[pl.ds(head * 8 + 7 - k, 1), :] = value[:, 128 * k : 128 * k + 128]


def attend_back(
    low_ref, rpe_ref, mask_ref, den_ref, ctx_ref, g_ctx_ref,
    g_feat_ref, g_low_ref, gvec_ref, grpe_ref,
    coef_ref, scores_ref, gk_ref, diag_ref, query_ref, key_ref, value_ref, num_ref,
):
    rows, breadth = ctx_ref.shape

    def pair_step(pair, carry):
        q_at = cols(pair, 128)
        k_at = pl.ds(pl.multiple_of(pair * 128 + breadth, 128), 128)
        v_at = pl.ds(pl.multiple_of(pair * 128 + 2 * breadth, 128), 128)
        lane = iota((128, 128), 1)
        ones = jnp.ones((128, 128), LOW)
        for side in range(2):
            coefficients(rpe_ref, pair * 2 + side, coef_ref)
            mine = lane >= 64 if side else lane < 64
            other = 0 if side else 64
            keep_half(low_ref, q_at, query_ref, side)
            keep_half(low_ref, k_at, key_ref, side)
            keep_half(low_ref, v_at, value_ref, side)
            diag_ref[...] = jnp.zeros_like(diag_ref)
            is_high, is_rest = lane == other, lane == other + 1
            extra = jnp.where(jnp.logical_or(is_high, is_rest), 1.0, 0.0)
            for block in range(rows // 128):
                at = slice(block * 128, block * 128 + 128)
                value_ref[at, :] = (value_ref[at, :].astype(F32) + extra).astype(LOW)
            for block in range(rows // 128):
                at = slice(block * 128, block * 128 + 128)
                kernel = mm(low_ref[at, q_at], key_ref[...], 1, 1)
                g_num = jnp.where(mine, g_ctx_ref[at, q_at] * (1.0 / den_ref[at, q_at]), 0.0)
                g_den = -mm2(g_num * ctx_ref[at, q_at], ones)
                num_ref[at, :] = g_num.astype(LOW)
                high = g_den.astype(LOW).astype(F32)
                extended = jnp.where(is_high, high, jnp.where(is_rest, g_den - high, g_num))
                g_scores = mm(extended.astype(LOW), value_ref[...], 1, 1)
                lead = 128 * (rows // 128 - 1 - block)
                weight = coef_ref[:, lead : lead + rows] * mask_ref[at, :]
                scores = kernel * weight
                g_kernel = (g_scores * weight).astype(LOW)
                diag_ref[:, lead : lead + rows] += g_scores * scores
                scores_ref[at, :] = scores.astype(LOW)
                gk_ref[at, :] = g_kernel
                g_query = mm(g_kernel, key_ref[...])
                if side:
                    g_query = g_query + g_feat_ref[at, q_at]
                g_feat_ref[at, q_at] = g_query
            g_key = mm(gk_ref[...], query_ref[...], 0, 0)
            g_value = mm(scores_ref[...], num_ref[...], 0, 0)
            if side:
                g_key = g_key + g_feat_ref[:, k_at]
                g_value = g_value + g_feat_ref[:, v_at]
            g_feat_ref[:, k_at] = g_key
            g_feat_ref[:, v_at] = g_value
            diagonals(diag_ref, grpe_ref, pair * 2 + side)
        g_value = g_feat_ref[:, v_at]
        gvec_ref[0:1, v_at] = column_sum(g_value)
        g_low_ref[:, v_at] = g_value.astype(LOW)
        return carry

    lax.fori_loop(0, breadth // 128, pair_step, 0)
    flip = (jnp.where(iota((128, 128), 0) + iota((128, 128), 1) == 127, 1.0, 0.0)).astype(LOW)
    grpe_ref[...] = mm2(grpe_ref[...], flip)


def project_back(
    tokens_ref, w_ref, g_hidden_ref, phi_ref, scaled_ref, block_ref, ones_ref,
    g_feat_ref, g_low_ref, gvec_ref, g_tokens_ref, d_qkv_ref, flip_ref,
):
    breadth = tokens_ref.shape[1]
    tile = ones_ref.shape[0]
    per_part = breadth // tile
    scale = 64 ** (-0.25)

    def features(step, carry):
        where = cols(step, tile)
        upward = g_feat_ref[:, where] * phi_ref[:, where]
        total = mm2(upward, ones_ref[...])
        grad = mm2(upward, block_ref[lax.rem(step, per_part)], 1) - scaled_ref[:, where] * total
        grad = grad * scale
        gvec_ref[0:1, where] = column_sum(grad)
        g_low_ref[:, where] = grad.astype(LOW)
        return carry

    lax.fori_loop(0, 2 * per_part, features, 0)
    flip_ref[...] = jnp.transpose(tokens_ref[...])

    def weights(step, carry):
        where = cols(step, tile)
        d_qkv_ref[:, where] = mm(flip_ref[...], g_low_ref[:, where]).astype(LOW)
        return carry

    lax.fori_loop(0, 3 * per_part, weights, 0)

    def inputs(step, carry):
        where = cols(step, tile)
        g_tokens_ref[:, where] = mm(g_low_ref[...], w_ref[where, :], 1, 1) + g_hidden_ref[:, where]
        return carry

    lax.fori_loop(0, per_part, inputs, 0)


def backward_kernel(
    seq_ref, tokens_ref, feat_ref, w_ref, rpe_ref, scaled_ref, phi_ref, low_ref, den_ref, ctx_ref,
    g_ctx_ref, g_hidden_ref,
    g_tokens_ref, d_qkv_ref, gvec_ref, grpe_ref,
    mask_ref, block_ref, ones_ref, coef_ref, g_feat_ref, g_low_ref, scores_ref, gk_ref, diag_ref,
    query_ref, key_ref, value_ref, num_ref, flip_ref,
):
    build_tables(seq_ref, feat_ref, mask_ref, block_ref, ones_ref)
    gvec_ref[...] = jnp.zeros_like(gvec_ref)
    attend_back(
        low_ref, rpe_ref, mask_ref, den_ref, ctx_ref, g_ctx_ref, g_feat_ref, g_low_ref, gvec_ref, grpe_ref,
        coef_ref, scores_ref, gk_ref, diag_ref, query_ref, key_ref, value_ref, num_ref,
    )
    project_back(
        tokens_ref, w_ref, g_hidden_ref, phi_ref, scaled_ref, block_ref, ones_ref,
        g_feat_ref, g_low_ref, gvec_ref, g_tokens_ref, d_qkv_ref, flip_ref,
    )


def vmem(count):
    return [pl.BlockSpec(memory_space=pltpu.VMEM)] * count


def shape(dims, kind):
    return jax.ShapeDtypeStruct(dims, kind)


SCALARS = pl.BlockSpec(memory_space=pltpu.SMEM)


def forward_call(seq, tokens, feat, w_qkv, vec, rpe):
    rows, breadth = tokens.shape
    span = 2 * rows
    return pl.pallas_call(
        forward_kernel,
        out_shape=(
            shape((rows, 2 * breadth), F32), shape((rows, 2 * breadth), F32), shape((rows, 3 * breadth), LOW),
            shape((rows, breadth), F32), shape((rows, breadth), F32), shape((rows, breadth), LOW),
        ),
        in_specs=[SCALARS] + vmem(5),
        out_specs=tuple(vmem(6)),
        scratch_shapes=[
            pltpu.VMEM((rows, rows), F32), pltpu.VMEM((breadth // 256, 256, 256), LOW),
            pltpu.VMEM((256, 256), LOW), pltpu.VMEM((128, span), F32), pltpu.VMEM((rows, 128), LOW),
        ],
        compiler_params=pltpu.CompilerParams(vmem_limit_bytes=60 * MIB),
        name="attend",
    )(seq, tokens, feat, w_qkv, vec, rpe)


def middle_call(seq, tokens, cotangent, ctx_low, vec, w_out, w_up, w_down):
    rows, breadth = tokens.shape
    hidden = w_up.shape[1]
    return pl.pallas_call(
        middle_kernel,
        out_shape=(
            shape((rows, breadth), LOW), shape((rows, breadth), F32), shape((rows, breadth), F32),
            shape(w_out.shape, LOW), shape(w_up.shape, LOW), shape(w_down.shape, LOW), shape(vec.shape, F32),
        ),
        in_specs=[SCALARS] + vmem(7),
        out_specs=tuple(vmem(7)),
        scratch_shapes=[
            pltpu.VMEM((rows, breadth), F32), pltpu.VMEM((rows, breadth), F32), pltpu.VMEM((rows, breadth), LOW),
            pltpu.VMEM((rows, breadth), F32), pltpu.VMEM((rows, 128), F32), pltpu.VMEM((rows, hidden), LOW),
            pltpu.VMEM((rows, hidden), F32), pltpu.VMEM((rows, breadth), F32), pltpu.VMEM((rows, breadth), LOW),
            pltpu.VMEM((rows, hidden), LOW), pltpu.VMEM((breadth, rows), LOW),
        ],
        compiler_params=pltpu.CompilerParams(vmem_limit_bytes=60 * MIB),
        name="feed_forward",
    )(seq, tokens, cotangent, ctx_low, vec, w_out, w_up, w_down)


def backward_call(seq, tokens, feat, w_qkv, rpe, scaled, phi, low, den, ctx, g_ctx, g_hidden, vec):
    rows, breadth = tokens.shape
    span = 2 * rows
    return pl.pallas_call(
        backward_kernel,
        out_shape=(
            shape((rows, breadth), F32), shape(w_qkv.shape, LOW), shape(vec.shape, F32), shape(rpe.shape, F32),
        ),
        in_specs=[SCALARS] + vmem(11),
        out_specs=tuple(vmem(4)),
        scratch_shapes=[
            pltpu.VMEM((rows, rows), F32), pltpu.VMEM((breadth // 256, 256, 256), LOW),
            pltpu.VMEM((256, 256), LOW), pltpu.VMEM((128, span), F32), pltpu.VMEM((rows, 3 * breadth), F32),
            pltpu.VMEM((rows, 3 * breadth), LOW), pltpu.VMEM((rows, rows), LOW), pltpu.VMEM((rows, rows), LOW),
            pltpu.VMEM((128, span), F32), pltpu.VMEM((rows, 128), LOW), pltpu.VMEM((rows, 128), LOW),
            pltpu.VMEM((rows, 128), LOW), pltpu.VMEM((rows, 128), LOW), pltpu.VMEM((breadth, rows), LOW),
        ],
        compiler_params=pltpu.CompilerParams(vmem_limit_bytes=60 * MIB),
        name="attend_back",
    )(seq, tokens, feat, w_qkv, rpe, scaled, phi, low, den, ctx, g_ctx, g_hidden)


PIECE = 16


def place():
    me = lax.axis_index("dp")
    core = lax.rem(me, 2)
    x = lax.rem(me // 2, 2)
    y = lax.rem(me // 4, 2)
    z = me // 8
    first = x * (1 - core) + y * core
    second = y * (1 - core) + x * core
    return core, z, first, second


class Plane:
    def __init__(self, depth):
        self.depth = depth
        self.core, self.z, self.first, self.second = place()
        self.chip = self.at(self.z, self.first, self.second)
        self.sibling = self.chip * 2 + 1 - self.core
        self.over_first = self.device(self.z, 1 - self.first, self.second)
        self.over_second = self.device(self.z, self.first, 1 - self.second)

    def at(self, z, first, second):
        return 4 * z + first * (1 + self.core) + second * (2 - self.core)

    def device(self, z, first, second):
        return 2 * self.at(z, first, second) + self.core

    def ahead(self, distance):
        return lax.rem(self.z + distance, self.depth)

    def behind(self, distance):
        return lax.rem(self.z + self.depth - distance, self.depth)

    def greet(self):
        barrier = pltpu.get_barrier_semaphore()
        others = [self.sibling, self.over_first, self.over_second]
        others += [self.device(self.ahead(d), self.first, self.second) for d in range(1, self.depth)]
        for other in others:
            pl.semaphore_signal(barrier, inc=1, device_id=(other,), device_id_type=MESH)
        pl.semaphore_wait(barrier, len(others))


def remote(source, target, sems, item, slot, device):
    return pltpu.make_async_remote_copy(
        src_ref=source, dst_ref=target, send_sem=sems[0].at[item, slot], recv_sem=sems[1].at[item, slot],
        device_id=(device,), device_id_type=MESH,
    )


def each(count, step):
    def run(index, carry):
        step(index)
        return carry

    lax.fori_loop(0, count, run, 0)


class Gather:
    def __init__(self, plane, own, full, sems, local):
        self.plane, self.own, self.full, self.sems, self.local = plane, own, full, sems, local
        depth = plane.depth
        self.first_slot = depth - 1
        self.second_slot = self.first_slot + depth
        self.core_slot = self.second_slot + 2 * depth
        self.slots = self.core_slot + 4 * depth

    def block(self, item, chip):
        return self.full[item].at[chip, self.plane.core]

    def to_first(self, item, z, source=None):
        block = self.block(item, self.plane.at(z, self.plane.first, self.plane.second))
        return remote(block if source is None else source, block, self.sems, item, self.first_slot + z, self.plane.over_first)

    def to_second(self, item, z, first, source=None):
        block = self.block(item, self.plane.at(z, first, self.plane.second))
        return remote(
            block if source is None else source, block, self.sems, item, self.second_slot + 2 * z + first, self.plane.over_second
        )

    def to_core(self, item, chip, source=None):
        block = self.block(item, chip)
        return remote(block if source is None else source, block, self.sems, item, self.core_slot + chip, self.plane.sibling)

    def to_depth(self, item, distance):
        plane = self.plane
        target = plane.device(plane.ahead(distance), plane.first, plane.second)
        return remote(self.own[item], self.block(item, plane.chip), self.sems, item, distance - 1, target)

    def copy_own(self, item):
        return pltpu.make_async_copy(self.own[item], self.block(item, self.plane.chip), self.local.at[item])

    def begin(self, item):
        plane = self.plane
        own = self.own[item]
        for distance in range(1, plane.depth):
            self.to_depth(item, distance).start()
        self.to_first(item, plane.z, own).start()
        self.to_second(item, plane.z, plane.first, own).start()
        self.to_core(item, plane.chip, own).start()
        self.copy_own(item).start()

    def arrived(self, copy):
        copy.wait_recv()

    def over_depth(self, item):
        plane = self.plane

        def step(index):
            z = plane.behind(index + 1)
            chip = plane.at(z, plane.first, plane.second)
            block = self.block(item, chip)
            remote(block, block, self.sems, item, index, plane.over_first).wait_recv()
            self.to_first(item, z).start()
            self.to_second(item, z, plane.first).start()
            self.to_core(item, chip).start()

        each(plane.depth - 1, step)

    def over_first(self, item):
        plane = self.plane

        def step(z):
            chip = plane.at(z, 1 - plane.first, plane.second)
            block = self.block(item, chip)
            remote(block, block, self.sems, item, self.first_slot + z, plane.over_first).wait_recv()
            self.to_second(item, z, 1 - plane.first).start()
            self.to_core(item, chip).start()

        each(plane.depth, step)

    def over_second(self, item):
        plane = self.plane

        def step(index):
            z, first = index // 2, lax.rem(index, 2)
            chip = plane.at(z, first, 1 - plane.second)
            block = self.block(item, chip)
            remote(block, block, self.sems, item, self.second_slot + index, plane.over_second).wait_recv()
            self.to_core(item, chip).start()

        each(2 * plane.depth, step)

    def over_core(self, item):
        plane = self.plane

        def step(chip):
            block = self.full[item].at[chip, 1 - plane.core]
            remote(block, block, self.sems, item, self.core_slot + chip, plane.sibling).wait_recv()

        each(4 * plane.depth, step)
        self.copy_own(item).wait()

    def sent(self, item):
        plane = self.plane
        block = self.block(item, plane.chip)

        def step(slot):
            remote(block, block, self.sems, item, slot, plane.sibling).wait_send()

        each(self.slots, step)


def one_hot(length, breadth):
    factor = (1 << 20) // length + 1
    col = iota((128, breadth), 1)
    owner = lax.shift_right_logical(col * factor, 20)
    return jnp.where(iota((128, breadth), 0) == col - owner * length, 1.0, 0.0).astype(LOW)


def owned(devices, length, breadth):
    factor = (1 << 20) // length + 1
    col = iota((devices, breadth), 1)
    return lax.shift_right_logical(col * factor, 20) == iota((devices, breadth), 0)


def pack_small(piece_refs, small_ref):
    small_ref[...] = jnp.zeros_like(small_ref)
    for row, piece in enumerate(piece_refs[:-1]):
        small_ref[row : row + 1, 0 : piece.shape[1]] = piece[...].astype(LOW).astype(F32)
    table = piece_refs[-1]
    for part in range(table.shape[1] // 128):
        row = len(piece_refs) - 1 + part
        small_ref[row : row + 1, :] = table[:, 128 * part : 128 * part + 128].astype(LOW).astype(F32)


def unpack_small(all_ref, lengths, table_rows, vec_ref, rpe_ref):
    devices = all_ref.shape[0] // PIECE
    vec_ref[...] = jnp.zeros_like(vec_ref)
    for row, length in enumerate(lengths):
        breadth = length * devices
        picked = all_ref[pl.ds(row, devices, stride=PIECE), :].astype(LOW)
        spread = jnp.where(owned(devices, length, breadth), mm(picked, one_hot(length, breadth)), 0.0)
        vec_ref[row : row + 1, 0:breadth] = column_sum(spread)
    for part in range(table_rows):
        rpe_ref[pl.ds(part, devices, stride=table_rows), :] = all_ref[
            pl.ds(len(lengths) + part, devices, stride=PIECE), :
        ]


def gather_kernel(depth, count, pieces, *refs):
    matrices, refs = refs[:count], refs[count:]
    piece_refs, refs = refs[:pieces], refs[pieces:]
    full, refs = refs[:count], refs[count:]
    vec_ref, rpe_ref = refs[:2]
    own, refs = refs[2 : 2 + count], refs[2 + count :]
    small_ref, all_ref, send, recv, local = refs
    plane = Plane(depth)
    pack_small(piece_refs, small_ref)
    for matrix, mine in zip(matrices, own):
        mine[...] = matrix[...].astype(LOW)
    plane.greet()
    gather = Gather(plane, [small_ref] + list(own), [all_ref] + list(full), (send, recv), local)
    items = count + 1
    for item in range(items):
        gather.begin(item)
    stages = (gather.over_depth, gather.over_first, gather.over_second, gather.over_core)
    for tick in range(items + len(stages) - 1):
        for late, stage in enumerate(stages):
            if 0 <= tick - late < items:
                stage(tick - late)
    for item in range(items):
        gather.sent(item)
    lengths = [piece.shape[1] for piece in piece_refs[:-1]]
    table_rows = piece_refs[-1].shape[1] // 128
    flat_ref = refs_flat(all_ref)
    unpack_small(flat_ref, lengths, table_rows, vec_ref, rpe_ref)


def refs_flat(ref):
    return ref.reshape(ref.shape[0] * ref.shape[1] * ref.shape[2], ref.shape[3])


ANYWHERE = pl.BlockSpec(memory_space=pl.ANY)


def gather_call(depth, matrices, pieces):
    chips = 4 * depth
    devices = 2 * chips
    items = len(matrices) + 1
    slots = depth - 1 + depth + 2 * depth + 4 * depth
    longest = max(piece.shape[1] for piece in pieces[:-1]) * devices
    table = pieces[-1].shape[1] * devices // 128
    result = pl.pallas_call(
        functools.partial(gather_kernel, depth, len(matrices), len(pieces)),
        out_shape=tuple(shape((chips, 2) + matrix.shape, LOW) for matrix in matrices)
        + (shape((len(pieces) - 1, longest), F32), shape((table, 128), F32)),
        in_specs=vmem(len(matrices) + len(pieces)),
        out_specs=(ANYWHERE,) * len(matrices) + tuple(vmem(2)),
        scratch_shapes=[pltpu.VMEM(matrix.shape, LOW) for matrix in matrices]
        + [
            pltpu.VMEM((PIECE, 128), F32), pltpu.VMEM((chips, 2, PIECE, 128), F32),
            pltpu.SemaphoreType.DMA((items, slots)), pltpu.SemaphoreType.DMA((items, slots)),
            pltpu.SemaphoreType.DMA((items,)),
        ],
        compiler_params=pltpu.CompilerParams(
            collective_id=0, has_side_effects=True, vmem_limit_bytes=16 * MIB
        ),
        name="gather",
    )(*matrices, *pieces)
    full = [
        piece.reshape(devices * matrix.shape[0], matrix.shape[1]) for piece, matrix in zip(result, matrices)
    ]
    return full, result[-2], result[-1]


class Scatter:
    def __init__(self, plane, given, total, from_core, from_second, from_first, from_depth, sems, local):
        self.plane, self.given, self.total = plane, given, total
        self.from_core, self.from_second = from_core, from_second
        self.from_first, self.from_depth = from_first, from_depth
        self.sems, self.local = sems, local
        depth = plane.depth
        self.first_slot = depth - 1
        self.second_slot = self.first_slot + depth
        self.core_slot = self.second_slot + 2 * depth
        self.slots = self.core_slot + 1

    def with_core(self, item):
        plane = self.plane
        return remote(
            self.given[item].at[:, 1 - plane.core], self.from_core[item], self.sems, item, self.core_slot,
            plane.sibling,
        )

    def keep_own(self, item):
        return pltpu.make_async_copy(
            self.given[item].at[:, self.plane.core], self.total[item], self.local.at[item]
        )

    def begin(self, item):
        self.with_core(item).start()
        self.keep_own(item).start()

    def to_second(self, item, index):
        plane = self.plane
        chip = plane.at(index // 2, lax.rem(index, 2), 1 - plane.second)
        return remote(
            self.total[item].at[chip], self.from_second[item].at[index], self.sems, item,
            self.second_slot + index, plane.over_second,
        )

    def to_first(self, item, z):
        plane = self.plane
        chip = plane.at(z, 1 - plane.first, plane.second)
        return remote(
            self.total[item].at[chip], self.from_first[item].at[z], self.sems, item, self.first_slot + z,
            plane.over_first,
        )

    def to_depth(self, item, index):
        plane = self.plane
        z = plane.ahead(index + 1)
        chip = plane.at(z, plane.first, plane.second)
        return remote(
            self.total[item].at[chip], self.from_depth[item].at[index], self.sems, item, index,
            plane.device(z, plane.first, plane.second),
        )

    def join(self, item, chip, piece):
        total = self.total[item]
        total[chip] = total[chip] + piece

    def over_core(self, item):
        plane = self.plane
        self.keep_own(item).wait()
        self.with_core(item).wait_recv()

        def away(index):
            chip = plane.at(index // 2, lax.rem(index, 2), 1 - plane.second)
            self.join(item, chip, self.from_core[item][chip])
            self.to_second(item, index).start()

        def stay(index):
            chip = plane.at(index // 2, lax.rem(index, 2), plane.second)
            self.join(item, chip, self.from_core[item][chip])

        each(2 * plane.depth, away)
        each(2 * plane.depth, stay)

    def over_second(self, item):
        plane = self.plane

        def away(z):
            index = 2 * z + 1 - plane.first
            self.to_second(item, index).wait_recv()
            self.join(item, plane.at(z, 1 - plane.first, plane.second), self.from_second[item][index])
            self.to_first(item, z).start()

        def stay(z):
            index = 2 * z + plane.first
            self.to_second(item, index).wait_recv()
            self.join(item, plane.at(z, plane.first, plane.second), self.from_second[item][index])

        each(plane.depth, away)
        each(plane.depth, stay)

    def over_first(self, item):
        plane = self.plane

        def away(index):
            z = plane.ahead(index + 1)
            self.to_first(item, z).wait_recv()
            self.join(item, plane.at(z, plane.first, plane.second), self.from_first[item][z])
            self.to_depth(item, index).start()

        each(plane.depth - 1, away)
        self.to_first(item, plane.z).wait_recv()
        self.join(item, plane.chip, self.from_first[item][plane.z])

    def over_depth(self, item, out_ref):
        plane = self.plane
        for index in range(plane.depth - 1):
            self.to_depth(item, index).wait_recv()
        value = self.total[item][plane.chip].astype(F32)
        for index in range(plane.depth - 1):
            value = value + self.from_depth[item][index].astype(F32)
        out_ref[...] = value

    def sent(self, item):
        def second(index):
            self.to_second(item, index).wait_send()

        def first(z):
            self.to_first(item, z).wait_send()

        def along(index):
            self.to_depth(item, index).wait_send()

        each(2 * self.plane.depth, second)
        each(self.plane.depth, first)
        each(self.plane.depth - 1, along)
        self.with_core(item).wait_send()


def pack_grads(vec_refs, rows_of, lengths, grpe_ref, flat_ref):
    devices = flat_ref.shape[0] // PIECE
    table_rows = grpe_ref.shape[0] // devices
    flat_ref[...] = jnp.zeros_like(flat_ref)
    for row, length in enumerate(lengths):
        breadth = length * devices
        value = vec_refs[rows_of[row]][row : row + 1, 0:breadth]
        spread = jnp.where(owned(devices, length, breadth), jnp.broadcast_to(value, (devices, breadth)), 0.0)
        flat_ref[pl.ds(row, devices, stride=PIECE), :] = mm2(spread, one_hot(length, breadth), 1)
    for part in range(table_rows):
        flat_ref[pl.ds(len(lengths) + part, devices, stride=PIECE), :] = grpe_ref[
            pl.ds(part, devices, stride=table_rows), :
        ]


def scatter_kernel(depth, count, lengths, *refs):
    given, refs = refs[:count], refs[count:]
    one_ref, two_ref, grpe_ref, refs = refs[0], refs[1], refs[2], refs[3:]
    outs, refs = refs[:count], refs[count:]
    pieces, refs = refs[: len(lengths) + 1], refs[len(lengths) + 1 :]
    items = count + 1
    total, refs = refs[:items], refs[items:]
    from_core, refs = refs[:items], refs[items:]
    from_second, refs = refs[:items], refs[items:]
    from_first, refs = refs[:items], refs[items:]
    from_depth, refs = refs[:items], refs[items:]
    flat_ref, sum_ref, send, recv, local = refs
    plane = Plane(depth)
    rows_of = [1] + [0] * (len(lengths) - 1)
    flat = flat_ref.reshape(2 * 4 * depth * PIECE, 128)
    pack_grads((one_ref, two_ref), rows_of, lengths, grpe_ref, flat)
    plane.greet()
    scatter = Scatter(
        plane, [flat_ref] + list(given), total, from_core, from_second, from_first, from_depth, (send, recv), local
    )
    for item in range(items):
        scatter.begin(item)
    targets = [sum_ref] + list(outs)
    stages = (
        scatter.over_core, scatter.over_second, scatter.over_first,
        lambda item: scatter.over_depth(item, targets[item]),
    )
    for tick in range(items + len(stages) - 1):
        for late, stage in enumerate(stages):
            if 0 <= tick - late < items:
                stage(tick - late)
    for item in range(items):
        scatter.sent(item)
    for row, length in enumerate(lengths):
        pieces[row][...] = sum_ref[row : row + 1, 0:length]
    table = pieces[-1]
    for part in range(table.shape[1] // 128):
        row = len(lengths) + part
        table[:, 128 * part : 128 * part + 128] = sum_ref[row : row + 1, :]


def scatter_call(depth, grads, gvec_one, gvec_two, grpe, lengths):
    chips = 4 * depth
    devices = 2 * chips
    items = len(grads) + 1
    slots = depth - 1 + depth + 2 * depth + 1
    blocks = [(grad.shape[0] // devices, grad.shape[1]) for grad in grads]
    kinds = [((PIECE, 128), F32)] + [(block, LOW) for block in blocks]
    table = grpe.shape[0] // devices * 128

    def buffers(number):
        return [pltpu.VMEM((number,) + block, kind) for block, kind in kinds]

    result = pl.pallas_call(
        functools.partial(scatter_kernel, depth, len(grads), lengths),
        out_shape=tuple(shape(block, F32) for block in blocks)
        + tuple(shape((1, length), F32) for length in lengths + (table,)),
        in_specs=[ANYWHERE] * len(grads) + vmem(3),
        out_specs=tuple(vmem(len(grads) + len(lengths) + 1)),
        scratch_shapes=buffers(chips) + buffers(chips) + buffers(2 * depth) + buffers(depth) + buffers(depth - 1)
        + [
            pltpu.VMEM((chips, 2, PIECE, 128), F32), pltpu.VMEM((PIECE, 128), F32),
            pltpu.SemaphoreType.DMA((items, slots)), pltpu.SemaphoreType.DMA((items, slots)),
            pltpu.SemaphoreType.DMA((items,)),
        ],
        compiler_params=pltpu.CompilerParams(
            collective_id=1, has_side_effects=True, vmem_limit_bytes=60 * MIB
        ),
        name="scatter",
    )(*[grad.reshape((chips, 2) + block) for grad, block in zip(grads, blocks)], gvec_one, gvec_two, grpe)
    matrices, pieces = result[: len(grads)], result[len(grads) :]
    return matrices, [piece.reshape(-1) for piece in pieces]


def plain_gather(value):
    return lax.all_gather(value.astype(LOW), "dp", axis=0, tiled=True)


def plain_scatter(value):
    return lax.psum_scatter(value.astype(F32), "dp", scatter_dimension=0, tiled=True)


def body(
    depth, tokens, cotangent, seq_lengths, random_feat, w_qkv, b_qkv, w_out, b_out, ln1_gain, ln1_bias,
    w_up, b_up, w_down, b_down, ln2_gain, ln2_bias, rpe_table,
):
    vectors = (b_qkv, b_up, b_out, ln1_gain, ln1_bias, b_down, ln2_gain, ln2_bias)
    matrices = (w_qkv, w_out, w_up, w_down)
    if depth:
        pieces = [piece.reshape(1, -1) for piece in vectors + (rpe_table,)]
        (full_qkv, full_out, full_up, full_down), vec, rpe = gather_call(depth, matrices, pieces)
    else:
        full_vectors = [plain_gather(piece).astype(F32) for piece in vectors]
        longest = max(piece.shape[0] for piece in full_vectors)
        vec = jnp.stack([jnp.pad(piece, (0, longest - piece.shape[0])) for piece in full_vectors])
        rpe = plain_gather(rpe_table).astype(F32).reshape(-1, 128)
        full_qkv, full_out, full_up, full_down = [plain_gather(piece) for piece in matrices]
    scaled, phi, low, den, ctx, ctx_low = forward_call(seq_lengths, tokens, random_feat, full_qkv, vec, rpe)
    out, g_hidden, g_ctx, d_out, d_up, d_down, gvec_one = middle_call(
        seq_lengths, tokens, cotangent, ctx_low, vec, full_out, full_up, full_down
    )
    g_tokens, d_qkv, gvec_two, grpe = backward_call(
        seq_lengths, tokens, random_feat, full_qkv, rpe, scaled, phi, low, den, ctx, g_ctx, g_hidden, vec
    )
    grads = (d_qkv, d_out, d_up, d_down)
    lengths = tuple(piece.shape[0] for piece in vectors)
    if depth:
        sums, pieces = scatter_call(depth, grads, gvec_one, gvec_two, grpe, lengths)
    else:
        gvec = gvec_one + gvec_two
        sums = [plain_scatter(grad) for grad in grads]
        devices = lax.axis_size("dp")
        pieces = [plain_scatter(gvec[row, : length * devices]) for row, length in enumerate(lengths)]
        pieces.append(plain_scatter(grpe.reshape(-1)))
    s_qkv, s_out, s_up, s_down = sums
    p_qkv, p_up, p_out, p_gain_one, p_bias_one, p_down, p_gain_two, p_bias_two, p_rpe = pieces
    return (
        out, g_tokens, s_qkv, p_qkv, s_out, p_out, p_gain_one, p_bias_one, s_up, p_up, s_down, p_down,
        p_gain_two, p_bias_two, p_rpe,
    )


def solution(mesh):
    wide, flat = P("dp", None), P("dp")
    devices = mesh.shape["dp"]
    depth = devices // 8 if devices in (16, 32) else 0
    in_specs = (
        wide, wide, wide, P(), wide, flat, wide, flat, flat, flat, wide, flat, wide, flat, flat, flat, flat,
    )
    out_specs = (
        wide, wide, wide, flat, wide, flat, flat, flat, wide, flat, wide, flat, flat, flat, flat,
    )
    return jax.shard_map(
        functools.partial(body, depth), mesh=mesh, in_specs=in_specs, out_specs=out_specs, check_vma=False
    )
```

```python
import functools

import jax
import jax.numpy as jnp
from jax import lax
from jax.experimental import pallas as pl
from jax.experimental.pallas import tpu as pltpu
from jax.sharding import PartitionSpec as P

EPSILON = 1e-05
F32 = jnp.float32
LOW = jnp.bfloat16
MESH = pl.DeviceIdType.MESH
MIB = 2**20


def mm(first_op, second_op, first_dim=1, second_dim=0):
    return lax.dot_general(
        first_op,
        second_op,
        (((first_dim,), (second_dim,)), ((), ())),
        preferred_element_type=F32,
    )


def mm2(value, weight, weight_dim=0):
    high = value.astype(LOW)
    rest = (value - high.astype(F32)).astype(LOW)
    return mm(high, weight, 1, weight_dim) + mm(rest, weight, 1, weight_dim)


def iota(shape, dim):
    return lax.broadcasted_iota(jnp.int32, shape, dim)


def cols(index, width):
    return pl.ds(pl.multiple_of(index * width, width), width)


def build_tables(seq_ref, feat_ref, mask_ref, block_ref, ones_ref):
    rows = mask_ref.shape[0]
    first_end = seq_ref[0, 0]
    second_end = first_end + seq_ref[0, 1]

    def segment(place):
        return (place >= first_end).astype(jnp.int32) + (place >= second_end).astype(jnp.int32)

    across = segment(iota((128, rows), 1))
    for start in range(0, rows, 128):
        down = segment(iota((128, rows), 0) + start)
        mask_ref[start : start + 128, :] = jnp.where(down == across, 1.0, 0.0)
    head_size = feat_ref.shape[1]
    breadth = ones_ref.shape[0]
    group = breadth // head_size
    bits = head_size.bit_length() - 1
    owner_row = lax.shift_right_logical(iota((breadth, breadth), 0), bits)
    owner_col = lax.shift_right_logical(iota((breadth, breadth), 1), bits)
    same = owner_row == owner_col
    ones_ref[...] = jnp.where(same, 1.0, 0.0).astype(LOW)
    for index in range(feat_ref.shape[0] // group):
        rows_of = []
        for inner in range(group):
            piece = feat_ref[index * group + inner].astype(F32)
            rows_of.append(jnp.concatenate([piece] * group, axis=1))
        full = jnp.concatenate(rows_of, axis=0)
        block_ref[index] = jnp.where(same, full, 0.0).astype(LOW)


def project(tokens_ref, w_ref, vec_ref, scaled_ref, phi_ref, low_ref, block_ref, ones_ref):
    breadth = tokens_ref.shape[1]
    tile = ones_ref.shape[0]
    per_part = breadth // tile
    scale = 64 ** (-0.25)

    def features(step, carry):
        where = cols(step, tile)
        acc = mm(tokens_ref[...], w_ref[:, where]) + vec_ref[0:1, where]
        scaled = acc * scale
        scaled_ref[:, where] = scaled
        block = block_ref[lax.rem(step, per_part)]
        mapped = mm2(scaled, block)
        squared = mm2(scaled * scaled, ones_ref[...])
        phi = jnp.exp(mapped - 0.5 * squared) * 0.125
        phi_ref[:, where] = phi
        low_ref[:, where] = phi.astype(LOW)
        return carry

    lax.fori_loop(0, 2 * per_part, features, 0)

    def plain(step, carry):
        where = cols(step + 2 * per_part, tile)
        acc = mm(tokens_ref[...], w_ref[:, where]) + vec_ref[0:1, where]
        low_ref[:, where] = acc.astype(LOW)
        return carry

    lax.fori_loop(0, per_part, plain, 0)


def coefficients(rpe_ref, head, coef_ref):
    flip = (iota((128, 128), 0) + iota((128, 128), 1) == 127).astype(F32).astype(LOW)
    raw = rpe_ref[pl.ds(pl.multiple_of(head * 8, 8), 8), :].astype(LOW)
    table = jnp.exp(mm(raw, flip))
    wide = jnp.concatenate(
        [jnp.broadcast_to(table[7 - k : 8 - k, :], (128, 128)) for k in range(8)], axis=1
    )
    coef_ref[...] = pltpu.roll(wide, 1024 - 127, axis=1, stride=1, stride_axis=0)


def attend(low_ref, rpe_ref, mask_ref, den_ref, ctx_ref, ctx_low_ref, coef_ref, key_ref):
    rows, breadth = ctx_ref.shape

    def pair_step(pair, carry):
        q_at = cols(pair, 128)
        k_at = pl.ds(pl.multiple_of(pair * 128 + breadth, 128), 128)
        v_at = pl.ds(pl.multiple_of(pair * 128 + 2 * breadth, 128), 128)
        lane = iota((128, 128), 1)
        for side in range(2):
            coefficients(rpe_ref, pair * 2 + side, coef_ref)
            mine = lane >= 64 if side else lane < 64
            keep_half(low_ref, k_at, key_ref, side)
            for block in range(rows // 128):
                at = slice(block * 128, block * 128 + 128)
                kernel = mm(low_ref[at, q_at], key_ref[...], 1, 1)
                lead = 128 * (rows // 128 - 1 - block)
                scores = kernel * (coef_ref[:, lead : lead + rows] * mask_ref[at, :])
                total = jnp.sum(scores, axis=1, keepdims=True)
                context = mm(scores.astype(LOW), low_ref[:, v_at]) * (1.0 / total)
                total = jnp.broadcast_to(total, (128, 128))
                if side == 0:
                    den_ref[at, q_at] = total
                    ctx_ref[at, q_at] = context
                else:
                    den_ref[at, q_at] = jnp.where(mine, total, den_ref[at, q_at])
                    context = jnp.where(mine, context, ctx_ref[at, q_at])
                    ctx_ref[at, q_at] = context
                    ctx_low_ref[at, q_at] = context.astype(LOW)
        return carry

    lax.fori_loop(0, breadth // 128, pair_step, 0)


def keep_half(low_ref, where, out_ref, side):
    rows = low_ref.shape[0]
    lane = iota((rows, 128), 1)
    mine = lane >= 64 if side else lane < 64
    out_ref[...] = jnp.where(mine, low_ref[:, where].astype(F32), 0.0).astype(LOW)


def forward_kernel(
    seq_ref, tokens_ref, feat_ref, w_ref, vec_ref, rpe_ref,
    scaled_ref, phi_ref, low_ref, den_ref, ctx_ref, ctx_low_ref,
    mask_ref, block_ref, ones_ref, coef_ref, key_ref,
):
    build_tables(seq_ref, feat_ref, mask_ref, block_ref, ones_ref)
    project(tokens_ref, w_ref, vec_ref, scaled_ref, phi_ref, low_ref, block_ref, ones_ref)
    attend(low_ref, rpe_ref, mask_ref, den_ref, ctx_ref, ctx_low_ref, coef_ref, key_ref)


def norm(value):
    centred = value - jnp.mean(value, axis=-1, keepdims=True)
    inverse = lax.rsqrt(jnp.mean(centred * centred, axis=-1, keepdims=True) + EPSILON)
    return centred * inverse, inverse


def norm_back(grad, xhat, inverse, gain):
    scaled = grad * gain
    mean = jnp.mean(scaled, axis=-1, keepdims=True)
    along = jnp.mean(scaled * xhat, axis=-1, keepdims=True)
    return inverse * (scaled - mean - xhat * along)


def add_to(ref, row, value):
    ref[row : row + 1, 0 : value.shape[1]] += value


def column_sum(value):
    return jnp.sum(value, axis=0, keepdims=True)


def middle_kernel(
    seq_ref, tokens_ref, cot_ref, ctx_low_ref, vec_ref, w_out_ref, w_up_ref, w_down_ref,
    out_ref, g_hidden_ref, g_ctx_ref, d_out_ref, d_up_ref, d_down_ref, gvec_ref,
    wide_ref, normed_ref, normed_low_ref, xhat_ref, inverse_ref, act_ref, slope_ref, g_sum_ref,
    g_low_ref, g_up_ref, flip_ref,
):
    rows, breadth = tokens_ref.shape
    hidden = w_up_ref.shape[1]
    height, tile = 128, 256
    blocks, tiles = rows // height, breadth // tile
    valid_rows = seq_ref[0, 0] + seq_ref[0, 1]
    gvec_ref[...] = jnp.zeros_like(gvec_ref)
    gain_one, bias_one = vec_ref[3:4, :breadth], vec_ref[4:5, :breadth]
    gain_two, bias_two = vec_ref[6:7, :breadth], vec_ref[7:8, :breadth]

    def rows_at(step):
        return pl.ds(pl.multiple_of(step * height, height), height)

    def loop(count, step):
        def run(index, carry):
            step(index)
            return carry

        lax.fori_loop(0, count, run, 0)

    def attended_step(step):
        where = cols(step, tile)
        wide_ref[:, where] = mm(ctx_low_ref[...], w_out_ref[:, where]) + vec_ref[2:3, where]

    loop(tiles, attended_step)

    def first_norm(step):
        at = rows_at(step)
        xhat, inverse = norm(tokens_ref[at, :].astype(F32) + wide_ref[at, :])
        xhat_ref[at, :] = xhat
        inverse_ref[at, :] = jnp.broadcast_to(inverse, (height, 128))
        normed = xhat * gain_one + bias_one
        normed_ref[at, :] = normed
        normed_low_ref[at, :] = normed.astype(LOW)

    loop(blocks, first_norm)

    def upward_step(step):
        where = cols(step, tile)
        upward = mm(normed_low_ref[...], w_up_ref[:, where]) + vec_ref[1:2, where]
        phi = 0.5 + 0.5 * lax.erf(upward * 0.5**0.5)
        density = jnp.exp(-0.5 * upward * upward) * 0.3989422804014327
        act_ref[:, where] = (upward * phi).astype(LOW)
        slope_ref[:, where] = phi + upward * density

    loop(hidden // tile, upward_step)

    def downward_step(step):
        where = cols(step, tile)
        wide_ref[:, where] = mm(act_ref[...], w_down_ref[:, where]) + vec_ref[5:6, where]

    loop(tiles, downward_step)

    def second_norm(step):
        at = rows_at(step)
        xhat, inverse = norm(normed_ref[at, :] + wide_ref[at, :])
        out_ref[at, :] = (xhat * gain_two + bias_two).astype(LOW)
        place = iota((height, breadth), 0) + step * height
        grad = jnp.where(place < valid_rows, cot_ref[at, :].astype(F32), 0.0)
        add_to(gvec_ref, 6, column_sum(grad * xhat))
        add_to(gvec_ref, 7, column_sum(grad))
        g_sum = norm_back(grad, xhat, inverse, gain_two)
        add_to(gvec_ref, 5, column_sum(g_sum))
        g_sum_ref[at, :] = g_sum
        g_low_ref[at, :] = g_sum.astype(LOW)

    loop(blocks, second_norm)
    flip_ref[...] = jnp.transpose(normed_low_ref[...])

    def down_step(step):
        where = cols(step, tile)
        g_upward = mm(g_low_ref[...], w_down_ref[where, :], 1, 1) * slope_ref[:, where]
        gvec_ref[1:2, where] = column_sum(g_upward)
        g_upward = g_upward.astype(LOW)
        g_up_ref[:, where] = g_upward
        d_down_ref[where, :] = mm(act_ref[:, where], g_low_ref[...], 0, 0).astype(LOW)
        d_up_ref[:, where] = mm(flip_ref[...], g_upward).astype(LOW)

    loop(hidden // tile, down_step)

    def up_back(step):
        where = cols(step, tile)
        wide_ref[:, where] = mm(g_up_ref[...], w_up_ref[where, :], 1, 1) + g_sum_ref[:, where]

    loop(tiles, up_back)

    def first_back(step):
        at = rows_at(step)
        g_normed = wide_ref[at, :]
        xhat = xhat_ref[at, :]
        add_to(gvec_ref, 3, column_sum(g_normed * xhat))
        add_to(gvec_ref, 4, column_sum(g_normed))
        g_hidden = norm_back(g_normed, xhat, inverse_ref[at, 0:1], gain_one)
        add_to(gvec_ref, 2, column_sum(g_hidden))
        g_hidden_ref[at, :] = g_hidden
        g_low_ref[at, :] = g_hidden.astype(LOW)

    loop(blocks, first_back)

    def out_back(step):
        where = cols(step, tile)
        g_ctx_ref[:, where] = mm(g_low_ref[...], w_out_ref[where, :], 1, 1)
        d_out_ref[where, :] = mm(ctx_low_ref[:, where], g_low_ref[...], 0, 0).astype(LOW)

    loop(tiles, out_back)


def plain_diagonals(diag_ref, out_ref, head):
    value = diag_ref[...]
    height = value.shape[0]
    while height > 1:
        height //= 2
        value = value[height:] + pltpu.roll(value[:height], height, axis=1)
    for k in range(8):
        out_ref[pl.ds(head * 8 + 7 - k, 1), :] = value[:, 128 * k : 128 * k + 128]


def attend_back(
    low_ref, rpe_ref, mask_ref, den_ref, ctx_ref, g_ctx_ref,
    g_feat_ref, g_low_ref, gvec_ref, grpe_ref,
    coef_ref, scores_ref, gk_ref, diag_ref, query_ref, key_ref, value_ref, num_ref,
):
    rows, breadth = ctx_ref.shape

    def pair_step(pair, carry):
        q_at = cols(pair, 128)
        k_at = pl.ds(pl.multiple_of(pair * 128 + breadth, 128), 128)
        v_at = pl.ds(pl.multiple_of(pair * 128 + 2 * breadth, 128), 128)
        lane = iota((128, 128), 1)
        ones = jnp.ones((128, 128), LOW)
        for side in range(2):
            coefficients(rpe_ref, pair * 2 + side, coef_ref)
            mine = lane >= 64 if side else lane < 64
            other = 0 if side else 64
            keep_half(low_ref, q_at, query_ref, side)
            keep_half(low_ref, k_at, key_ref, side)
            keep_half(low_ref, v_at, value_ref, side)
            diag_ref[...] = jnp.zeros_like(diag_ref)
            is_high, is_rest = lane == other, lane == other + 1
            extra = jnp.where(jnp.logical_or(is_high, is_rest), 1.0, 0.0)
            for block in range(rows // 128):
                at = slice(block * 128, block * 128 + 128)
                value_ref[at, :] = (value_ref[at, :].astype(F32) + extra).astype(LOW)
            for block in range(rows // 128):
                at = slice(block * 128, block * 128 + 128)
                kernel = mm(low_ref[at, q_at], key_ref[...], 1, 1)
                g_num = jnp.where(mine, g_ctx_ref[at, q_at] * (1.0 / den_ref[at, q_at]), 0.0)
                g_den = -mm2(g_num * ctx_ref[at, q_at], ones)
                num_ref[at, :] = g_num.astype(LOW)
                high = g_den.astype(LOW).astype(F32)
                extended = jnp.where(is_high, high, jnp.where(is_rest, g_den - high, g_num))
                g_scores = mm(extended.astype(LOW), value_ref[...], 1, 1)
                lead = 128 * (rows // 128 - 1 - block)
                weight = coef_ref[:, lead : lead + rows] * mask_ref[at, :]
                scores = kernel * weight
                g_kernel = (g_scores * weight).astype(LOW)
                diag_ref[:, lead : lead + rows] += g_scores * scores
                scores_ref[at, :] = scores.astype(LOW)
                gk_ref[at, :] = g_kernel
                g_query = mm(g_kernel, key_ref[...])
                if side:
                    g_query = g_query + g_feat_ref[at, q_at]
                g_feat_ref[at, q_at] = g_query
            g_key = mm(gk_ref[...], query_ref[...], 0, 0)
            g_value = mm(scores_ref[...], num_ref[...], 0, 0)
            if side:
                g_key = g_key + g_feat_ref[:, k_at]
                g_value = g_value + g_feat_ref[:, v_at]
            g_feat_ref[:, k_at] = g_key
            g_feat_ref[:, v_at] = g_value
            plain_diagonals(diag_ref, grpe_ref, pair * 2 + side)
        g_value = g_feat_ref[:, v_at]
        gvec_ref[0:1, v_at] = column_sum(g_value)
        g_low_ref[:, v_at] = g_value.astype(LOW)
        return carry

    lax.fori_loop(0, breadth // 128, pair_step, 0)
    flip = (jnp.where(iota((128, 128), 0) + iota((128, 128), 1) == 127, 1.0, 0.0)).astype(LOW)
    grpe_ref[...] = mm2(grpe_ref[...], flip)


def project_back(
    tokens_ref, w_ref, g_hidden_ref, phi_ref, scaled_ref, block_ref, ones_ref,
    g_feat_ref, g_low_ref, gvec_ref, g_tokens_ref, d_qkv_ref, flip_ref,
):
    breadth = tokens_ref.shape[1]
    tile = ones_ref.shape[0]
    per_part = breadth // tile
    scale = 64 ** (-0.25)

    def features(step, carry):
        where = cols(step, tile)
        upward = g_feat_ref[:, where] * phi_ref[:, where]
        total = mm2(upward, ones_ref[...])
        grad = mm2(upward, block_ref[lax.rem(step, per_part)], 1) - scaled_ref[:, where] * total
        grad = grad * scale
        gvec_ref[0:1, where] = column_sum(grad)
        g_low_ref[:, where] = grad.astype(LOW)
        return carry

    lax.fori_loop(0, 2 * per_part, features, 0)
    flip_ref[...] = jnp.transpose(tokens_ref[...])

    def weights(step, carry):
        where = cols(step, tile)
        d_qkv_ref[:, where] = mm(flip_ref[...], g_low_ref[:, where]).astype(LOW)
        return carry

    lax.fori_loop(0, 3 * per_part, weights, 0)

    def inputs(step, carry):
        where = cols(step, tile)
        g_tokens_ref[:, where] = mm(g_low_ref[...], w_ref[where, :], 1, 1) + g_hidden_ref[:, where]
        return carry

    lax.fori_loop(0, per_part, inputs, 0)


def backward_kernel(
    seq_ref, tokens_ref, feat_ref, w_ref, rpe_ref, scaled_ref, phi_ref, low_ref, den_ref, ctx_ref,
    g_ctx_ref, g_hidden_ref,
    g_tokens_ref, d_qkv_ref, gvec_ref, grpe_ref,
    mask_ref, block_ref, ones_ref, coef_ref, g_feat_ref, g_low_ref, scores_ref, gk_ref, diag_ref,
    query_ref, key_ref, value_ref, num_ref, flip_ref,
):
    build_tables(seq_ref, feat_ref, mask_ref, block_ref, ones_ref)
    gvec_ref[...] = jnp.zeros_like(gvec_ref)
    attend_back(
        low_ref, rpe_ref, mask_ref, den_ref, ctx_ref, g_ctx_ref, g_feat_ref, g_low_ref, gvec_ref, grpe_ref,
        coef_ref, scores_ref, gk_ref, diag_ref, query_ref, key_ref, value_ref, num_ref,
    )
    project_back(
        tokens_ref, w_ref, g_hidden_ref, phi_ref, scaled_ref, block_ref, ones_ref,
        g_feat_ref, g_low_ref, gvec_ref, g_tokens_ref, d_qkv_ref, flip_ref,
    )


def vmem(count):
    return [pl.BlockSpec(memory_space=pltpu.VMEM)] * count


def shape(dims, kind):
    return jax.ShapeDtypeStruct(dims, kind)


SCALARS = pl.BlockSpec(memory_space=pltpu.SMEM)


def forward_call(seq, tokens, feat, w_qkv, vec, rpe):
    rows, breadth = tokens.shape
    span = 2 * rows
    return pl.pallas_call(
        forward_kernel,
        out_shape=(
            shape((rows, 2 * breadth), F32), shape((rows, 2 * breadth), F32), shape((rows, 3 * breadth), LOW),
            shape((rows, breadth), F32), shape((rows, breadth), F32), shape((rows, breadth), LOW),
        ),
        in_specs=[SCALARS] + vmem(5),
        out_specs=tuple(vmem(6)),
        scratch_shapes=[
            pltpu.VMEM((rows, rows), F32), pltpu.VMEM((breadth // 256, 256, 256), LOW),
            pltpu.VMEM((256, 256), LOW), pltpu.VMEM((128, span), F32), pltpu.VMEM((rows, 128), LOW),
        ],
        compiler_params=pltpu.CompilerParams(vmem_limit_bytes=60 * MIB),
        name="attend",
    )(seq, tokens, feat, w_qkv, vec, rpe)


def middle_call(seq, tokens, cotangent, ctx_low, vec, w_out, w_up, w_down):
    rows, breadth = tokens.shape
    hidden = w_up.shape[1]
    return pl.pallas_call(
        middle_kernel,
        out_shape=(
            shape((rows, breadth), LOW), shape((rows, breadth), F32), shape((rows, breadth), F32),
            shape(w_out.shape, LOW), shape(w_up.shape, LOW), shape(w_down.shape, LOW), shape(vec.shape, F32),
        ),
        in_specs=[SCALARS] + vmem(7),
        out_specs=tuple(vmem(7)),
        scratch_shapes=[
            pltpu.VMEM((rows, breadth), F32), pltpu.VMEM((rows, breadth), F32), pltpu.VMEM((rows, breadth), LOW),
            pltpu.VMEM((rows, breadth), F32), pltpu.VMEM((rows, 128), F32), pltpu.VMEM((rows, hidden), LOW),
            pltpu.VMEM((rows, hidden), F32), pltpu.VMEM((rows, breadth), F32), pltpu.VMEM((rows, breadth), LOW),
            pltpu.VMEM((rows, hidden), LOW), pltpu.VMEM((breadth, rows), LOW),
        ],
        compiler_params=pltpu.CompilerParams(vmem_limit_bytes=60 * MIB),
        name="feed_forward",
    )(seq, tokens, cotangent, ctx_low, vec, w_out, w_up, w_down)


def backward_call(seq, tokens, feat, w_qkv, rpe, scaled, phi, low, den, ctx, g_ctx, g_hidden, vec):
    rows, breadth = tokens.shape
    span = 2 * rows
    return pl.pallas_call(
        backward_kernel,
        out_shape=(
            shape((rows, breadth), F32), shape(w_qkv.shape, LOW), shape(vec.shape, F32), shape(rpe.shape, F32),
        ),
        in_specs=[SCALARS] + vmem(11),
        out_specs=tuple(vmem(4)),
        scratch_shapes=[
            pltpu.VMEM((rows, rows), F32), pltpu.VMEM((breadth // 256, 256, 256), LOW),
            pltpu.VMEM((256, 256), LOW), pltpu.VMEM((128, span), F32), pltpu.VMEM((rows, 3 * breadth), F32),
            pltpu.VMEM((rows, 3 * breadth), LOW), pltpu.VMEM((rows, rows), LOW), pltpu.VMEM((rows, rows), LOW),
            pltpu.VMEM((128, span), F32), pltpu.VMEM((rows, 128), LOW), pltpu.VMEM((rows, 128), LOW),
            pltpu.VMEM((rows, 128), LOW), pltpu.VMEM((rows, 128), LOW), pltpu.VMEM((breadth, rows), LOW),
        ],
        compiler_params=pltpu.CompilerParams(vmem_limit_bytes=60 * MIB),
        name="attend_back",
    )(seq, tokens, feat, w_qkv, rpe, scaled, phi, low, den, ctx, g_ctx, g_hidden)


PIECE = 16
BLOCK_ROWS = 256


def place():
    me = lax.axis_index("dp")
    core = lax.rem(me, 2)
    x = lax.rem(me // 2, 2)
    y = lax.rem(me // 4, 2)
    z = me // 8
    first = x * (1 - core) + y * core
    second = y * (1 - core) + x * core
    return core, z, first, second


class Plane:
    def __init__(self, depth):
        self.depth = depth
        self.core, self.z, self.first, self.second = place()
        self.chip = self.at(self.z, self.first, self.second)
        self.sibling = self.chip * 2 + 1 - self.core
        self.over_first = self.device(self.z, 1 - self.first, self.second)
        self.over_second = self.device(self.z, self.first, 1 - self.second)

    def at(self, z, first, second):
        return 4 * z + first * (1 + self.core) + second * (2 - self.core)

    def device(self, z, first, second):
        return 2 * self.at(z, first, second) + self.core

    def spot(self, first, second):
        return first * (1 + self.core) + second * (2 - self.core)

    def ahead(self, distance):
        return lax.rem(self.z + distance, self.depth)

    def behind(self, distance):
        return lax.rem(self.z + self.depth - distance, self.depth)

    def greet(self):
        barrier = pltpu.get_barrier_semaphore()
        others = [self.sibling, self.over_first, self.over_second]
        others += [self.device(self.ahead(d), self.first, self.second) for d in range(1, self.depth)]
        for other in others:
            pl.semaphore_signal(barrier, inc=1, device_id=(other,), device_id_type=MESH)
        pl.semaphore_wait(barrier, len(others))


def remote(source, target, sems, item, slot, device):
    return pltpu.make_async_remote_copy(
        src_ref=source, dst_ref=target, send_sem=sems[0].at[item, slot], recv_sem=sems[1].at[item, slot],
        device_id=(device,), device_id_type=MESH,
    )


def each(count, step):
    def run(index, carry):
        step(index)
        return carry

    lax.fori_loop(0, count, run, 0)


def span(start, stop, step):
    def run(index, carry):
        step(index)
        return carry

    lax.fori_loop(start, stop, run, 0)


def half(ref, zs, spot, core):
    if len(ref.shape) == 5:
        return ref.at[zs, spot, core]
    breadth = ref.shape[3] // 2
    return ref.at[zs, spot, :, pl.ds(pl.multiple_of(core * breadth, 128), breadth)]


ALL = slice(None)


class Gather:
    def __init__(self, plane, full, sems):
        self.plane, self.full, self.sems = plane, full, sems
        self.here = plane.spot(plane.first, plane.second)
        self.across = plane.spot(1 - plane.first, plane.second)
        self.first_slot = plane.depth - 1
        self.second_slot = self.first_slot + 1
        self.core_slot = self.second_slot + 2

    def copy(self, item, zs, spot, slot, device, core=None):
        part = half(self.full[item], zs, spot, self.plane.core if core is None else core)
        return remote(part, part, self.sems, item, slot, device)

    def to_depth(self, item, distance):
        plane = self.plane
        target = plane.device(plane.ahead(distance), plane.first, plane.second)
        return self.copy(item, plane.z, self.here, distance - 1, target)

    def to_first(self, item):
        return self.copy(item, ALL, self.here, self.first_slot, self.plane.over_first)

    def to_second(self, item, first):
        spot = self.plane.spot(first, self.plane.second)
        return self.copy(item, ALL, spot, self.second_slot + first, self.plane.over_second)

    def to_core(self, item, spot):
        return self.copy(item, ALL, spot, self.core_slot + spot, self.plane.sibling)

    def begin(self, item):
        for distance in range(1, self.plane.depth):
            self.to_depth(item, distance).start()

    def over_depth(self, item):
        plane = self.plane
        for distance in range(1, plane.depth):
            self.copy(item, plane.behind(distance), self.here, distance - 1, plane.sibling).wait_recv()
        self.to_first(item).start()
        self.to_second(item, plane.first).start()
        self.to_core(item, self.here).start()

    def over_first(self, item):
        plane = self.plane
        self.copy(item, ALL, self.across, self.first_slot, plane.over_first).wait_recv()
        self.to_second(item, 1 - plane.first).start()
        self.to_core(item, self.across).start()

    def over_second(self, item):
        plane = self.plane
        for first in (plane.first, 1 - plane.first):
            spot = plane.spot(first, 1 - plane.second)
            self.copy(item, ALL, spot, self.second_slot + first, plane.over_second).wait_recv()
            self.to_core(item, spot).start()

    def over_core(self, item):
        plane = self.plane
        for spot in range(4):
            self.copy(item, ALL, spot, self.core_slot + spot, plane.sibling, 1 - plane.core).wait_recv()

    def sent(self, item):
        plane = self.plane
        for distance in range(1, plane.depth):
            self.to_depth(item, distance).wait_send()
        self.to_first(item).wait_send()
        for first in range(2):
            self.to_second(item, first).wait_send()
        for spot in range(4):
            self.to_core(item, spot).wait_send()


def one_hot(length, breadth):
    factor = (1 << 20) // length + 1
    col = iota((128, breadth), 1)
    owner = lax.shift_right_logical(col * factor, 20)
    return jnp.where(iota((128, breadth), 0) == col - owner * length, 1.0, 0.0).astype(LOW)


def owned(devices, length, breadth):
    factor = (1 << 20) // length + 1
    col = iota((devices, breadth), 1)
    return lax.shift_right_logical(col * factor, 20) == iota((devices, breadth), 0)


def pack_small(piece_refs, small_ref):
    small_ref[...] = jnp.zeros_like(small_ref)
    for row, piece in enumerate(piece_refs[:-1]):
        small_ref[row : row + 1, 0 : piece.shape[1]] = piece[...].astype(LOW).astype(F32)
    table = piece_refs[-1]
    for part in range(table.shape[1] // 128):
        row = len(piece_refs) - 1 + part
        small_ref[row : row + 1, :] = table[:, 128 * part : 128 * part + 128].astype(LOW).astype(F32)


def unpack_small(all_ref, lengths, table_rows, vec_ref, rpe_ref):
    devices = all_ref.shape[0] // PIECE
    vec_ref[...] = jnp.zeros_like(vec_ref)
    for row, length in enumerate(lengths):
        breadth = length * devices
        picked = all_ref[pl.ds(row, devices, stride=PIECE), :].astype(LOW)
        spread = jnp.where(owned(devices, length, breadth), mm(picked, one_hot(length, breadth)), 0.0)
        vec_ref[row : row + 1, 0:breadth] = column_sum(spread)
    for part in range(table_rows):
        rpe_ref[pl.ds(part, devices, stride=table_rows), :] = all_ref[
            pl.ds(len(lengths) + part, devices, stride=PIECE), :
        ]


ANYWHERE = pl.BlockSpec(memory_space=pl.ANY)


class Saver:
    def __init__(self, sources, targets, sems):
        self.copies = [
            pltpu.make_async_copy(source, target, sems.at[index])
            for index, (source, target) in enumerate(zip(sources, targets))
        ]

    def start(self, *indices):
        for index in indices:
            self.copies[index].start()

    def finish(self):
        for copy in self.copies:
            copy.wait()


def norm_forward(tokens_ref, wide_ref, vec_ref, xhat_ref, inverse_ref, normed_ref, normed_low_ref):
    rows, breadth = tokens_ref.shape
    gain, bias = vec_ref[3:4, :breadth], vec_ref[4:5, :breadth]

    def step(index):
        at = pl.ds(pl.multiple_of(index * 128, 128), 128)
        xhat, inverse = norm(tokens_ref[at, :].astype(F32) + wide_ref[at, :])
        xhat_ref[at, :] = xhat
        inverse_ref[at, :] = jnp.broadcast_to(inverse, (128, 128))
        normed = xhat * gain + bias
        normed_ref[at, :] = normed
        normed_low_ref[at, :] = normed.astype(LOW)

    each(rows // 128, step)


def norm_result(seq_ref, normed_ref, wide_ref, vec_ref, cot_ref, out_ref, g_sum_ref, gvec_ref):
    rows, breadth = normed_ref.shape
    gain, bias = vec_ref[6:7, :breadth], vec_ref[7:8, :breadth]
    valid_rows = seq_ref[0, 0] + seq_ref[0, 1]
    gvec_ref[...] = jnp.zeros_like(gvec_ref)

    def step(index):
        at = pl.ds(pl.multiple_of(index * 128, 128), 128)
        xhat, inverse = norm(normed_ref[at, :] + wide_ref[at, :])
        out_ref[at, :] = (xhat * gain + bias).astype(LOW)
        spot = iota((128, breadth), 0) + index * 128
        grad = jnp.where(spot < valid_rows, cot_ref[at, :].astype(F32), 0.0)
        add_to(gvec_ref, 6, column_sum(grad * xhat))
        add_to(gvec_ref, 7, column_sum(grad))
        g_sum = norm_back(grad, xhat, inverse, gain)
        add_to(gvec_ref, 5, column_sum(g_sum))
        g_sum_ref[at, :] = g_sum

    each(rows // 128, step)


def attend_pair(pair, q_at, k_at, v_at, low_ref, rpe_ref, mask_ref, den_ref, ctx_ref, ctx_low_ref, coef_ref, key_ref, score_ref, serve):
    rows = mask_ref.shape[0]
    tall = BLOCK_ROWS
    lower = iota((tall, 128), 1) < 64
    here = cols(pair, 128)
    for side in range(2):
        serve(pair, side)
        coefficients(rpe_ref, pair * 2 + side, coef_ref)
        keep_half(low_ref, k_at, key_ref, side)
        for block in range(rows // tall):
            at = slice(block * tall, block * tall + tall)
            kernel = mm(low_ref[at, q_at], key_ref[...], 1, 1)
            totals = []
            for part in range(tall // 128):
                start = block * tall + part * 128
                lead = rows - 128 - start
                weight = coef_ref[:, lead : lead + rows] * mask_ref[start : start + 128, :]
                scores = kernel[part * 128 : part * 128 + 128] * weight
                totals.append(jnp.sum(scores, axis=1, keepdims=True))
                score_ref[start : start + 128, :] = scores.astype(LOW)
            total = jnp.broadcast_to(jnp.concatenate(totals, axis=0), (tall, 128))
            context = mm(score_ref[at, :], low_ref[:, v_at]) * (1.0 / total)
            if side == 0:
                den_ref[at, here] = total
                ctx_ref[at, here] = context
            else:
                den_ref[at, here] = jnp.where(lower, den_ref[at, here], total)
                context = jnp.where(lower, ctx_ref[at, here], context)
                ctx_ref[at, here] = context
                ctx_low_ref[at, here] = context.astype(LOW)


def upward_tile(normed_low_ref, w, bias, act_ref, slope_ref, where):
    upward = mm(normed_low_ref[...], w[...]) + bias
    phi = 0.5 + 0.5 * lax.erf(upward * 0.5**0.5)
    density = jnp.exp(-0.5 * upward * upward) * 0.3989422804014327
    act_ref[:, where] = (upward * phi).astype(LOW)
    slope_ref[:, where] = phi + upward * density


def build_stack(feat_ref, stack_ref):
    tile = stack_ref.shape[2]
    head_size = feat_ref.shape[1]
    group = tile // head_size
    bits = head_size.bit_length() - 1
    same = lax.shift_right_logical(iota((tile, tile), 0), bits) == lax.shift_right_logical(iota((tile, tile), 1), bits)
    half = jnp.where(same, -0.5, 0.0).astype(LOW)
    for index in range(stack_ref.shape[0]):
        rows_of = []
        for inner in range(group):
            piece = feat_ref[index * group + inner].astype(F32)
            rows_of.append(jnp.concatenate([piece] * group, axis=1))
        full = jnp.where(same, jnp.concatenate(rows_of, axis=0), 0.0).astype(LOW)
        for part, value in enumerate((full, full, half, half)):
            stack_ref[index, part * tile : part * tile + tile, :] = value


def two_parts(value):
    high = value.astype(LOW)
    return [high, (value - high.astype(F32)).astype(LOW)]


def segment_mask(seq_ref, mask_ref):
    rows = mask_ref.shape[0]
    first_end = seq_ref[0, 0]
    second_end = first_end + seq_ref[0, 1]

    def segment(place):
        return (place >= first_end).astype(jnp.int32) + (place >= second_end).astype(jnp.int32)

    across = segment(iota((128, rows), 1))
    for start in range(0, rows, 128):
        down = segment(iota((128, rows), 0) + start)
        mask_ref[start : start + 128, :] = jnp.where(down == across, 1.0, 0.0)


def ahead_kernel(depth, pieces, *refs):
    seq_ref, tokens_ref, cot_ref, feat_ref, refs = refs[0], refs[1], refs[2], refs[3], refs[4:]
    matrices, refs = refs[:4], refs[4:]
    piece_refs, refs = refs[:pieces], refs[pieces:]
    out_ref, gvec_ref, vec_ref, rpe_ref, wide_ref, refs = refs[:5] + (refs[5:],)
    weights_hbm, kept_hbm, refs = refs[:4], refs[4:15], refs[15:]
    w_qkv, w_out, w_up, w_down, refs = refs[:4] + (refs[4:],)
    kept, refs = refs[:11], refs[11:]
    peers, refs = refs[:4], refs[4:]
    small_ref, all_ref, mask_ref, stack_ref, coef_ref, key_ref, score_ref, normed_ref = refs[:8]
    send, recv, peer_send, peer_recv, save_sem = refs[8:]
    scaled_ref, phi_ref, low_ref, den_ref, ctx_ref, ctx_low_ref = kept[:6]
    normed_low_ref, xhat_ref, inverse_ref, act_ref, slope_ref = kept[6:]
    rows, breadth = tokens_ref.shape
    groups, tile = w_qkv.shape[0], stack_ref.shape[2]
    up_tile, down_tile = w_up.shape[4], w_down.shape[4]

    plane = Plane(depth)
    core = plane.core
    pack_small(piece_refs, small_ref)
    thirds = range(groups)
    full = [all_ref] + [w_qkv.at[g] for g in thirds] + [w_out]
    full += [w_up.at[g] for g in thirds] + [w_down.at[g] for g in thirds]
    gather = Gather(plane, full, (send, recv))
    all_ref[plane.z, gather.here, core] = small_ref[...]
    plane.greet()
    swaps = [
        remote(matrix, peer, (peer_send, peer_recv), 0, index, plane.sibling)
        for index, (matrix, peer) in enumerate(zip(matrices, peers))
    ]
    for swap in swaps:
        swap.start()

    def assemble(item, matrix, starts, breadth_of):
        mine, other = matrices[matrix], peers[matrix]
        offset = core * (len(starts) * breadth_of)
        for number, start in enumerate(starts):
            at = pl.ds(pl.multiple_of(start, 128), breadth_of)
            own, peer = mine[:, at], other[:, at]
            both = jnp.concatenate([jnp.where(core == 0, own, peer), jnp.where(core == 0, peer, own)], axis=0)
            to = pl.ds(pl.multiple_of(offset + number * breadth_of, 128), breadth_of)
            full[item][plane.z, gather.here, :, to] = both.astype(LOW)

    def assemble_qkv(group):
        starts = []
        for number in range(3):
            place_of = 3 * core + number
            starts.append((place_of // 2) * breadth + group * tile + lax.rem(place_of, 2) * 128)
        assemble(1 + group, 0, starts, 128)

    flat_qkv = w_qkv.reshape(groups, breadth, 3 * tile)
    flat_out = w_out.reshape(breadth, breadth)
    flat_up = w_up.reshape(groups, breadth, up_tile)
    flat_down = w_down.reshape(groups, w_down.shape[1] * w_down.shape[2] * w_down.shape[3], down_tile)
    sources = [flat_qkv.at[g] for g in thirds] + [flat_out] + [flat_up.at[g] for g in thirds]
    sources += [flat_down.at[g] for g in thirds]
    targets = [weights_hbm[0].at[g] for g in thirds] + [weights_hbm[1]]
    targets += [weights_hbm[2].at[:, g * up_tile : g * up_tile + up_tile] for g in thirds]
    targets += [weights_hbm[3].at[:, g * down_tile : g * down_tile + down_tile] for g in thirds]
    saver = Saver(sources + list(kept), targets + list(kept_hbm), save_sem)
    first_kept = len(targets)

    def keep(*indices):
        saver.start(*[first_kept + index for index in indices])

    begin, along, first, second = gather.begin, gather.over_depth, gather.over_first, gather.over_second

    def whole(item):
        gather.over_core(item)
        if item:
            saver.start(item - 1)

    plan = {
        ("head", 1): ((second, 2), (along, 5)),
        ("head", 3): ((first, 4), (begin, 8), (whole, 2), (along, 6), (begin, 7)),
        ("project", 1): ((first, 5), (second, 3)),
        ("head", 5): ((second, 4),),
        ("project", 2): (
            (along, 7), (second, 5), (whole, 3), (begin, 9), (first, 6), (along, 8), (first, 7), (whole, 4),
        ),
        ("head", 8): ((whole, 5), (second, 6), (first, 8), (begin, 10)),
        ("head", 11): ((along, 9), (second, 7)),
        ("up", 0): ((second, 8), (first, 9), (whole, 6)),
        ("up", 2): ((first, 10), (whole, 8)),
        ("down", 0): ((second, 9),),
        ("down", 1): ((whole, 9), (second, 10)),
        ("down", 2): ((whole, 10),),
    }

    def serve(kind, index):
        for (work, number), steps in plan.items():
            if work == kind:

                @pl.when(index == number)
                def _(steps=steps):
                    for step, item in steps:
                        step(item)

    begin(0)
    swaps[0].wait_recv()
    assemble_qkv(0)
    begin(1)
    assemble_qkv(1)
    assemble_qkv(2)
    for swap in swaps[1:]:
        swap.wait_recv()
    assemble(4, 1, [core * (breadth // 2)], breadth // 2)
    for group in thirds:
        assemble(5 + group, 2, [group * up_tile + core * (up_tile // 2)], up_tile // 2)
        assemble(8 + group, 3, [group * down_tile + core * (down_tile // 2)], down_tile // 2)
    along(0)
    begin(2)
    segment_mask(seq_ref, mask_ref)
    first(0)
    along(1)
    second(0)
    along(2)
    begin(3)
    whole(0)
    begin(4)
    build_stack(feat_ref, stack_ref)
    first(1)
    along(3)
    first(2)
    begin(5)
    second(1)
    lengths = [piece.shape[1] for piece in piece_refs[:-1]]
    flat_all = all_ref.reshape(8 * depth * PIECE, 128)
    unpack_small(flat_all, lengths, piece_refs[-1].shape[1] // 128, vec_ref, rpe_ref)
    along(4)
    begin(6)
    whole(1)
    first(3)
    scale = 64 ** (-0.25)

    def serve_pair(pair, side):
        for (work, number), steps in plan.items():
            if work == "head" and number % 2 == side:

                @pl.when(pair == number // 2)
                def _(steps=steps):
                    for step, item in steps:
                        step(item)

    def group_step(group):
        serve("project", group)
        wide_ref[...] = mm(tokens_ref[...], flat_qkv[group])
        for part in range(3):
            where = pl.ds(pl.multiple_of(part * breadth + group * tile, tile), tile)
            value = wide_ref[:, part * tile : part * tile + tile] + vec_ref[0:1, where]
            if part < 2:
                scaled = value * scale
                scaled_ref[:, where] = scaled
                operand = jnp.concatenate(two_parts(scaled) + two_parts(scaled * scaled), axis=1)
                value = jnp.exp(mm(operand, stack_ref[group])) * 0.125
                phi_ref[:, where] = value
            low_ref[:, where] = value.astype(LOW)

        def pair_step(inner):
            pair = 2 * group + inner
            attend_pair(
                pair, cols(pair, 128), pl.ds(pl.multiple_of(pair * 128 + breadth, 128), 128),
                pl.ds(pl.multiple_of(pair * 128 + 2 * breadth, 128), 128),
                low_ref, rpe_ref, mask_ref, den_ref, ctx_ref, ctx_low_ref, coef_ref, key_ref, score_ref, serve_pair,
            )

        each(2, pair_step)

    each(groups, group_step)
    keep(0, 1, 2, 3, 4, 5)
    along(10)
    whole(7)
    wide_ref[...] = mm(ctx_low_ref[...], flat_out[...]) + vec_ref[2:3, :breadth]
    norm_forward(tokens_ref, wide_ref, vec_ref, xhat_ref, inverse_ref, normed_ref, normed_low_ref)
    keep(6, 7, 8)

    def upward_step(index):
        serve("up", index)
        where = cols(index, up_tile)
        upward_tile(normed_low_ref, flat_up.at[index], vec_ref[1:2, where], act_ref, slope_ref, where)

    each(groups, upward_step)
    keep(9, 10)

    def downward_step(index):
        serve("down", index)
        where = cols(index, down_tile)
        wide_ref[:, where] = mm(act_ref[...], flat_down[index]) + vec_ref[5:6, where]

    each(groups, downward_step)
    norm_result(seq_ref, normed_ref, wide_ref, vec_ref, cot_ref, out_ref, wide_ref, gvec_ref)
    for item in range(len(full)):
        gather.sent(item)
    for swap in swaps:
        swap.wait_send()
    saver.finish()


def ahead_call(depth, seq, tokens, cotangent, feat, matrices, pieces):
    rows, breadth = tokens.shape
    span_length = 2 * rows
    devices = 8 * depth
    groups, tile = 3, 256
    slots = depth - 1 + 1 + 2 + 4
    longest = max(piece.shape[1] for piece in pieces[:-1]) * devices
    table = pieces[-1].shape[1] * devices // 128
    w_qkv, w_out, w_up, w_down = matrices
    hidden = w_up.shape[1]
    lead = (depth, 4)
    full = [
        (groups,) + lead + (2 * w_qkv.shape[0], 3 * tile), lead + (2 * w_out.shape[0], breadth),
        (groups,) + lead + (2 * w_up.shape[0], hidden // groups),
        (groups,) + lead + (2 * w_down.shape[0], breadth // groups),
    ]
    saved = [(groups, breadth, 3 * tile), (breadth, breadth), (devices * w_up.shape[0], hidden), (devices * w_down.shape[0], breadth)]
    kept = [
        ((rows, 2 * breadth), F32), ((rows, 2 * breadth), F32), ((rows, 3 * breadth), LOW),
        ((rows, breadth), F32), ((rows, breadth), F32), ((rows, breadth), LOW),
        ((rows, breadth), LOW), ((rows, breadth), F32), ((rows, 128), F32), ((rows, hidden), LOW),
        ((rows, hidden), F32),
    ]
    items = 2 + 3 * groups
    return pl.pallas_call(
        functools.partial(ahead_kernel, depth, len(pieces)),
        out_shape=(
            shape((rows, breadth), LOW), shape((len(pieces) - 1, longest), F32),
            shape((len(pieces) - 1, longest), F32), shape((table, 128), F32), shape((rows, breadth), F32),
        )
        + tuple(shape(dims, LOW) for dims in saved)
        + tuple(shape(dims, kind) for dims, kind in kept),
        in_specs=[SCALARS] + vmem(3 + len(matrices) + len(pieces)),
        out_specs=tuple(vmem(5)) + (ANYWHERE,) * len(saved + kept),
        scratch_shapes=[pltpu.VMEM(dims, LOW) for dims in full]
        + [pltpu.VMEM(dims, kind) for dims, kind in kept]
        + [pltpu.VMEM(matrix.shape, F32) for matrix in matrices]
        + [
            pltpu.VMEM((PIECE, 128), F32), pltpu.VMEM((depth, 4, 2, PIECE, 128), F32),
            pltpu.VMEM((rows, rows), F32), pltpu.VMEM((groups, 4 * tile, tile), LOW),
            pltpu.VMEM((128, span_length), F32), pltpu.VMEM((rows, 128), LOW), pltpu.VMEM((rows, rows), LOW),
            pltpu.VMEM((rows, breadth), F32),
            pltpu.SemaphoreType.DMA((items, slots)), pltpu.SemaphoreType.DMA((items, slots)),
            pltpu.SemaphoreType.DMA((1, 4)), pltpu.SemaphoreType.DMA((1, 4)), pltpu.SemaphoreType.DMA((items - 1 + len(kept),)),
        ],
        compiler_params=pltpu.CompilerParams(
            collective_id=0, has_side_effects=True, vmem_limit_bytes=60 * MIB
        ),
        name="ahead",
    )(seq, tokens, cotangent, feat, *matrices, *pieces)


def prepare_back(group, slot, low_ref, den_ref, ctx_ref, g_ctx_ref, swap_ref, ext_ref, key_ref, val_ref, num_ref, flip_ref):
    rows = g_ctx_ref.shape[0]
    breadth = swap_ref.shape[0]
    where = cols(group, breadth)
    lane = jnp.bitwise_and(iota((128, breadth), 1), 127)
    lower = lane < 64

    def step(index):
        at = pl.ds(pl.multiple_of(index * 128, 128), 128)
        g_num = g_ctx_ref[at, where] * (1.0 / den_ref[slot, at, :])
        g_den = -mm2(g_num * ctx_ref[slot, at, :], swap_ref[...])
        high = g_den.astype(LOW).astype(F32)
        rest = g_den - high
        key = low_ref[slot, 1, at, :].astype(F32)
        value = low_ref[slot, 2, at, :].astype(F32)
        for side in range(2):
            mine = jnp.logical_not(lower) if side else lower
            other = 0 if side else 64
            is_high, is_rest = lane == other, lane == other + 1
            extended = jnp.where(mine, g_num, jnp.where(is_high, high, jnp.where(is_rest, rest, 0.0)))
            ext_ref[side, at, :] = extended.astype(LOW)
            key_ref[side, at, :] = jnp.where(mine, key, 0.0).astype(LOW)
            ones = jnp.where(jnp.logical_or(is_high, is_rest), 1.0, 0.0)
            val_ref[side, at, :] = jnp.where(mine, value, ones).astype(LOW)
        num_ref[at, :] = g_num.astype(LOW)

    each(rows // 128, step)
    flip_ref[0] = jnp.transpose(low_ref[slot, 0])
    flip_ref[1] = jnp.transpose(num_ref[...])


def attend_back_pair(
    pair, inner, slot, low_ref, rpe_ref, mask_ref, g_feat_ref, grpe_ref, coef_ref, scores_ref, gk_ref, diag_ref,
    ext_ref, key_ref, val_ref, flip_ref, turn_ref, serve,
):
    rows = mask_ref.shape[0]
    tall = BLOCK_ROWS
    here = cols(inner, 128)
    lower = iota((tall, 128), 1) < 64
    for side in range(2):
        serve(pair, side)
        coefficients(rpe_ref, pair * 2 + side, coef_ref)
        diag_ref[...] = jnp.zeros_like(diag_ref)
        for block in range(rows // tall):
            at = slice(block * tall, block * tall + tall)
            kernel = mm(low_ref[slot, 0, at, here], key_ref[side, :, here], 1, 1)
            g_scores = mm(ext_ref[side, at, here], val_ref[side, :, here], 1, 1)
            for part in range(tall // 128):
                start = block * tall + part * 128
                lead = rows - 128 - start
                inside = slice(part * 128, part * 128 + 128)
                weight = coef_ref[:, lead : lead + rows] * mask_ref[start : start + 128, :]
                scores = kernel[inside] * weight
                diag_ref[:, lead : lead + rows] += g_scores[inside] * scores
                scores_ref[start : start + 128, :] = scores.astype(LOW)
                gk_ref[start : start + 128, :] = (g_scores[inside] * weight).astype(LOW)
            g_query = mm(gk_ref[at, :], low_ref[slot, 1, :, here])
            if side:
                g_query = jnp.where(lower, g_feat_ref[at, here], g_query)
            g_feat_ref[at, here] = g_query
        head_rows = pl.ds(pl.multiple_of(inner * 128 + side * 64, 64), 64)
        turn_ref[0, head_rows, :] = mm(flip_ref[0, head_rows, :], gk_ref[...])
        turn_ref[1, head_rows, :] = mm(flip_ref[1, head_rows, :], scores_ref[...])
        diagonals(diag_ref, grpe_ref, pair * 2 + side)


def diagonals(diag_ref, out_ref, head):
    flip = jnp.where(iota((128, 128), 0) + iota((128, 128), 1) == 127, 1.0, 0.0).astype(LOW)
    value = diag_ref[...]
    high = value.astype(LOW)
    rest = (value - high.astype(F32)).astype(LOW)
    value = pltpu.roll(mm(flip, high) + mm(flip, rest), 0, axis=1, stride=1, stride_axis=0)
    sums = jnp.sum(value, axis=0, keepdims=True)
    for k in range(8):
        out_ref[pl.ds(head * 8 + 7 - k, 1), :] = sums[:, 128 * k : 128 * k + 128]


class Item:
    def __init__(self, given, buffers, row):
        self.given = given
        self.from_core, self.from_second, self.from_first, self.from_depth, self.leaving = buffers
        self.row = row


class Scatter:
    def __init__(self, plane, sems):
        self.plane, self.sems = plane, sems
        self.here = plane.spot(plane.first, plane.second)
        self.across = plane.spot(1 - plane.first, plane.second)
        self.first_slot = plane.depth - 1
        self.second_slot = self.first_slot + 1
        self.core_slot = self.second_slot + 2
        self.last_slot = self.core_slot + 1

    def with_core(self, item):
        return remote(
            half(item.given, ALL, ALL, 1 - self.plane.core), item.from_core, self.sems, item.row, self.core_slot,
            self.plane.sibling,
        )

    def begin(self, item):
        self.with_core(item).start()

    def to_second(self, item, first):
        spot = self.plane.spot(first, 1 - self.plane.second)
        return remote(
            half(item.given, ALL, spot, self.plane.core), item.from_second.at[first], self.sems, item.row,
            self.second_slot + first, self.plane.over_second,
        )

    def to_first(self, item):
        return remote(
            half(item.given, ALL, self.across, self.plane.core), item.from_first, self.sems, item.row,
            self.first_slot, self.plane.over_first,
        )

    def to_depth(self, item, distance):
        plane = self.plane
        z = plane.ahead(distance)
        return remote(
            half(item.given, z, self.here, plane.core), item.from_depth.at[distance - 1], self.sems, item.row,
            distance - 1, plane.device(z, plane.first, plane.second),
        )

    def join(self, item, spot, piece):
        def step(z):
            target = half(item.given, z, spot, self.plane.core)
            target[...] = target[...] + piece(z)

        each(self.plane.depth, step)

    def core(self, item):
        plane = self.plane
        self.with_core(item).wait_recv()
        for first in range(2):
            spot = plane.spot(first, 1 - plane.second)
            self.join(item, spot, lambda z, spot=spot: item.from_core[z, spot])
            self.to_second(item, first).start()
        for first in range(2):
            spot = plane.spot(first, plane.second)
            self.join(item, spot, lambda z, spot=spot: item.from_core[z, spot])

    def second(self, item):
        plane = self.plane
        away = 1 - plane.first
        self.to_second(item, away).wait_recv()
        self.join(item, self.across, lambda z: item.from_second[away, z])
        self.to_first(item).start()
        self.to_second(item, plane.first).wait_recv()
        self.join(item, self.here, lambda z: item.from_second[plane.first, z])

    def first(self, item):
        self.to_first(item).wait_recv()
        self.join(item, self.here, lambda z: item.from_first[z])
        for distance in range(1, self.plane.depth):
            self.to_depth(item, distance).start()

    def summed(self, item):
        plane = self.plane
        for distance in range(1, plane.depth):
            self.to_depth(item, distance).wait_recv()
        value = half(item.given, plane.z, self.here, plane.core)[...].astype(F32)
        for distance in range(1, plane.depth):
            value = value + item.from_depth[distance - 1].astype(F32)
        return value

    def columns(self, item, core):
        breadth = item.leaving.shape[1]
        return pl.ds(pl.multiple_of(core * breadth, 128), breadth)

    def last(self, item, target):
        core = self.plane.core
        return remote(
            item.leaving, target.at[:, self.columns(item, core)], self.sems, item.row, self.last_slot,
            self.plane.sibling,
        )

    def along(self, item, target):
        core = self.plane.core
        value = self.summed(item)
        height = value.shape[0] // 2
        upper, lower = value[:height], value[height:]
        target[:, self.columns(item, core)] = jnp.where(core == 0, upper, lower)
        item.leaving[...] = jnp.where(core == 0, lower, upper)
        self.last(item, target).start()

    def sent(self, item, target=None):
        self.with_core(item).wait_send()
        for first in range(2):
            self.to_second(item, first).wait_send()
        self.to_first(item).wait_send()
        for distance in range(1, self.plane.depth):
            self.to_depth(item, distance).wait_send()
        if target is not None:
            core = self.plane.core
            self.last(item, target).wait_send()
            arrived = target.at[:, self.columns(item, 1 - core)]
            remote(
                item.leaving, arrived, self.sems, item.row, self.last_slot, self.plane.sibling
            ).wait_recv()


def pack_grads(gvec_ref, lengths, grpe_ref, flat_ref):
    devices = flat_ref.shape[0] // PIECE
    table_rows = grpe_ref.shape[0] // devices
    flat_ref[...] = jnp.zeros_like(flat_ref)
    for row, length in enumerate(lengths):
        breadth = length * devices
        value = gvec_ref[row : row + 1, 0:breadth]
        spread = jnp.where(owned(devices, length, breadth), jnp.broadcast_to(value, (devices, breadth)), 0.0)
        flat_ref[pl.ds(row, devices, stride=PIECE), :] = mm2(spread, one_hot(length, breadth), 1)
    for part in range(table_rows):
        flat_ref[pl.ds(len(lengths) + part, devices, stride=PIECE), :] = grpe_ref[
            pl.ds(part, devices, stride=table_rows), :
        ]


def build_back(feat_ref, stack_ref):
    tile = stack_ref.shape[2]
    head_size = feat_ref.shape[1]
    group = tile // head_size
    bits = head_size.bit_length() - 1
    same = lax.shift_right_logical(iota((tile, tile), 0), bits) == lax.shift_right_logical(iota((tile, tile), 1), bits)
    last = stack_ref.shape[0] - 1
    for index in range(last):
        rows_of = []
        for inner in range(group):
            piece = jnp.transpose(feat_ref[index * group + inner].astype(F32))
            rows_of.append(jnp.concatenate([piece] * group, axis=1))
        full = jnp.where(same, jnp.concatenate(rows_of, axis=0), 0.0).astype(LOW)
        for part in range(2):
            stack_ref[index, part * tile : part * tile + tile, :] = full
    for part in range(2):
        stack_ref[last, part * tile : part * tile + tile, :] = jnp.where(same, 1.0, 0.0).astype(LOW)


def build_swap(swap_ref):
    tile = swap_ref.shape[0]
    down = lax.shift_right_logical(iota((tile, tile), 0), 6)
    across = lax.shift_right_logical(iota((tile, tile), 1), 6)
    swap_ref[...] = jnp.where(jnp.bitwise_xor(down, 1) == across, 1.0, 0.0).astype(LOW)


def behind_kernel(depth, lengths, *refs):
    seq_ref, feat_ref, vec_ref, rpe_ref, gvec_in_ref, g_sum_ref, refs = refs[:6] + (refs[6:],)
    w_qkv_hbm, w_out_hbm, w_up_hbm, w_down_hbm, refs = refs[:4] + (refs[4:],)
    scaled_hbm, phi_hbm, low_hbm, den_hbm, ctx_hbm, ctx_low_hbm, refs = refs[:6] + (refs[6:],)
    normed_low_hbm, xhat_hbm, inverse_hbm, act_hbm, slope_hbm, tokens_hbm, refs = refs[:6] + (refs[6:],)
    g_tokens_hbm, s_qkv, s_out, s_up, s_down, s_small, refs = refs[:6] + (refs[6:],)
    d_qkv, d_out, d_up, d_down, d_small, refs = refs[:5] + (refs[5:],)
    buffers, refs = [refs[5 * index : 5 * index + 5] for index in range(5)], refs[25:]
    g_hidden_ref, g_ctx_ref, g_low_ref, gvec_ref, grpe_ref, g_qkv_ref, refs = refs[:6] + (refs[6:],)
    send, recv, load_sem = refs
    rows, breadth = g_sum_ref.shape
    hidden = w_up_hbm.shape[1]
    tile, height = 256, 128
    wide = min(768, breadth)
    plane = Plane(depth)
    scatter = Scatter(plane, (send, recv))
    down, up, out = [
        Item(given, buffers[index], 2 - index)
        for given, index in ((d_down, 2), (d_up, 1), (d_out, 0))
    ]
    small = Item(d_small, buffers[4], 3)
    flat_down, flat_up, flat_out, flat_qkv = d_down.reshape(hidden, breadth), d_up.reshape(breadth, hidden), (
        d_out.reshape(breadth, breadth)
    ), d_qkv.reshape(breadth // tile, breadth, 3 * tile)
    flat_small = d_small.reshape(8 * depth * PIECE, 128)

    def qkv(group):
        return Item(d_qkv.at[group], [buffer.at[group] for buffer in buffers[3]], 4 + group)

    def load(source, target, index):
        return pltpu.make_async_copy(source, target, load_sem.at[index])

    def feed_forward(
        w_out_ref, w_up_ref, w_down_ref, act_ref, slope_ref, normed_low_ref, flip_ref,
        inverse_ref, ctx_low_ref,
    ):
        chunk = slope_ref.shape[2]
        chunks = hidden // chunk
        pending = {}

        def columns(index):
            return slice(index * chunk, index * chunk + chunk)

        acts = [
            load(act_hbm.at[:, columns(index)], act_ref.at[:, columns(index)], 2 * chunks + index)
            for index in range(chunks)
        ]

        def fetch(index):
            at = columns(index)
            pending[index] = [
                load(w_down_hbm.at[at, :], w_down_ref.at[at, :], 2 * index),
                load(slope_hbm.at[:, at], slope_ref.at[index % 2], 2 * index + 1),
            ]
            for copy in pending[index]:
                copy.start()

        for copy in acts:
            copy.start()
        fetch(0)
        fetch(1)
        base = 3 * chunks
        later = [
            load(normed_low_hbm, normed_low_ref, base), load(w_up_hbm, w_up_ref, base + 1),
            load(xhat_hbm, g_hidden_ref, base + 2), load(inverse_hbm, inverse_ref, base + 3),
            load(w_out_hbm, w_out_ref, base + 4), load(ctx_low_hbm, ctx_low_ref, base + 5),
        ]
        g_low_ref[...] = g_sum_ref[...].astype(LOW)
        gvec_ref[...] = gvec_in_ref[...]
        plane.greet()
        for index in range(chunks):
            acts[index].wait()

            at = columns(index)
            flat_down[at, :] = mm(act_ref[:, at], g_low_ref[...], 0, 0).astype(LOW)
        scatter.begin(down)
        for index in range(chunks):
            for copy in pending[index]:
                copy.wait()
            if index == 2:
                scatter.core(down)

            at = columns(index)
            g_upward = mm(g_low_ref[...], w_down_ref[at, :], 1, 1) * slope_ref[index % 2]
            gvec_ref[1:2, at] = column_sum(g_upward)
            act_ref[:, at] = g_upward.astype(LOW)
            if index + 2 < chunks:
                fetch(index + 2)
            if index == 0:
                for copy in later:
                    copy.start()
        for copy in later:
            copy.wait()
        flip_ref[...] = jnp.transpose(normed_low_ref[...])

        def up_step(step):
            where = cols(step, wide)
            flat_up[:, where] = mm(flip_ref[...], act_ref[:, where]).astype(LOW)

        each(hidden // wide, up_step)
        scatter.begin(up)

        g_sum_ref[...] = mm(act_ref[...], w_up_ref[...], 1, 1) + g_sum_ref[...]
        gain_one = vec_ref[3:4, :breadth]

        def first_back(step):
            at = pl.ds(pl.multiple_of(step * height, height), height)
            g_normed = g_sum_ref[at, :]
            xhat = g_hidden_ref[at, :]
            add_to(gvec_ref, 3, column_sum(g_normed * xhat))
            add_to(gvec_ref, 4, column_sum(g_normed))
            g_hidden = norm_back(g_normed, xhat, inverse_ref[at, 0:1], gain_one)
            add_to(gvec_ref, 2, column_sum(g_hidden))
            g_hidden_ref[at, :] = g_hidden
            g_low_ref[at, :] = g_hidden.astype(LOW)

        each(rows // height, first_back)

        flat_out[...] = mm(ctx_low_ref[...], g_low_ref[...], 0, 0).astype(LOW)
        scatter.begin(out)
        scatter.core(up)
        scatter.second(down)
        g_ctx_ref[...] = mm(g_low_ref[...], w_out_ref[...], 1, 1)

    chunk = min(768, hidden)
    pl.run_scoped(
        feed_forward,
        pltpu.VMEM(w_out_hbm.shape, LOW), pltpu.VMEM(w_up_hbm.shape, LOW), pltpu.VMEM(w_down_hbm.shape, LOW),
        pltpu.VMEM((rows, hidden), LOW), pltpu.VMEM((2, rows, chunk), F32),
        pltpu.VMEM((rows, breadth), LOW), pltpu.VMEM((breadth, rows), LOW),
        pltpu.VMEM((rows, 128), F32), pltpu.VMEM((rows, breadth), LOW),
    )

    calls = {
        4: (lambda: scatter.core(out), lambda: scatter.first(down)),
        7: (lambda: scatter.second(up),),
        9: (lambda: scatter.core(qkv(0)), lambda: scatter.first(up)),
        11: (lambda: scatter.second(out), lambda: scatter.core(qkv(1))),
    }

    def serve(pair, side):
        for head, steps in calls.items():
            if head % 2 == side:

                @pl.when(pair == head // 2)
                def _(steps=steps):
                    for step in steps:
                        step()

    def attention(
        w_qkv_ref, flip_ref, scaled_ref, phi_ref, low_ref, den_ref, ctx_ref, g_feat_ref, coef_ref,
        scores_ref, gk_ref, diag_ref, ext_ref, key_ref, val_ref, num_ref, turn_low_ref, turn_ref, swap_ref, mask_ref, stack_ref,
    ):
        groups = breadth // tile

        def part(ref, at, number):
            return ref.at[:, pl.ds(pl.multiple_of(at * tile + number * breadth, tile), tile)]

        def loads(group):
            slot = lax.rem(group, 2)
            copies = []
            for number in range(3):
                copies.append((part(low_hbm, group, number), low_ref.at[slot, number]))
            copies.append((part(den_hbm, group, 0), den_ref.at[slot]))
            copies.append((part(ctx_hbm, group, 0), ctx_ref.at[slot]))
            for number in range(2):
                copies.append((part(scaled_hbm, group, number), scaled_ref.at[slot, number]))
                copies.append((part(phi_hbm, group, number), phi_ref.at[slot, number]))
            return [
                load(source, target, slot * 9 + index) for index, (source, target) in enumerate(copies)
            ]

        base = 18
        tokens_copy = load(tokens_hbm, g_low_ref, base)

        def weights(group):
            return load(w_qkv_hbm.at[group], w_qkv_ref.at[group % 2], base + 1 + group)

        for copy in loads(0):
            copy.start()
        for copy in (tokens_copy, weights(0), weights(1)):
            copy.start()
        segment_mask(seq_ref, mask_ref)
        build_back(feat_ref, stack_ref)
        tokens_copy.wait()
        flip_ref[...] = jnp.transpose(g_low_ref[...])
        build_swap(swap_ref)
        scale = 64 ** (-0.25)

        def group_step(group):
            slot = lax.rem(group, 2)
            for copy in loads(group):
                copy.wait()

            @pl.when(group + 1 < groups)
            def _():
                for copy in loads(group + 1):
                    copy.start()

            prepare_back(
                group, slot, low_ref, den_ref, ctx_ref, g_ctx_ref, swap_ref, ext_ref, key_ref, val_ref, num_ref,
                turn_low_ref,
            )

            def pair_step(inner):
                pair = 2 * group + inner
                attend_back_pair(
                    pair, inner, slot, low_ref, rpe_ref, mask_ref, g_feat_ref, grpe_ref, coef_ref, scores_ref,
                    gk_ref, diag_ref, ext_ref, key_ref, val_ref, turn_low_ref, turn_ref, serve,
                )

            each(2, pair_step)

            g_feat_ref[:, tile : 2 * tile] = jnp.transpose(turn_ref[0])
            g_feat_ref[:, 2 * tile : 3 * tile] = jnp.transpose(turn_ref[1])
            for number in range(3):
                at = slice(number * tile, number * tile + tile)
                where = pl.ds(pl.multiple_of(group * tile + number * breadth, tile), tile)
                grad = g_feat_ref[:, at]
                if number < 2:
                    upward = jnp.concatenate(two_parts(grad * phi_ref[slot, number]), axis=1)
                    total = mm(upward, stack_ref[groups])
                    grad = mm(upward, stack_ref[group]) - scaled_ref[slot, number] * total
                    grad = grad * scale
                gvec_ref[0:1, where] = column_sum(grad)
                g_qkv_ref[group, :, at] = grad.astype(LOW)
            flat_qkv[group] = mm(flip_ref[...], g_qkv_ref[group]).astype(LOW)
            scatter.begin(qkv(group))

        each(groups, group_step)
        scatter.second(qkv(0))
        scatter.core(qkv(2))
        scatter.along(down, s_down)
        scatter.first(out)
        scatter.first(qkv(0))
        flip = jnp.where(iota((128, 128), 0) + iota((128, 128), 1) == 127, 1.0, 0.0).astype(LOW)
        grpe_ref[...] = mm2(grpe_ref[...], flip)
        pack_grads(gvec_ref, lengths, grpe_ref, flat_small)
        scatter.begin(small)
        scatter.second(qkv(1))

        def inputs(group):
            weights(group).wait()
            g_hidden_ref[...] += mm(g_qkv_ref[group], w_qkv_ref[group % 2], 1, 1)
            if group + 2 < groups:
                weights(group + 2).start()

        inputs(0)
        inputs(1)
        scatter.core(small)
        inputs(2)

    pl.run_scoped(
        attention,
        pltpu.VMEM((2,) + w_qkv_hbm.shape[1:], LOW), pltpu.VMEM((breadth, rows), LOW),
        pltpu.VMEM((2, 2, rows, tile), F32), pltpu.VMEM((2, 2, rows, tile), F32),
        pltpu.VMEM((2, 3, rows, tile), LOW), pltpu.VMEM((2, rows, tile), F32), pltpu.VMEM((2, rows, tile), F32),
        pltpu.VMEM((rows, 3 * tile), F32), pltpu.VMEM((128, 2 * rows), F32), pltpu.VMEM((rows, rows), LOW),
        pltpu.VMEM((rows, rows), LOW), pltpu.VMEM((128, 2 * rows), F32), pltpu.VMEM((2, rows, tile), LOW),
        pltpu.VMEM((2, rows, tile), LOW), pltpu.VMEM((2, rows, tile), LOW), pltpu.VMEM((rows, tile), LOW),
        pltpu.VMEM((2, tile, rows), LOW), pltpu.VMEM((2, tile, rows), F32), pltpu.VMEM((tile, tile), LOW),
        pltpu.VMEM((rows, rows), F32), pltpu.VMEM((breadth // tile + 1, 2 * tile, tile), LOW),
    )
    result = load(g_hidden_ref, g_tokens_hbm, 31)
    result.start()
    scatter.second(qkv(2))
    scatter.first(qkv(1))
    scatter.second(small)
    scatter.along(out, s_out)
    scatter.along(up, s_up)
    scatter.first(small)
    scatter.first(qkv(2))
    scatter.along(qkv(1), s_qkv.at[1])
    scatter.along(qkv(0), s_qkv.at[0])
    scatter.along(qkv(2), s_qkv.at[2])
    s_small[...] = scatter.summed(small)
    for item, target in ((down, s_down), (up, s_up), (out, s_out), (small, None)):
        scatter.sent(item, target)
    for group in range(breadth // tile):
        scatter.sent(qkv(group), s_qkv.at[group])
    result.wait()


def behind_call(depth, seq, feat, vec, rpe, gvec, g_sum, weights, kept, tokens, lengths):
    rows, breadth = tokens.shape
    chips = 4 * depth
    devices = 2 * chips
    w_qkv, w_out, w_up, w_down = weights
    group = 3 * 256
    groups = w_qkv.shape[0]
    table = rpe.shape[0]
    blocks = [(w.shape[0] // devices, w.shape[1]) for w in (w_out, w_up, w_down)]
    lead = (depth, 4)
    given = [lead + (2 * block[0], block[1]) for block in blocks]
    qkv_block = (w_qkv.shape[1] // devices, group)

    def buffers(block, kind, front=()):
        if kind == LOW:
            part, leaving = (2 * block[0], block[1] // 2), (block[0], block[1] // 2)
        else:
            part, leaving = block, (8, 128)
        numbers = [lead, (2, depth), (depth,), (depth - 1,)]
        return [pltpu.VMEM(front + number + part, kind) for number in numbers] + [pltpu.VMEM(front + leaving, F32)]

    slots = depth - 1 + 1 + 2 + 2
    scratch = [pltpu.VMEM((groups,) + lead + (2 * qkv_block[0], group), LOW)]
    scratch += [pltpu.VMEM(dims, LOW) for dims in given]
    scratch += [pltpu.VMEM(lead + (2, PIECE, 128), F32)]
    for block in blocks:
        scratch += buffers(block, LOW)
    scratch += buffers(qkv_block, LOW, (groups,)) + buffers((PIECE, 128), F32)
    scratch += [
        pltpu.VMEM((rows, breadth), F32), pltpu.VMEM((rows, breadth), F32), pltpu.VMEM((rows, breadth), LOW),
        pltpu.VMEM(vec.shape, F32), pltpu.VMEM((table, 128), F32), pltpu.VMEM((groups, rows, group), LOW),
        pltpu.SemaphoreType.DMA((7, slots)), pltpu.SemaphoreType.DMA((7, slots)), pltpu.SemaphoreType.DMA((32,)),
    ]
    return pl.pallas_call(
        functools.partial(behind_kernel, depth, lengths),
        out_shape=(
            shape((rows, breadth), F32), shape((groups,) + qkv_block, F32),
        ) + tuple(shape(block, F32) for block in blocks) + (shape((PIECE, 128), F32),),
        in_specs=[SCALARS] + vmem(5) + [ANYWHERE] * (4 + len(kept) + 1),
        out_specs=(ANYWHERE,) + tuple(vmem(5)),
        scratch_shapes=scratch,
        compiler_params=pltpu.CompilerParams(
            collective_id=1, has_side_effects=True, vmem_limit_bytes=62 * MIB
        ),
        name="behind",
    )(seq, feat, vec, rpe, gvec, g_sum, *weights, *kept, tokens)


def emit_kernel(count, lengths, *refs):
    big, small, refs = refs[:count], refs[count], refs[count + 1 :]
    outs, refs = refs[:count], refs[count:]
    pieces, held, sems = refs[: len(lengths) + 1], refs[len(lengths) + 1 : -1], refs[-1]
    inward = []
    for index in range(count):
        if len(big[index].shape) == 3:
            groups, _, breadth = big[index].shape
            tile = breadth // 3
            for group in range(groups):
                for part in range(3):
                    start = part * breadth + group * tile
                    source = big[index].at[group, :, part * tile : part * tile + tile]
                    inward.append((source, held[index].at[:, start : start + tile]))
        else:
            inward.append((big[index], held[index]))
    inward = [
        pltpu.make_async_copy(source, target, sems.at[0, index]) for index, (source, target) in enumerate(inward)
    ]
    outward = [pltpu.make_async_copy(held[index], outs[index], sems.at[1, index]) for index in range(count)]
    for copy in inward:
        copy.start()
    for row, length in enumerate(lengths):
        pieces[row][...] = small[row : row + 1, 0:length]
    table = pieces[-1]
    for part in range(table.shape[1] // 128):
        row = len(lengths) + part
        table[:, 128 * part : 128 * part + 128] = small[row : row + 1, :]
    for copy in inward:
        copy.wait()
    for copy in outward:
        copy.start()
    for copy in outward:
        copy.wait()


def emit_call(arrays, small, lengths, table):
    shapes = [
        (array.shape[1], array.shape[0] * array.shape[2]) if len(array.shape) == 3 else array.shape for array in arrays
    ]
    result = pl.pallas_call(
        functools.partial(emit_kernel, len(arrays), lengths),
        out_shape=tuple(shape(dims, array.dtype) for dims, array in zip(shapes, arrays))
        + tuple(shape((1, length), F32) for length in lengths + (table,)),
        in_specs=[ANYWHERE] * len(arrays) + vmem(1),
        out_specs=(ANYWHERE,) * len(arrays) + tuple(vmem(len(lengths) + 1)),
        scratch_shapes=[pltpu.VMEM(dims, array.dtype) for dims, array in zip(shapes, arrays)]
        + [pltpu.SemaphoreType.DMA((2, len(arrays) + 8))],
        compiler_params=pltpu.CompilerParams(vmem_limit_bytes=60 * MIB),
        name="emit",
    )(*arrays, small)
    return result[: len(arrays)], [piece.reshape(-1) for piece in result[len(arrays) :]]


def plain_gather(value):
    return lax.all_gather(value.astype(LOW), "dp", axis=0, tiled=True)


def plain_scatter(value):
    return lax.psum_scatter(value.astype(F32), "dp", scatter_dimension=0, tiled=True)


def body(
    depth, tokens, cotangent, seq_lengths, random_feat, w_qkv, b_qkv, w_out, b_out, ln1_gain, ln1_bias,
    w_up, b_up, w_down, b_down, ln2_gain, ln2_bias, rpe_table,
):
    vectors = (b_qkv, b_up, b_out, ln1_gain, ln1_bias, b_down, ln2_gain, ln2_bias)
    matrices = (w_qkv, w_out, w_up, w_down)
    lengths = tuple(piece.shape[0] for piece in vectors)
    if depth:
        pieces = [piece.reshape(1, -1) for piece in vectors + (rpe_table,)]
        result = ahead_call(depth, seq_lengths, tokens, cotangent, random_feat, matrices, pieces)
        out, gvec, vec, rpe = result[:4]
        g_sum, weights, kept = result[4], result[5:9], result[9:]
        g_tokens, s_qkv, s_out, s_up, s_down, small = behind_call(
            depth, seq_lengths, random_feat, vec, rpe, gvec, g_sum, weights, kept, tokens, lengths
        )
        arrays, pieces = emit_call(
            (out, g_tokens, s_qkv, s_out, s_up, s_down), small, lengths, rpe_table.shape[0]
        )
        out, g_tokens, s_qkv, s_out, s_up, s_down = arrays
    else:
        full_vectors = [plain_gather(piece).astype(F32) for piece in vectors]
        longest = max(piece.shape[0] for piece in full_vectors)
        vec = jnp.stack([jnp.pad(piece, (0, longest - piece.shape[0])) for piece in full_vectors])
        rpe = plain_gather(rpe_table).astype(F32).reshape(-1, 128)
        full_qkv, full_out, full_up, full_down = [plain_gather(piece) for piece in matrices]
        scaled, phi, low, den, ctx, ctx_low = forward_call(seq_lengths, tokens, random_feat, full_qkv, vec, rpe)
        out, g_hidden, g_ctx, d_out, d_up, d_down, gvec_one = middle_call(
            seq_lengths, tokens, cotangent, ctx_low, vec, full_out, full_up, full_down
        )
        g_tokens, d_qkv, gvec_two, grpe = backward_call(
            seq_lengths, tokens, random_feat, full_qkv, rpe, scaled, phi, low, den, ctx, g_ctx, g_hidden, vec
        )
        gvec = gvec_one + gvec_two
        s_qkv, s_out, s_up, s_down = [plain_scatter(grad) for grad in (d_qkv, d_out, d_up, d_down)]
        devices = lax.axis_size("dp")
        pieces = [plain_scatter(gvec[row, : length * devices]) for row, length in enumerate(lengths)]
        pieces.append(plain_scatter(grpe.reshape(-1)))
    p_qkv, p_up, p_out, p_gain_one, p_bias_one, p_down, p_gain_two, p_bias_two, p_rpe = pieces
    return (
        out, g_tokens, s_qkv, p_qkv, s_out, p_out, p_gain_one, p_bias_one, s_up, p_up, s_down, p_down,
        p_gain_two, p_bias_two, p_rpe,
    )


def solution(mesh):
    wide, flat = P("dp", None), P("dp")
    devices = mesh.shape["dp"]
    depth = devices // 8 if devices == 32 else 0
    in_specs = (
        wide, wide, wide, P(), wide, flat, wide, flat, flat, flat, wide, flat, wide, flat, flat, flat, flat,
    )
    out_specs = (
        wide, wide, wide, flat, wide, flat, flat, flat, wide, flat, wide, flat, flat, flat, flat,
    )
    return jax.shard_map(
        functools.partial(body, depth), mesh=mesh, in_specs=in_specs, out_specs=out_specs, check_vma=False
    )
```

```python
import functools

import jax
import jax.numpy as jnp
from jax import lax
from jax.experimental import pallas as pl
from jax.experimental.pallas import tpu as pltpu
from jax.sharding import PartitionSpec as P

EPSILON = 1e-05
F32 = jnp.float32
LOW = jnp.bfloat16
MESH = pl.DeviceIdType.MESH
MIB = 2**20


def mm(first_op, second_op, first_dim=1, second_dim=0):
    return lax.dot_general(
        first_op,
        second_op,
        (((first_dim,), (second_dim,)), ((), ())),
        preferred_element_type=F32,
    )


def mm2(value, weight, weight_dim=0):
    high = value.astype(LOW)
    rest = (value - high.astype(F32)).astype(LOW)
    return mm(high, weight, 1, weight_dim) + mm(rest, weight, 1, weight_dim)


def iota(shape, dim):
    return lax.broadcasted_iota(jnp.int32, shape, dim)


def cols(index, width):
    return pl.ds(pl.multiple_of(index * width, width), width)


def build_tables(seq_ref, feat_ref, mask_ref, block_ref, ones_ref):
    rows = mask_ref.shape[0]
    first_end = seq_ref[0, 0]
    second_end = first_end + seq_ref[0, 1]

    def segment(place):
        return (place >= first_end).astype(jnp.int32) + (place >= second_end).astype(jnp.int32)

    across = segment(iota((128, rows), 1))
    for start in range(0, rows, 128):
        down = segment(iota((128, rows), 0) + start)
        mask_ref[start : start + 128, :] = jnp.where(down == across, 1.0, 0.0)
    head_size = feat_ref.shape[1]
    breadth = ones_ref.shape[0]
    group = breadth // head_size
    bits = head_size.bit_length() - 1
    owner_row = lax.shift_right_logical(iota((breadth, breadth), 0), bits)
    owner_col = lax.shift_right_logical(iota((breadth, breadth), 1), bits)
    same = owner_row == owner_col
    ones_ref[...] = jnp.where(same, 1.0, 0.0).astype(LOW)
    for index in range(feat_ref.shape[0] // group):
        rows_of = []
        for inner in range(group):
            piece = feat_ref[index * group + inner].astype(F32)
            rows_of.append(jnp.concatenate([piece] * group, axis=1))
        full = jnp.concatenate(rows_of, axis=0)
        block_ref[index] = jnp.where(same, full, 0.0).astype(LOW)


def project(tokens_ref, w_ref, vec_ref, scaled_ref, phi_ref, low_ref, block_ref, ones_ref):
    breadth = tokens_ref.shape[1]
    tile = ones_ref.shape[0]
    per_part = breadth // tile
    scale = 64 ** (-0.25)

    def features(step, carry):
        where = cols(step, tile)
        acc = mm(tokens_ref[...], w_ref[:, where]) + vec_ref[0:1, where]
        scaled = acc * scale
        scaled_ref[:, where] = scaled
        block = block_ref[lax.rem(step, per_part)]
        mapped = mm2(scaled, block)
        squared = mm2(scaled * scaled, ones_ref[...])
        phi = jnp.exp(mapped - 0.5 * squared) * 0.125
        phi_ref[:, where] = phi
        low_ref[:, where] = phi.astype(LOW)
        return carry

    lax.fori_loop(0, 2 * per_part, features, 0)

    def plain(step, carry):
        where = cols(step + 2 * per_part, tile)
        acc = mm(tokens_ref[...], w_ref[:, where]) + vec_ref[0:1, where]
        low_ref[:, where] = acc.astype(LOW)
        return carry

    lax.fori_loop(0, per_part, plain, 0)


def coefficients(rpe_ref, head, coef_ref):
    flip = (iota((128, 128), 0) + iota((128, 128), 1) == 127).astype(F32).astype(LOW)
    raw = rpe_ref[pl.ds(pl.multiple_of(head * 8, 8), 8), :].astype(LOW)
    table = jnp.exp(mm(raw, flip))
    wide = jnp.concatenate(
        [jnp.broadcast_to(table[7 - k : 8 - k, :], (128, 128)) for k in range(8)], axis=1
    )
    coef_ref[...] = pltpu.roll(wide, 1024 - 127, axis=1, stride=1, stride_axis=0)


def attend(low_ref, rpe_ref, mask_ref, den_ref, ctx_ref, ctx_low_ref, coef_ref, key_ref):
    rows, breadth = ctx_ref.shape

    def pair_step(pair, carry):
        q_at = cols(pair, 128)
        k_at = pl.ds(pl.multiple_of(pair * 128 + breadth, 128), 128)
        v_at = pl.ds(pl.multiple_of(pair * 128 + 2 * breadth, 128), 128)
        lane = iota((128, 128), 1)
        for side in range(2):
            coefficients(rpe_ref, pair * 2 + side, coef_ref)
            mine = lane >= 64 if side else lane < 64
            keep_half(low_ref, k_at, key_ref, side)
            for block in range(rows // 128):
                at = slice(block * 128, block * 128 + 128)
                kernel = mm(low_ref[at, q_at], key_ref[...], 1, 1)
                lead = 128 * (rows // 128 - 1 - block)
                scores = kernel * (coef_ref[:, lead : lead + rows] * mask_ref[at, :])
                total = jnp.sum(scores, axis=1, keepdims=True)
                context = mm(scores.astype(LOW), low_ref[:, v_at]) * (1.0 / total)
                total = jnp.broadcast_to(total, (128, 128))
                if side == 0:
                    den_ref[at, q_at] = total
                    ctx_ref[at, q_at] = context
                else:
                    den_ref[at, q_at] = jnp.where(mine, total, den_ref[at, q_at])
                    context = jnp.where(mine, context, ctx_ref[at, q_at])
                    ctx_ref[at, q_at] = context
                    ctx_low_ref[at, q_at] = context.astype(LOW)
        return carry

    lax.fori_loop(0, breadth // 128, pair_step, 0)


def keep_half(low_ref, where, out_ref, side):
    rows = low_ref.shape[0]
    lane = iota((rows, 128), 1)
    mine = lane >= 64 if side else lane < 64
    out_ref[...] = jnp.where(mine, low_ref[:, where].astype(F32), 0.0).astype(LOW)


def forward_kernel(
    seq_ref, tokens_ref, feat_ref, w_ref, vec_ref, rpe_ref,
    scaled_ref, phi_ref, low_ref, den_ref, ctx_ref, ctx_low_ref,
    mask_ref, block_ref, ones_ref, coef_ref, key_ref,
):
    build_tables(seq_ref, feat_ref, mask_ref, block_ref, ones_ref)
    project(tokens_ref, w_ref, vec_ref, scaled_ref, phi_ref, low_ref, block_ref, ones_ref)
    attend(low_ref, rpe_ref, mask_ref, den_ref, ctx_ref, ctx_low_ref, coef_ref, key_ref)


def norm(value):
    centred = value - jnp.mean(value, axis=-1, keepdims=True)
    inverse = lax.rsqrt(jnp.mean(centred * centred, axis=-1, keepdims=True) + EPSILON)
    return centred * inverse, inverse


def norm_back(grad, xhat, inverse, gain):
    scaled = grad * gain
    mean = jnp.mean(scaled, axis=-1, keepdims=True)
    along = jnp.mean(scaled * xhat, axis=-1, keepdims=True)
    return inverse * (scaled - mean - xhat * along)


def add_to(ref, row, value):
    ref[row : row + 1, 0 : value.shape[1]] += value


def column_sum(value):
    return jnp.sum(value, axis=0, keepdims=True)


def middle_kernel(
    seq_ref, tokens_ref, cot_ref, ctx_low_ref, vec_ref, w_out_ref, w_up_ref, w_down_ref,
    out_ref, g_hidden_ref, g_ctx_ref, d_out_ref, d_up_ref, d_down_ref, gvec_ref,
    wide_ref, normed_ref, normed_low_ref, xhat_ref, inverse_ref, act_ref, slope_ref, g_sum_ref,
    g_low_ref, g_up_ref, flip_ref,
):
    rows, breadth = tokens_ref.shape
    hidden = w_up_ref.shape[1]
    height, tile = 128, 256
    blocks, tiles = rows // height, breadth // tile
    valid_rows = seq_ref[0, 0] + seq_ref[0, 1]
    gvec_ref[...] = jnp.zeros_like(gvec_ref)
    gain_one, bias_one = vec_ref[3:4, :breadth], vec_ref[4:5, :breadth]
    gain_two, bias_two = vec_ref[6:7, :breadth], vec_ref[7:8, :breadth]

    def rows_at(step):
        return pl.ds(pl.multiple_of(step * height, height), height)

    def loop(count, step):
        def run(index, carry):
            step(index)
            return carry

        lax.fori_loop(0, count, run, 0)

    def attended_step(step):
        where = cols(step, tile)
        wide_ref[:, where] = mm(ctx_low_ref[...], w_out_ref[:, where]) + vec_ref[2:3, where]

    loop(tiles, attended_step)

    def first_norm(step):
        at = rows_at(step)
        xhat, inverse = norm(tokens_ref[at, :].astype(F32) + wide_ref[at, :])
        xhat_ref[at, :] = xhat
        inverse_ref[at, :] = jnp.broadcast_to(inverse, (height, 128))
        normed = xhat * gain_one + bias_one
        normed_ref[at, :] = normed
        normed_low_ref[at, :] = normed.astype(LOW)

    loop(blocks, first_norm)

    def upward_step(step):
        where = cols(step, tile)
        upward = mm(normed_low_ref[...], w_up_ref[:, where]) + vec_ref[1:2, where]
        phi = 0.5 + 0.5 * lax.erf(upward * 0.5**0.5)
        density = jnp.exp(-0.5 * upward * upward) * 0.3989422804014327
        act_ref[:, where] = (upward * phi).astype(LOW)
        slope_ref[:, where] = phi + upward * density

    loop(hidden // tile, upward_step)

    def downward_step(step):
        where = cols(step, tile)
        wide_ref[:, where] = mm(act_ref[...], w_down_ref[:, where]) + vec_ref[5:6, where]

    loop(tiles, downward_step)

    def second_norm(step):
        at = rows_at(step)
        xhat, inverse = norm(normed_ref[at, :] + wide_ref[at, :])
        out_ref[at, :] = (xhat * gain_two + bias_two).astype(LOW)
        place = iota((height, breadth), 0) + step * height
        grad = jnp.where(place < valid_rows, cot_ref[at, :].astype(F32), 0.0)
        add_to(gvec_ref, 6, column_sum(grad * xhat))
        add_to(gvec_ref, 7, column_sum(grad))
        g_sum = norm_back(grad, xhat, inverse, gain_two)
        add_to(gvec_ref, 5, column_sum(g_sum))
        g_sum_ref[at, :] = g_sum
        g_low_ref[at, :] = g_sum.astype(LOW)

    loop(blocks, second_norm)
    flip_ref[...] = jnp.transpose(normed_low_ref[...])

    def down_step(step):
        where = cols(step, tile)
        g_upward = mm(g_low_ref[...], w_down_ref[where, :], 1, 1) * slope_ref[:, where]
        gvec_ref[1:2, where] = column_sum(g_upward)
        g_upward = g_upward.astype(LOW)
        g_up_ref[:, where] = g_upward
        d_down_ref[where, :] = mm(act_ref[:, where], g_low_ref[...], 0, 0).astype(LOW)
        d_up_ref[:, where] = mm(flip_ref[...], g_upward).astype(LOW)

    loop(hidden // tile, down_step)

    def up_back(step):
        where = cols(step, tile)
        wide_ref[:, where] = mm(g_up_ref[...], w_up_ref[where, :], 1, 1) + g_sum_ref[:, where]

    loop(tiles, up_back)

    def first_back(step):
        at = rows_at(step)
        g_normed = wide_ref[at, :]
        xhat = xhat_ref[at, :]
        add_to(gvec_ref, 3, column_sum(g_normed * xhat))
        add_to(gvec_ref, 4, column_sum(g_normed))
        g_hidden = norm_back(g_normed, xhat, inverse_ref[at, 0:1], gain_one)
        add_to(gvec_ref, 2, column_sum(g_hidden))
        g_hidden_ref[at, :] = g_hidden
        g_low_ref[at, :] = g_hidden.astype(LOW)

    loop(blocks, first_back)

    def out_back(step):
        where = cols(step, tile)
        g_ctx_ref[:, where] = mm(g_low_ref[...], w_out_ref[where, :], 1, 1)
        d_out_ref[where, :] = mm(ctx_low_ref[:, where], g_low_ref[...], 0, 0).astype(LOW)

    loop(tiles, out_back)


def plain_diagonals(diag_ref, out_ref, head):
    value = diag_ref[...]
    height = value.shape[0]
    while height > 1:
        height //= 2
        value = value[height:] + pltpu.roll(value[:height], height, axis=1)
    for k in range(8):
        out_ref[pl.ds(head * 8 + 7 - k, 1), :] = value[:, 128 * k : 128 * k + 128]


def attend_back(
    low_ref, rpe_ref, mask_ref, den_ref, ctx_ref, g_ctx_ref,
    g_feat_ref, g_low_ref, gvec_ref, grpe_ref,
    coef_ref, scores_ref, gk_ref, diag_ref, query_ref, key_ref, value_ref, num_ref,
):
    rows, breadth = ctx_ref.shape

    def pair_step(pair, carry):
        q_at = cols(pair, 128)
        k_at = pl.ds(pl.multiple_of(pair * 128 + breadth, 128), 128)
        v_at = pl.ds(pl.multiple_of(pair * 128 + 2 * breadth, 128), 128)
        lane = iota((128, 128), 1)
        ones = jnp.ones((128, 128), LOW)
        for side in range(2):
            coefficients(rpe_ref, pair * 2 + side, coef_ref)
            mine = lane >= 64 if side else lane < 64
            other = 0 if side else 64
            keep_half(low_ref, q_at, query_ref, side)
            keep_half(low_ref, k_at, key_ref, side)
            keep_half(low_ref, v_at, value_ref, side)
            diag_ref[...] = jnp.zeros_like(diag_ref)
            is_high, is_rest = lane == other, lane == other + 1
            extra = jnp.where(jnp.logical_or(is_high, is_rest), 1.0, 0.0)
            for block in range(rows // 128):
                at = slice(block * 128, block * 128 + 128)
                value_ref[at, :] = (value_ref[at, :].astype(F32) + extra).astype(LOW)
            for block in range(rows // 128):
                at = slice(block * 128, block * 128 + 128)
                kernel = mm(low_ref[at, q_at], key_ref[...], 1, 1)
                g_num = jnp.where(mine, g_ctx_ref[at, q_at] * (1.0 / den_ref[at, q_at]), 0.0)
                g_den = -mm2(g_num * ctx_ref[at, q_at], ones)
                num_ref[at, :] = g_num.astype(LOW)
                high = g_den.astype(LOW).astype(F32)
                extended = jnp.where(is_high, high, jnp.where(is_rest, g_den - high, g_num))
                g_scores = mm(extended.astype(LOW), value_ref[...], 1, 1)
                lead = 128 * (rows // 128 - 1 - block)
                weight = coef_ref[:, lead : lead + rows] * mask_ref[at, :]
                scores = kernel * weight
                g_kernel = (g_scores * weight).astype(LOW)
                diag_ref[:, lead : lead + rows] += g_scores * scores
                scores_ref[at, :] = scores.astype(LOW)
                gk_ref[at, :] = g_kernel
                g_query = mm(g_kernel, key_ref[...])
                if side:
                    g_query = g_query + g_feat_ref[at, q_at]
                g_feat_ref[at, q_at] = g_query
            g_key = mm(gk_ref[...], query_ref[...], 0, 0)
            g_value = mm(scores_ref[...], num_ref[...], 0, 0)
            if side:
                g_key = g_key + g_feat_ref[:, k_at]
                g_value = g_value + g_feat_ref[:, v_at]
            g_feat_ref[:, k_at] = g_key
            g_feat_ref[:, v_at] = g_value
            plain_diagonals(diag_ref, grpe_ref, pair * 2 + side)
        g_value = g_feat_ref[:, v_at]
        gvec_ref[0:1, v_at] = column_sum(g_value)
        g_low_ref[:, v_at] = g_value.astype(LOW)
        return carry

    lax.fori_loop(0, breadth // 128, pair_step, 0)
    flip = (jnp.where(iota((128, 128), 0) + iota((128, 128), 1) == 127, 1.0, 0.0)).astype(LOW)
    grpe_ref[...] = mm2(grpe_ref[...], flip)


def project_back(
    tokens_ref, w_ref, g_hidden_ref, phi_ref, scaled_ref, block_ref, ones_ref,
    g_feat_ref, g_low_ref, gvec_ref, g_tokens_ref, d_qkv_ref, flip_ref,
):
    breadth = tokens_ref.shape[1]
    tile = ones_ref.shape[0]
    per_part = breadth // tile
    scale = 64 ** (-0.25)

    def features(step, carry):
        where = cols(step, tile)
        upward = g_feat_ref[:, where] * phi_ref[:, where]
        total = mm2(upward, ones_ref[...])
        grad = mm2(upward, block_ref[lax.rem(step, per_part)], 1) - scaled_ref[:, where] * total
        grad = grad * scale
        gvec_ref[0:1, where] = column_sum(grad)
        g_low_ref[:, where] = grad.astype(LOW)
        return carry

    lax.fori_loop(0, 2 * per_part, features, 0)
    flip_ref[...] = jnp.transpose(tokens_ref[...])

    def weights(step, carry):
        where = cols(step, tile)
        d_qkv_ref[:, where] = mm(flip_ref[...], g_low_ref[:, where]).astype(LOW)
        return carry

    lax.fori_loop(0, 3 * per_part, weights, 0)

    def inputs(step, carry):
        where = cols(step, tile)
        g_tokens_ref[:, where] = mm(g_low_ref[...], w_ref[where, :], 1, 1) + g_hidden_ref[:, where]
        return carry

    lax.fori_loop(0, per_part, inputs, 0)


def backward_kernel(
    seq_ref, tokens_ref, feat_ref, w_ref, rpe_ref, scaled_ref, phi_ref, low_ref, den_ref, ctx_ref,
    g_ctx_ref, g_hidden_ref,
    g_tokens_ref, d_qkv_ref, gvec_ref, grpe_ref,
    mask_ref, block_ref, ones_ref, coef_ref, g_feat_ref, g_low_ref, scores_ref, gk_ref, diag_ref,
    query_ref, key_ref, value_ref, num_ref, flip_ref,
):
    build_tables(seq_ref, feat_ref, mask_ref, block_ref, ones_ref)
    gvec_ref[...] = jnp.zeros_like(gvec_ref)
    attend_back(
        low_ref, rpe_ref, mask_ref, den_ref, ctx_ref, g_ctx_ref, g_feat_ref, g_low_ref, gvec_ref, grpe_ref,
        coef_ref, scores_ref, gk_ref, diag_ref, query_ref, key_ref, value_ref, num_ref,
    )
    project_back(
        tokens_ref, w_ref, g_hidden_ref, phi_ref, scaled_ref, block_ref, ones_ref,
        g_feat_ref, g_low_ref, gvec_ref, g_tokens_ref, d_qkv_ref, flip_ref,
    )


def vmem(count):
    return [pl.BlockSpec(memory_space=pltpu.VMEM)] * count


def shape(dims, kind):
    return jax.ShapeDtypeStruct(dims, kind)


SCALARS = pl.BlockSpec(memory_space=pltpu.SMEM)


def forward_call(seq, tokens, feat, w_qkv, vec, rpe):
    rows, breadth = tokens.shape
    span = 2 * rows
    return pl.pallas_call(
        forward_kernel,
        out_shape=(
            shape((rows, 2 * breadth), F32), shape((rows, 2 * breadth), F32), shape((rows, 3 * breadth), LOW),
            shape((rows, breadth), F32), shape((rows, breadth), F32), shape((rows, breadth), LOW),
        ),
        in_specs=[SCALARS] + vmem(5),
        out_specs=tuple(vmem(6)),
        scratch_shapes=[
            pltpu.VMEM((rows, rows), F32), pltpu.VMEM((breadth // 256, 256, 256), LOW),
            pltpu.VMEM((256, 256), LOW), pltpu.VMEM((128, span), F32), pltpu.VMEM((rows, 128), LOW),
        ],
        compiler_params=pltpu.CompilerParams(vmem_limit_bytes=60 * MIB),
        name="attend",
    )(seq, tokens, feat, w_qkv, vec, rpe)


def middle_call(seq, tokens, cotangent, ctx_low, vec, w_out, w_up, w_down):
    rows, breadth = tokens.shape
    hidden = w_up.shape[1]
    return pl.pallas_call(
        middle_kernel,
        out_shape=(
            shape((rows, breadth), LOW), shape((rows, breadth), F32), shape((rows, breadth), F32),
            shape(w_out.shape, LOW), shape(w_up.shape, LOW), shape(w_down.shape, LOW), shape(vec.shape, F32),
        ),
        in_specs=[SCALARS] + vmem(7),
        out_specs=tuple(vmem(7)),
        scratch_shapes=[
            pltpu.VMEM((rows, breadth), F32), pltpu.VMEM((rows, breadth), F32), pltpu.VMEM((rows, breadth), LOW),
            pltpu.VMEM((rows, breadth), F32), pltpu.VMEM((rows, 128), F32), pltpu.VMEM((rows, hidden), LOW),
            pltpu.VMEM((rows, hidden), F32), pltpu.VMEM((rows, breadth), F32), pltpu.VMEM((rows, breadth), LOW),
            pltpu.VMEM((rows, hidden), LOW), pltpu.VMEM((breadth, rows), LOW),
        ],
        compiler_params=pltpu.CompilerParams(vmem_limit_bytes=60 * MIB),
        name="feed_forward",
    )(seq, tokens, cotangent, ctx_low, vec, w_out, w_up, w_down)


def backward_call(seq, tokens, feat, w_qkv, rpe, scaled, phi, low, den, ctx, g_ctx, g_hidden, vec):
    rows, breadth = tokens.shape
    span = 2 * rows
    return pl.pallas_call(
        backward_kernel,
        out_shape=(
            shape((rows, breadth), F32), shape(w_qkv.shape, LOW), shape(vec.shape, F32), shape(rpe.shape, F32),
        ),
        in_specs=[SCALARS] + vmem(11),
        out_specs=tuple(vmem(4)),
        scratch_shapes=[
            pltpu.VMEM((rows, rows), F32), pltpu.VMEM((breadth // 256, 256, 256), LOW),
            pltpu.VMEM((256, 256), LOW), pltpu.VMEM((128, span), F32), pltpu.VMEM((rows, 3 * breadth), F32),
            pltpu.VMEM((rows, 3 * breadth), LOW), pltpu.VMEM((rows, rows), LOW), pltpu.VMEM((rows, rows), LOW),
            pltpu.VMEM((128, span), F32), pltpu.VMEM((rows, 128), LOW), pltpu.VMEM((rows, 128), LOW),
            pltpu.VMEM((rows, 128), LOW), pltpu.VMEM((rows, 128), LOW), pltpu.VMEM((breadth, rows), LOW),
        ],
        compiler_params=pltpu.CompilerParams(vmem_limit_bytes=60 * MIB),
        name="attend_back",
    )(seq, tokens, feat, w_qkv, rpe, scaled, phi, low, den, ctx, g_ctx, g_hidden)


PIECE = 16
BLOCK_ROWS = 256


def place():
    me = lax.axis_index("dp")
    core = lax.rem(me, 2)
    x = lax.rem(me // 2, 2)
    y = lax.rem(me // 4, 2)
    z = me // 8
    first = x * (1 - core) + y * core
    second = y * (1 - core) + x * core
    return core, z, first, second


class Plane:
    def __init__(self, depth):
        self.depth = depth
        self.core, self.z, self.first, self.second = place()
        self.chip = self.at(self.z, self.first, self.second)
        self.sibling = self.chip * 2 + 1 - self.core
        self.over_first = self.device(self.z, 1 - self.first, self.second)
        self.over_second = self.device(self.z, self.first, 1 - self.second)

    def at(self, z, first, second):
        return 4 * z + first * (1 + self.core) + second * (2 - self.core)

    def device(self, z, first, second):
        return 2 * self.at(z, first, second) + self.core

    def spot(self, first, second):
        return first * (1 + self.core) + second * (2 - self.core)

    def ahead(self, distance):
        return lax.rem(self.z + distance, self.depth)

    def behind(self, distance):
        return lax.rem(self.z + self.depth - distance, self.depth)

    def greet(self):
        barrier = pltpu.get_barrier_semaphore()
        others = [self.sibling, self.over_first, self.over_second]
        others += [self.device(self.ahead(d), self.first, self.second) for d in range(1, self.depth)]
        for other in others:
            pl.semaphore_signal(barrier, inc=1, device_id=(other,), device_id_type=MESH)
        pl.semaphore_wait(barrier, len(others))


def remote(source, target, sems, item, slot, device):
    return pltpu.make_async_remote_copy(
        src_ref=source, dst_ref=target, send_sem=sems[0].at[item, slot], recv_sem=sems[1].at[item, slot],
        device_id=(device,), device_id_type=MESH,
    )


def each(count, step):
    def run(index, carry):
        step(index)
        return carry

    lax.fori_loop(0, count, run, 0)


def span(start, stop, step):
    def run(index, carry):
        step(index)
        return carry

    lax.fori_loop(start, stop, run, 0)


def half(ref, zs, spot, core):
    if len(ref.shape) == 5:
        return ref.at[zs, spot, core]
    breadth = ref.shape[3] // 2
    return ref.at[zs, spot, :, pl.ds(pl.multiple_of(core * breadth, 128), breadth)]


ALL = slice(None)


class Gather:
    def __init__(self, plane, full, sems):
        self.plane, self.full, self.sems = plane, full, sems
        self.here = plane.spot(plane.first, plane.second)
        self.across = plane.spot(1 - plane.first, plane.second)
        self.first_slot = plane.depth - 1
        self.second_slot = self.first_slot + 1
        self.core_slot = self.second_slot + 2

    def copy(self, item, zs, spot, slot, device, core=None):
        part = half(self.full[item], zs, spot, self.plane.core if core is None else core)
        return remote(part, part, self.sems, item, slot, device)

    def to_depth(self, item, distance):
        plane = self.plane
        target = plane.device(plane.ahead(distance), plane.first, plane.second)
        return self.copy(item, plane.z, self.here, distance - 1, target)

    def to_first(self, item):
        return self.copy(item, ALL, self.here, self.first_slot, self.plane.over_first)

    def to_second(self, item, first):
        spot = self.plane.spot(first, self.plane.second)
        return self.copy(item, ALL, spot, self.second_slot + first, self.plane.over_second)

    def to_core(self, item, spot):
        return self.copy(item, ALL, spot, self.core_slot + spot, self.plane.sibling)

    def begin(self, item):
        for distance in range(1, self.plane.depth):
            self.to_depth(item, distance).start()

    def over_depth(self, item):
        plane = self.plane
        for distance in range(1, plane.depth):
            self.copy(item, plane.behind(distance), self.here, distance - 1, plane.sibling).wait_recv()
        self.to_first(item).start()
        self.to_second(item, plane.first).start()
        self.to_core(item, self.here).start()

    def over_first(self, item):
        plane = self.plane
        self.copy(item, ALL, self.across, self.first_slot, plane.over_first).wait_recv()
        self.to_second(item, 1 - plane.first).start()
        self.to_core(item, self.across).start()

    def over_second(self, item):
        plane = self.plane
        for first in (plane.first, 1 - plane.first):
            spot = plane.spot(first, 1 - plane.second)
            self.copy(item, ALL, spot, self.second_slot + first, plane.over_second).wait_recv()
            self.to_core(item, spot).start()

    def over_core(self, item):
        plane = self.plane
        for spot in range(4):
            self.copy(item, ALL, spot, self.core_slot + spot, plane.sibling, 1 - plane.core).wait_recv()

    def sent(self, item):
        plane = self.plane
        for distance in range(1, plane.depth):
            self.to_depth(item, distance).wait_send()
        self.to_first(item).wait_send()
        for first in range(2):
            self.to_second(item, first).wait_send()
        for spot in range(4):
            self.to_core(item, spot).wait_send()


def one_hot(length, breadth):
    factor = (1 << 20) // length + 1
    col = iota((128, breadth), 1)
    owner = lax.shift_right_logical(col * factor, 20)
    return jnp.where(iota((128, breadth), 0) == col - owner * length, 1.0, 0.0).astype(LOW)


def owned(devices, length, breadth):
    factor = (1 << 20) // length + 1
    col = iota((devices, breadth), 1)
    return lax.shift_right_logical(col * factor, 20) == iota((devices, breadth), 0)


def pack_small(piece_refs, small_ref):
    small_ref[...] = jnp.zeros_like(small_ref)
    for row, piece in enumerate(piece_refs[:-1]):
        small_ref[row : row + 1, 0 : piece.shape[1]] = piece[...].astype(LOW).astype(F32)
    table = piece_refs[-1]
    for part in range(table.shape[0] // 128):
        row = len(piece_refs) - 1 + part
        value = table[128 * part : 128 * part + 128].reshape(1, 128)
        small_ref[row : row + 1, :] = value.astype(LOW).astype(F32)


def unpack_small(all_ref, lengths, table_rows, vec_ref, rpe_ref):
    devices = all_ref.shape[0] // PIECE
    vec_ref[...] = jnp.zeros_like(vec_ref)
    for row, length in enumerate(lengths):
        breadth = length * devices
        picked = all_ref[pl.ds(row, devices, stride=PIECE), :].astype(LOW)
        spread = jnp.where(owned(devices, length, breadth), mm(picked, one_hot(length, breadth)), 0.0)
        vec_ref[row : row + 1, 0:breadth] = column_sum(spread)
    for part in range(table_rows):
        rpe_ref[pl.ds(part, devices, stride=table_rows), :] = all_ref[
            pl.ds(len(lengths) + part, devices, stride=PIECE), :
        ]


ANYWHERE = pl.BlockSpec(memory_space=pl.ANY)


class Saver:
    def __init__(self, sources, targets, sems):
        self.copies = [
            pltpu.make_async_copy(source, target, sems.at[index])
            for index, (source, target) in enumerate(zip(sources, targets))
        ]

    def start(self, *indices):
        for index in indices:
            self.copies[index].start()

    def finish(self):
        for copy in self.copies:
            copy.wait()


def norm_forward(tokens_ref, wide_ref, vec_ref, xhat_ref, inverse_ref, normed_ref, normed_low_ref):
    rows, breadth = tokens_ref.shape
    gain, bias = vec_ref[3:4, :breadth], vec_ref[4:5, :breadth]

    def step(index):
        at = pl.ds(pl.multiple_of(index * 128, 128), 128)
        xhat, inverse = norm(tokens_ref[at, :].astype(F32) + wide_ref[at, :])
        xhat_ref[at, :] = xhat
        inverse_ref[at, :] = jnp.broadcast_to(inverse, (128, 128))
        normed = xhat * gain + bias
        normed_ref[at, :] = normed
        normed_low_ref[at, :] = normed.astype(LOW)

    each(rows // 128, step)


def norm_result(seq_ref, normed_ref, wide_ref, vec_ref, cot_ref, out_ref, g_sum_ref, gvec_ref):
    rows, breadth = normed_ref.shape
    gain, bias = vec_ref[6:7, :breadth], vec_ref[7:8, :breadth]
    valid_rows = seq_ref[0, 0] + seq_ref[0, 1]
    gvec_ref[...] = jnp.zeros_like(gvec_ref)

    def step(index):
        at = pl.ds(pl.multiple_of(index * 128, 128), 128)
        xhat, inverse = norm(normed_ref[at, :] + wide_ref[at, :])
        out_ref[at, :] = (xhat * gain + bias).astype(LOW)
        spot = iota((128, breadth), 0) + index * 128
        grad = jnp.where(spot < valid_rows, cot_ref[at, :].astype(F32), 0.0)
        add_to(gvec_ref, 6, column_sum(grad * xhat))
        add_to(gvec_ref, 7, column_sum(grad))
        g_sum = norm_back(grad, xhat, inverse, gain)
        add_to(gvec_ref, 5, column_sum(g_sum))
        g_sum_ref[at, :] = g_sum

    each(rows // 128, step)


def attend_pair(pair, q_at, k_at, v_at, low_ref, rpe_ref, mask_ref, den_ref, ctx_ref, ctx_low_ref, coef_ref, key_ref, score_ref, serve):
    rows = mask_ref.shape[0]
    tall = BLOCK_ROWS
    lower = iota((tall, 128), 1) < 64
    here = cols(pair, 128)
    for side in range(2):
        serve(pair, side)
        coefficients(rpe_ref, pair * 2 + side, coef_ref)
        keep_half(low_ref, k_at, key_ref, side)
        for block in range(rows // tall):
            at = slice(block * tall, block * tall + tall)
            kernel = mm(low_ref[at, q_at], key_ref[...], 1, 1)
            totals = []
            for part in range(tall // 128):
                start = block * tall + part * 128
                lead = rows - 128 - start
                weight = coef_ref[:, lead : lead + rows] * mask_ref[start : start + 128, :]
                scores = kernel[part * 128 : part * 128 + 128] * weight
                totals.append(jnp.sum(scores, axis=1, keepdims=True))
                score_ref[start : start + 128, :] = scores.astype(LOW)
            total = jnp.broadcast_to(jnp.concatenate(totals, axis=0), (tall, 128))
            context = mm(score_ref[at, :], low_ref[:, v_at]) * (1.0 / total)
            if side == 0:
                den_ref[at, here] = total
                ctx_ref[at, here] = context
            else:
                den_ref[at, here] = jnp.where(lower, den_ref[at, here], total)
                context = jnp.where(lower, ctx_ref[at, here], context)
                ctx_ref[at, here] = context
                ctx_low_ref[at, here] = context.astype(LOW)


def upward_tile(normed_low_ref, w, bias, act_ref, slope_ref, where):
    upward = mm(normed_low_ref[...], w[...]) + bias
    phi = 0.5 + 0.5 * lax.erf(upward * 0.5**0.5)
    density = jnp.exp(-0.5 * upward * upward) * 0.3989422804014327
    act_ref[:, where] = (upward * phi).astype(LOW)
    slope_ref[:, where] = phi + upward * density


def build_stack(feat_ref, stack_ref):
    tile = stack_ref.shape[2]
    head_size = feat_ref.shape[1]
    group = tile // head_size
    bits = head_size.bit_length() - 1
    same = lax.shift_right_logical(iota((tile, tile), 0), bits) == lax.shift_right_logical(iota((tile, tile), 1), bits)
    half = jnp.where(same, -0.5, 0.0).astype(LOW)
    for index in range(stack_ref.shape[0]):
        rows_of = []
        for inner in range(group):
            piece = feat_ref[index * group + inner].astype(F32)
            rows_of.append(jnp.concatenate([piece] * group, axis=1))
        full = jnp.where(same, jnp.concatenate(rows_of, axis=0), 0.0).astype(LOW)
        for part, value in enumerate((full, full, half, half)):
            stack_ref[index, part * tile : part * tile + tile, :] = value


def two_parts(value):
    high = value.astype(LOW)
    return [high, (value - high.astype(F32)).astype(LOW)]


def segment_mask(seq_ref, mask_ref):
    rows = mask_ref.shape[0]
    first_end = seq_ref[0, 0]
    second_end = first_end + seq_ref[0, 1]

    def segment(place):
        return (place >= first_end).astype(jnp.int32) + (place >= second_end).astype(jnp.int32)

    across = segment(iota((128, rows), 1))
    for start in range(0, rows, 128):
        down = segment(iota((128, rows), 0) + start)
        mask_ref[start : start + 128, :] = jnp.where(down == across, 1.0, 0.0)


def ahead_kernel(depth, pieces, *refs):
    seq_ref, tokens_ref, cot_ref, feat_ref, refs = refs[0], refs[1], refs[2], refs[3], refs[4:]
    matrices, refs = refs[:4], refs[4:]
    piece_refs, refs = refs[:pieces], refs[pieces:]
    out_ref, gvec_ref, vec_ref, rpe_ref, wide_ref, refs = refs[:5] + (refs[5:],)
    weights_hbm, kept_hbm, refs = refs[:4], refs[4:15], refs[15:]
    w_qkv, w_out, w_up, w_down, refs = refs[:4] + (refs[4:],)
    kept, refs = refs[:11], refs[11:]
    peers, refs = refs[:4], refs[4:]
    small_ref, all_ref, mask_ref, stack_ref, coef_ref, key_ref, score_ref, normed_ref = refs[:8]
    send, recv, peer_send, peer_recv, save_sem = refs[8:]
    scaled_ref, phi_ref, low_ref, den_ref, ctx_ref, ctx_low_ref = kept[:6]
    normed_low_ref, xhat_ref, inverse_ref, act_ref, slope_ref = kept[6:]
    rows, breadth = tokens_ref.shape
    groups, tile = w_qkv.shape[0], stack_ref.shape[2]
    up_tile, down_tile = w_up.shape[4], w_down.shape[4]

    plane = Plane(depth)
    core = plane.core
    pack_small(piece_refs, small_ref)
    thirds = range(groups)
    full = [all_ref] + [w_qkv.at[g] for g in thirds] + [w_out]
    full += [w_up.at[g] for g in thirds] + [w_down.at[g] for g in thirds]
    gather = Gather(plane, full, (send, recv))
    all_ref[plane.z, gather.here, core] = small_ref[...]
    plane.greet()
    swaps = [
        remote(matrix, peer, (peer_send, peer_recv), 0, index, plane.sibling)
        for index, (matrix, peer) in enumerate(zip(matrices, peers))
    ]
    for swap in swaps:
        swap.start()

    def assemble(item, matrix, starts, breadth_of):
        mine, other = matrices[matrix], peers[matrix]
        offset = core * (len(starts) * breadth_of)
        for number, start in enumerate(starts):
            at = pl.ds(pl.multiple_of(start, 128), breadth_of)
            own, peer = mine[:, at], other[:, at]
            both = jnp.concatenate([jnp.where(core == 0, own, peer), jnp.where(core == 0, peer, own)], axis=0)
            to = pl.ds(pl.multiple_of(offset + number * breadth_of, 128), breadth_of)
            full[item][plane.z, gather.here, :, to] = both.astype(LOW)

    def assemble_qkv(group):
        starts = []
        for number in range(3):
            place_of = 3 * core + number
            starts.append((place_of // 2) * breadth + group * tile + lax.rem(place_of, 2) * 128)
        assemble(1 + group, 0, starts, 128)

    flat_qkv = w_qkv.reshape(groups, breadth, 3 * tile)
    flat_out = w_out.reshape(breadth, breadth)
    flat_up = w_up.reshape(groups, breadth, up_tile)
    flat_down = w_down.reshape(groups, w_down.shape[1] * w_down.shape[2] * w_down.shape[3], down_tile)
    sources = [flat_qkv.at[g] for g in thirds] + [flat_out] + [flat_up.at[g] for g in thirds]
    sources += [flat_down.at[g] for g in thirds]
    targets = [weights_hbm[0].at[g] for g in thirds] + [weights_hbm[1]]
    targets += [weights_hbm[2].at[:, g * up_tile : g * up_tile + up_tile] for g in thirds]
    targets += [weights_hbm[3].at[:, g * down_tile : g * down_tile + down_tile] for g in thirds]
    saver = Saver(sources + list(kept), targets + list(kept_hbm), save_sem)
    first_kept = len(targets)

    def keep(*indices):
        saver.start(*[first_kept + index for index in indices])

    begin, along, first, second = gather.begin, gather.over_depth, gather.over_first, gather.over_second

    def whole(item):
        gather.over_core(item)
        if item:
            saver.start(item - 1)

    plan = {
        ("head", 1): ((second, 2), (along, 5)),
        ("head", 3): ((first, 4), (begin, 8), (whole, 2), (along, 6), (begin, 7)),
        ("project", 1): ((first, 5), (second, 3)),
        ("head", 5): ((second, 4),),
        ("project", 2): (
            (along, 7), (second, 5), (whole, 3), (begin, 9), (first, 6), (along, 8), (first, 7), (whole, 4),
        ),
        ("head", 8): ((whole, 5), (second, 6), (first, 8), (begin, 10)),
        ("head", 11): ((along, 9), (second, 7)),
        ("up", 0): ((second, 8), (first, 9), (whole, 6)),
        ("up", 2): ((first, 10), (whole, 8)),
        ("down", 0): ((second, 9),),
        ("down", 1): ((whole, 9), (second, 10)),
        ("down", 2): ((whole, 10),),
    }

    def serve(kind, index):
        for (work, number), steps in plan.items():
            if work == kind:

                @pl.when(index == number)
                def _(steps=steps):
                    for step, item in steps:
                        step(item)

    begin(0)
    swaps[0].wait_recv()
    assemble_qkv(0)
    begin(1)
    assemble_qkv(1)
    assemble_qkv(2)
    for swap in swaps[1:]:
        swap.wait_recv()
    assemble(4, 1, [core * (breadth // 2)], breadth // 2)
    for group in thirds:
        assemble(5 + group, 2, [group * up_tile + core * (up_tile // 2)], up_tile // 2)
        assemble(8 + group, 3, [group * down_tile + core * (down_tile // 2)], down_tile // 2)
    along(0)
    begin(2)
    segment_mask(seq_ref, mask_ref)
    first(0)
    along(1)
    second(0)
    along(2)
    begin(3)
    whole(0)
    begin(4)
    build_stack(feat_ref, stack_ref)
    first(1)
    along(3)
    first(2)
    begin(5)
    second(1)
    lengths = [piece.shape[1] for piece in piece_refs[:-1]]
    flat_all = all_ref.reshape(8 * depth * PIECE, 128)
    unpack_small(flat_all, lengths, piece_refs[-1].shape[0] // 128, vec_ref, rpe_ref)
    along(4)
    begin(6)
    whole(1)
    first(3)
    scale = 64 ** (-0.25)

    def serve_pair(pair, side):
        for (work, number), steps in plan.items():
            if work == "head" and number % 2 == side:

                @pl.when(pair == number // 2)
                def _(steps=steps):
                    for step, item in steps:
                        step(item)

    def group_step(group):
        serve("project", group)
        wide_ref[...] = mm(tokens_ref[...], flat_qkv[group])
        for part in range(3):
            where = pl.ds(pl.multiple_of(part * breadth + group * tile, tile), tile)
            value = wide_ref[:, part * tile : part * tile + tile] + vec_ref[0:1, where]
            if part < 2:
                scaled = value * scale
                scaled_ref[:, where] = scaled
                operand = jnp.concatenate(two_parts(scaled) + two_parts(scaled * scaled), axis=1)
                value = jnp.exp(mm(operand, stack_ref[group])) * 0.125
                phi_ref[:, where] = value
            low_ref[:, where] = value.astype(LOW)

        def pair_step(inner):
            pair = 2 * group + inner
            attend_pair(
                pair, cols(pair, 128), pl.ds(pl.multiple_of(pair * 128 + breadth, 128), 128),
                pl.ds(pl.multiple_of(pair * 128 + 2 * breadth, 128), 128),
                low_ref, rpe_ref, mask_ref, den_ref, ctx_ref, ctx_low_ref, coef_ref, key_ref, score_ref, serve_pair,
            )

        each(2, pair_step)

    each(groups, group_step)
    keep(0, 1, 2, 3, 4, 5)
    along(10)
    whole(7)
    wide_ref[...] = mm(ctx_low_ref[...], flat_out[...]) + vec_ref[2:3, :breadth]
    norm_forward(tokens_ref, wide_ref, vec_ref, xhat_ref, inverse_ref, normed_ref, normed_low_ref)
    keep(6, 7, 8)

    def upward_step(index):
        serve("up", index)
        where = cols(index, up_tile)
        upward_tile(normed_low_ref, flat_up.at[index], vec_ref[1:2, where], act_ref, slope_ref, where)

    each(groups, upward_step)
    keep(9, 10)

    def downward_step(index):
        serve("down", index)
        where = cols(index, down_tile)
        wide_ref[:, where] = mm(act_ref[...], flat_down[index]) + vec_ref[5:6, where]

    each(groups, downward_step)
    norm_result(seq_ref, normed_ref, wide_ref, vec_ref, cot_ref, out_ref, wide_ref, gvec_ref)
    for item in range(len(full)):
        gather.sent(item)
    for swap in swaps:
        swap.wait_send()
    saver.finish()


def ahead_call(depth, seq, tokens, cotangent, feat, matrices, pieces):
    rows, breadth = tokens.shape
    span_length = 2 * rows
    devices = 8 * depth
    groups, tile = 3, 256
    slots = depth - 1 + 1 + 2 + 4
    longest = max(piece.shape[1] for piece in pieces[:-1]) * devices
    table = pieces[-1].shape[0] * devices // 128
    w_qkv, w_out, w_up, w_down = matrices
    hidden = w_up.shape[1]
    lead = (depth, 4)
    full = [
        (groups,) + lead + (2 * w_qkv.shape[0], 3 * tile), lead + (2 * w_out.shape[0], breadth),
        (groups,) + lead + (2 * w_up.shape[0], hidden // groups),
        (groups,) + lead + (2 * w_down.shape[0], breadth // groups),
    ]
    saved = [(groups, breadth, 3 * tile), (breadth, breadth), (devices * w_up.shape[0], hidden), (devices * w_down.shape[0], breadth)]
    kept = [
        ((rows, 2 * breadth), F32), ((rows, 2 * breadth), F32), ((rows, 3 * breadth), LOW),
        ((rows, breadth), F32), ((rows, breadth), F32), ((rows, breadth), LOW),
        ((rows, breadth), LOW), ((rows, breadth), F32), ((rows, 128), F32), ((rows, hidden), LOW),
        ((rows, hidden), F32),
    ]
    items = 2 + 3 * groups
    return pl.pallas_call(
        functools.partial(ahead_kernel, depth, len(pieces)),
        out_shape=(
            shape((rows, breadth), LOW), shape((len(pieces) - 1, longest), F32),
            shape((len(pieces) - 1, longest), F32), shape((table, 128), F32), shape((rows, breadth), F32),
        )
        + tuple(shape(dims, LOW) for dims in saved)
        + tuple(shape(dims, kind) for dims, kind in kept),
        in_specs=[SCALARS] + vmem(3 + len(matrices) + len(pieces)),
        out_specs=tuple(vmem(5)) + (ANYWHERE,) * len(saved + kept),
        scratch_shapes=[pltpu.VMEM(dims, LOW) for dims in full]
        + [pltpu.VMEM(dims, kind) for dims, kind in kept]
        + [pltpu.VMEM(matrix.shape, F32) for matrix in matrices]
        + [
            pltpu.VMEM((PIECE, 128), F32), pltpu.VMEM((depth, 4, 2, PIECE, 128), F32),
            pltpu.VMEM((rows, rows), F32), pltpu.VMEM((groups, 4 * tile, tile), LOW),
            pltpu.VMEM((128, span_length), F32), pltpu.VMEM((rows, 128), LOW), pltpu.VMEM((rows, rows), LOW),
            pltpu.VMEM((rows, breadth), F32),
            pltpu.SemaphoreType.DMA((items, slots)), pltpu.SemaphoreType.DMA((items, slots)),
            pltpu.SemaphoreType.DMA((1, 4)), pltpu.SemaphoreType.DMA((1, 4)), pltpu.SemaphoreType.DMA((items - 1 + len(kept),)),
        ],
        compiler_params=pltpu.CompilerParams(
            collective_id=0, has_side_effects=True, vmem_limit_bytes=60 * MIB
        ),
        name="ahead",
    )(seq, tokens, cotangent, feat, *matrices, *pieces)


def prepare_back(group, slot, low_ref, den_ref, ctx_ref, g_ctx_ref, swap_ref, ext_ref, key_ref, val_ref, num_ref, flip_ref):
    rows = g_ctx_ref.shape[0]
    breadth = swap_ref.shape[0]
    where = cols(group, breadth)
    lane = jnp.bitwise_and(iota((128, breadth), 1), 127)
    lower = lane < 64

    def step(index):
        at = pl.ds(pl.multiple_of(index * 128, 128), 128)
        g_num = g_ctx_ref[at, where] * (1.0 / den_ref[slot, at, :])
        g_den = -mm2(g_num * ctx_ref[slot, at, :], swap_ref[...])
        high = g_den.astype(LOW).astype(F32)
        rest = g_den - high
        key = low_ref[slot, 1, at, :].astype(F32)
        value = low_ref[slot, 2, at, :].astype(F32)
        for side in range(2):
            mine = jnp.logical_not(lower) if side else lower
            other = 0 if side else 64
            is_high, is_rest = lane == other, lane == other + 1
            extended = jnp.where(mine, g_num, jnp.where(is_high, high, jnp.where(is_rest, rest, 0.0)))
            ext_ref[side, at, :] = extended.astype(LOW)
            key_ref[side, at, :] = jnp.where(mine, key, 0.0).astype(LOW)
            ones = jnp.where(jnp.logical_or(is_high, is_rest), 1.0, 0.0)
            val_ref[side, at, :] = jnp.where(mine, value, ones).astype(LOW)
        num_ref[at, :] = g_num.astype(LOW)

    each(rows // 128, step)
    flip_ref[0] = jnp.transpose(low_ref[slot, 0])
    flip_ref[1] = jnp.transpose(num_ref[...])


def attend_back_pair(
    pair, inner, slot, low_ref, rpe_ref, mask_ref, g_feat_ref, grpe_ref, coef_ref, scores_ref, gk_ref, diag_ref,
    ext_ref, key_ref, val_ref, flip_ref, turn_ref, serve,
):
    rows = mask_ref.shape[0]
    tall = BLOCK_ROWS
    here = cols(inner, 128)
    lower = iota((tall, 128), 1) < 64
    for side in range(2):
        serve(pair, side)
        coefficients(rpe_ref, pair * 2 + side, coef_ref)
        diag_ref[...] = jnp.zeros_like(diag_ref)
        for block in range(rows // tall):
            at = slice(block * tall, block * tall + tall)
            kernel = mm(low_ref[slot, 0, at, here], key_ref[side, :, here], 1, 1)
            g_scores = mm(ext_ref[side, at, here], val_ref[side, :, here], 1, 1)
            for part in range(tall // 128):
                start = block * tall + part * 128
                lead = rows - 128 - start
                inside = slice(part * 128, part * 128 + 128)
                weight = coef_ref[:, lead : lead + rows] * mask_ref[start : start + 128, :]
                scores = kernel[inside] * weight
                diag_ref[:, lead : lead + rows] += g_scores[inside] * scores
                scores_ref[start : start + 128, :] = scores.astype(LOW)
                gk_ref[start : start + 128, :] = (g_scores[inside] * weight).astype(LOW)
            g_query = mm(gk_ref[at, :], low_ref[slot, 1, :, here])
            if side:
                g_query = jnp.where(lower, g_feat_ref[at, here], g_query)
            g_feat_ref[at, here] = g_query
        head_rows = pl.ds(pl.multiple_of(inner * 128 + side * 64, 64), 64)
        turn_ref[0, head_rows, :] = mm(flip_ref[0, head_rows, :], gk_ref[...])
        turn_ref[1, head_rows, :] = mm(flip_ref[1, head_rows, :], scores_ref[...])
        diagonals(diag_ref, grpe_ref, pair * 2 + side)


def diagonals(diag_ref, out_ref, head):
    flip = jnp.where(iota((128, 128), 0) + iota((128, 128), 1) == 127, 1.0, 0.0).astype(LOW)
    value = diag_ref[...]
    high = value.astype(LOW)
    rest = (value - high.astype(F32)).astype(LOW)
    value = pltpu.roll(mm(flip, high) + mm(flip, rest), 0, axis=1, stride=1, stride_axis=0)
    sums = jnp.sum(value, axis=0, keepdims=True)
    for k in range(8):
        out_ref[pl.ds(head * 8 + 7 - k, 1), :] = sums[:, 128 * k : 128 * k + 128]


class Item:
    def __init__(self, given, buffers, row):
        self.given = given
        self.from_core, self.from_second, self.from_first, self.from_depth, self.leaving = buffers
        self.row = row


class Scatter:
    def __init__(self, plane, sems):
        self.plane, self.sems = plane, sems
        self.here = plane.spot(plane.first, plane.second)
        self.across = plane.spot(1 - plane.first, plane.second)
        self.first_slot = plane.depth - 1
        self.second_slot = self.first_slot + 1
        self.core_slot = self.second_slot + 2
        self.last_slot = self.core_slot + 1

    def with_core(self, item):
        return remote(
            half(item.given, ALL, ALL, 1 - self.plane.core), item.from_core, self.sems, item.row, self.core_slot,
            self.plane.sibling,
        )

    def begin(self, item):
        self.with_core(item).start()

    def to_second(self, item, first):
        spot = self.plane.spot(first, 1 - self.plane.second)
        return remote(
            half(item.given, ALL, spot, self.plane.core), item.from_second.at[first], self.sems, item.row,
            self.second_slot + first, self.plane.over_second,
        )

    def to_first(self, item):
        return remote(
            half(item.given, ALL, self.across, self.plane.core), item.from_first, self.sems, item.row,
            self.first_slot, self.plane.over_first,
        )

    def to_depth(self, item, distance):
        plane = self.plane
        z = plane.ahead(distance)
        return remote(
            half(item.given, z, self.here, plane.core), item.from_depth.at[distance - 1], self.sems, item.row,
            distance - 1, plane.device(z, plane.first, plane.second),
        )

    def join(self, item, spot, piece):
        def step(z):
            target = half(item.given, z, spot, self.plane.core)
            target[...] = target[...] + piece(z)

        each(self.plane.depth, step)

    def core(self, item):
        plane = self.plane
        self.with_core(item).wait_recv()
        for first in range(2):
            spot = plane.spot(first, 1 - plane.second)
            self.join(item, spot, lambda z, spot=spot: item.from_core[z, spot])
            self.to_second(item, first).start()
        for first in range(2):
            spot = plane.spot(first, plane.second)
            self.join(item, spot, lambda z, spot=spot: item.from_core[z, spot])

    def second(self, item):
        plane = self.plane
        away = 1 - plane.first
        self.to_second(item, away).wait_recv()
        self.join(item, self.across, lambda z: item.from_second[away, z])
        self.to_first(item).start()
        self.to_second(item, plane.first).wait_recv()
        self.join(item, self.here, lambda z: item.from_second[plane.first, z])

    def first(self, item):
        self.to_first(item).wait_recv()
        self.join(item, self.here, lambda z: item.from_first[z])
        for distance in range(1, self.plane.depth):
            self.to_depth(item, distance).start()

    def summed(self, item):
        plane = self.plane
        for distance in range(1, plane.depth):
            self.to_depth(item, distance).wait_recv()
        value = half(item.given, plane.z, self.here, plane.core)[...].astype(F32)
        for distance in range(1, plane.depth):
            value = value + item.from_depth[distance - 1].astype(F32)
        return value

    def columns(self, item, core):
        breadth = item.leaving.shape[1]
        return pl.ds(pl.multiple_of(core * breadth, 128), breadth)

    def last(self, item, target):
        core = self.plane.core
        return remote(
            item.leaving, target.at[:, self.columns(item, core)], self.sems, item.row, self.last_slot,
            self.plane.sibling,
        )

    def along(self, item, target):
        core = self.plane.core
        value = self.summed(item)
        height = value.shape[0] // 2
        upper, lower = value[:height], value[height:]
        target[:, self.columns(item, core)] = jnp.where(core == 0, upper, lower)
        item.leaving[...] = jnp.where(core == 0, lower, upper)
        self.last(item, target).start()

    def sent(self, item, target=None):
        self.with_core(item).wait_send()
        for first in range(2):
            self.to_second(item, first).wait_send()
        self.to_first(item).wait_send()
        for distance in range(1, self.plane.depth):
            self.to_depth(item, distance).wait_send()
        if target is not None:
            core = self.plane.core
            self.last(item, target).wait_send()
            arrived = target.at[:, self.columns(item, 1 - core)]
            remote(
                item.leaving, arrived, self.sems, item.row, self.last_slot, self.plane.sibling
            ).wait_recv()


def pack_grads(gvec_ref, lengths, grpe_ref, flat_ref):
    devices = flat_ref.shape[0] // PIECE
    table_rows = grpe_ref.shape[0] // devices
    flat_ref[...] = jnp.zeros_like(flat_ref)
    for row, length in enumerate(lengths):
        breadth = length * devices
        value = gvec_ref[row : row + 1, 0:breadth]
        spread = jnp.where(owned(devices, length, breadth), jnp.broadcast_to(value, (devices, breadth)), 0.0)
        flat_ref[pl.ds(row, devices, stride=PIECE), :] = mm2(spread, one_hot(length, breadth), 1)
    for part in range(table_rows):
        flat_ref[pl.ds(len(lengths) + part, devices, stride=PIECE), :] = grpe_ref[
            pl.ds(part, devices, stride=table_rows), :
        ]


def build_back(feat_ref, stack_ref):
    tile = stack_ref.shape[2]
    head_size = feat_ref.shape[1]
    group = tile // head_size
    bits = head_size.bit_length() - 1
    same = lax.shift_right_logical(iota((tile, tile), 0), bits) == lax.shift_right_logical(iota((tile, tile), 1), bits)
    last = stack_ref.shape[0] - 1
    for index in range(last):
        rows_of = []
        for inner in range(group):
            piece = jnp.transpose(feat_ref[index * group + inner].astype(F32))
            rows_of.append(jnp.concatenate([piece] * group, axis=1))
        full = jnp.where(same, jnp.concatenate(rows_of, axis=0), 0.0).astype(LOW)
        for part in range(2):
            stack_ref[index, part * tile : part * tile + tile, :] = full
    for part in range(2):
        stack_ref[last, part * tile : part * tile + tile, :] = jnp.where(same, 1.0, 0.0).astype(LOW)


def build_swap(swap_ref):
    tile = swap_ref.shape[0]
    down = lax.shift_right_logical(iota((tile, tile), 0), 6)
    across = lax.shift_right_logical(iota((tile, tile), 1), 6)
    swap_ref[...] = jnp.where(jnp.bitwise_xor(down, 1) == across, 1.0, 0.0).astype(LOW)


def behind_kernel(depth, lengths, *refs):
    seq_ref, feat_ref, vec_ref, rpe_ref, gvec_in_ref, g_sum_ref, refs = refs[:6] + (refs[6:],)
    w_qkv_hbm, w_out_hbm, w_up_hbm, w_down_hbm, refs = refs[:4] + (refs[4:],)
    scaled_hbm, phi_hbm, low_hbm, den_hbm, ctx_hbm, ctx_low_hbm, refs = refs[:6] + (refs[6:],)
    normed_low_hbm, xhat_hbm, inverse_hbm, act_hbm, slope_hbm, tokens_hbm, refs = refs[:6] + (refs[6:],)
    g_tokens_hbm, s_qkv, s_out, s_up, s_down, s_small, refs = refs[:6] + (refs[6:],)
    d_qkv, d_out, d_up, d_down, d_small, refs = refs[:5] + (refs[5:],)
    buffers, refs = [refs[5 * index : 5 * index + 5] for index in range(5)], refs[25:]
    g_hidden_ref, g_ctx_ref, g_low_ref, gvec_ref, grpe_ref, g_qkv_ref, refs = refs[:6] + (refs[6:],)
    send, recv, load_sem = refs
    rows, breadth = g_sum_ref.shape
    hidden = w_up_hbm.shape[1]
    tile, height = 256, 128
    wide = min(768, breadth)
    plane = Plane(depth)
    scatter = Scatter(plane, (send, recv))
    down, up, out = [
        Item(given, buffers[index], 2 - index)
        for given, index in ((d_down, 2), (d_up, 1), (d_out, 0))
    ]
    small = Item(d_small, buffers[4], 3)
    flat_down, flat_up, flat_out, flat_qkv = d_down.reshape(hidden, breadth), d_up.reshape(breadth, hidden), (
        d_out.reshape(breadth, breadth)
    ), d_qkv.reshape(breadth // tile, breadth, 3 * tile)
    flat_small = d_small.reshape(8 * depth * PIECE, 128)

    def qkv(group):
        return Item(d_qkv.at[group], [buffer.at[group] for buffer in buffers[3]], 4 + group)

    def load(source, target, index):
        return pltpu.make_async_copy(source, target, load_sem.at[index])

    def feed_forward(
        w_out_ref, w_up_ref, w_down_ref, act_ref, slope_ref, normed_low_ref, flip_ref,
        inverse_ref, ctx_low_ref,
    ):
        chunk = slope_ref.shape[2]
        chunks = hidden // chunk
        pending = {}

        def columns(index):
            return slice(index * chunk, index * chunk + chunk)

        acts = [
            load(act_hbm.at[:, columns(index)], act_ref.at[:, columns(index)], 2 * chunks + index)
            for index in range(chunks)
        ]

        def fetch(index):
            at = columns(index)
            pending[index] = [
                load(w_down_hbm.at[at, :], w_down_ref.at[at, :], 2 * index),
                load(slope_hbm.at[:, at], slope_ref.at[index % 2], 2 * index + 1),
            ]
            for copy in pending[index]:
                copy.start()

        for copy in acts:
            copy.start()
        fetch(0)
        fetch(1)
        base = 3 * chunks
        later = [
            load(normed_low_hbm, normed_low_ref, base), load(w_up_hbm, w_up_ref, base + 1),
            load(xhat_hbm, g_hidden_ref, base + 2), load(inverse_hbm, inverse_ref, base + 3),
            load(w_out_hbm, w_out_ref, base + 4), load(ctx_low_hbm, ctx_low_ref, base + 5),
        ]
        g_low_ref[...] = g_sum_ref[...].astype(LOW)
        gvec_ref[...] = gvec_in_ref[...]
        plane.greet()
        for index in range(chunks):
            acts[index].wait()

            at = columns(index)
            flat_down[at, :] = mm(act_ref[:, at], g_low_ref[...], 0, 0).astype(LOW)
        scatter.begin(down)
        for index in range(chunks):
            for copy in pending[index]:
                copy.wait()
            if index == 2:
                scatter.core(down)

            at = columns(index)
            g_upward = mm(g_low_ref[...], w_down_ref[at, :], 1, 1) * slope_ref[index % 2]
            gvec_ref[1:2, at] = column_sum(g_upward)
            act_ref[:, at] = g_upward.astype(LOW)
            if index + 2 < chunks:
                fetch(index + 2)
            if index == 0:
                for copy in later:
                    copy.start()
        for copy in later:
            copy.wait()
        flip_ref[...] = jnp.transpose(normed_low_ref[...])

        def up_step(step):
            where = cols(step, wide)
            flat_up[:, where] = mm(flip_ref[...], act_ref[:, where]).astype(LOW)

        each(hidden // wide, up_step)
        scatter.begin(up)

        g_sum_ref[...] = mm(act_ref[...], w_up_ref[...], 1, 1) + g_sum_ref[...]
        gain_one = vec_ref[3:4, :breadth]

        def first_back(step):
            at = pl.ds(pl.multiple_of(step * height, height), height)
            g_normed = g_sum_ref[at, :]
            xhat = g_hidden_ref[at, :]
            add_to(gvec_ref, 3, column_sum(g_normed * xhat))
            add_to(gvec_ref, 4, column_sum(g_normed))
            g_hidden = norm_back(g_normed, xhat, inverse_ref[at, 0:1], gain_one)
            add_to(gvec_ref, 2, column_sum(g_hidden))
            g_hidden_ref[at, :] = g_hidden
            g_low_ref[at, :] = g_hidden.astype(LOW)

        each(rows // height, first_back)

        flat_out[...] = mm(ctx_low_ref[...], g_low_ref[...], 0, 0).astype(LOW)
        scatter.begin(out)
        scatter.core(up)
        scatter.second(down)
        g_ctx_ref[...] = mm(g_low_ref[...], w_out_ref[...], 1, 1)

    chunk = min(768, hidden)
    pl.run_scoped(
        feed_forward,
        pltpu.VMEM(w_out_hbm.shape, LOW), pltpu.VMEM(w_up_hbm.shape, LOW), pltpu.VMEM(w_down_hbm.shape, LOW),
        pltpu.VMEM((rows, hidden), LOW), pltpu.VMEM((2, rows, chunk), F32),
        pltpu.VMEM((rows, breadth), LOW), pltpu.VMEM((breadth, rows), LOW),
        pltpu.VMEM((rows, 128), F32), pltpu.VMEM((rows, breadth), LOW),
    )

    calls = {
        4: (lambda: scatter.core(out), lambda: scatter.first(down)),
        7: (lambda: scatter.second(up),),
        9: (lambda: scatter.core(qkv(0)), lambda: scatter.first(up)),
        11: (lambda: scatter.second(out), lambda: scatter.core(qkv(1))),
    }

    def serve(pair, side):
        for head, steps in calls.items():
            if head % 2 == side:

                @pl.when(pair == head // 2)
                def _(steps=steps):
                    for step in steps:
                        step()

    def attention(
        w_qkv_ref, flip_ref, scaled_ref, phi_ref, low_ref, den_ref, ctx_ref, g_feat_ref, coef_ref,
        scores_ref, gk_ref, diag_ref, ext_ref, key_ref, val_ref, num_ref, turn_low_ref, turn_ref, swap_ref, mask_ref, stack_ref,
    ):
        groups = breadth // tile

        def part(ref, at, number):
            return ref.at[:, pl.ds(pl.multiple_of(at * tile + number * breadth, tile), tile)]

        def loads(group):
            slot = lax.rem(group, 2)
            copies = []
            for number in range(3):
                copies.append((part(low_hbm, group, number), low_ref.at[slot, number]))
            copies.append((part(den_hbm, group, 0), den_ref.at[slot]))
            copies.append((part(ctx_hbm, group, 0), ctx_ref.at[slot]))
            for number in range(2):
                copies.append((part(scaled_hbm, group, number), scaled_ref.at[slot, number]))
                copies.append((part(phi_hbm, group, number), phi_ref.at[slot, number]))
            return [
                load(source, target, slot * 9 + index) for index, (source, target) in enumerate(copies)
            ]

        base = 18
        tokens_copy = load(tokens_hbm, g_low_ref, base)

        def weights(group):
            return load(w_qkv_hbm.at[group], w_qkv_ref.at[group % 2], base + 1 + group)

        for copy in loads(0):
            copy.start()
        for copy in (tokens_copy, weights(0), weights(1)):
            copy.start()
        segment_mask(seq_ref, mask_ref)
        build_back(feat_ref, stack_ref)
        tokens_copy.wait()
        flip_ref[...] = jnp.transpose(g_low_ref[...])
        build_swap(swap_ref)
        scale = 64 ** (-0.25)

        def group_step(group):
            slot = lax.rem(group, 2)
            for copy in loads(group):
                copy.wait()

            @pl.when(group + 1 < groups)
            def _():
                for copy in loads(group + 1):
                    copy.start()

            prepare_back(
                group, slot, low_ref, den_ref, ctx_ref, g_ctx_ref, swap_ref, ext_ref, key_ref, val_ref, num_ref,
                turn_low_ref,
            )

            def pair_step(inner):
                pair = 2 * group + inner
                attend_back_pair(
                    pair, inner, slot, low_ref, rpe_ref, mask_ref, g_feat_ref, grpe_ref, coef_ref, scores_ref,
                    gk_ref, diag_ref, ext_ref, key_ref, val_ref, turn_low_ref, turn_ref, serve,
                )

            each(2, pair_step)

            g_feat_ref[:, tile : 2 * tile] = jnp.transpose(turn_ref[0])
            g_feat_ref[:, 2 * tile : 3 * tile] = jnp.transpose(turn_ref[1])
            for number in range(3):
                at = slice(number * tile, number * tile + tile)
                where = pl.ds(pl.multiple_of(group * tile + number * breadth, tile), tile)
                grad = g_feat_ref[:, at]
                if number < 2:
                    upward = jnp.concatenate(two_parts(grad * phi_ref[slot, number]), axis=1)
                    total = mm(upward, stack_ref[groups])
                    grad = mm(upward, stack_ref[group]) - scaled_ref[slot, number] * total
                    grad = grad * scale
                gvec_ref[0:1, where] = column_sum(grad)
                g_qkv_ref[group, :, at] = grad.astype(LOW)
            flat_qkv[group] = mm(flip_ref[...], g_qkv_ref[group]).astype(LOW)
            scatter.begin(qkv(group))

        each(groups, group_step)
        scatter.second(qkv(0))
        scatter.core(qkv(2))
        scatter.along(down, s_down)
        scatter.first(out)
        scatter.first(qkv(0))
        flip = jnp.where(iota((128, 128), 0) + iota((128, 128), 1) == 127, 1.0, 0.0).astype(LOW)
        grpe_ref[...] = mm2(grpe_ref[...], flip)
        pack_grads(gvec_ref, lengths, grpe_ref, flat_small)
        scatter.begin(small)
        scatter.second(qkv(1))

        def inputs(group):
            weights(group).wait()
            g_hidden_ref[...] += mm(g_qkv_ref[group], w_qkv_ref[group % 2], 1, 1)
            if group + 2 < groups:
                weights(group + 2).start()

        inputs(0)
        inputs(1)
        scatter.core(small)
        inputs(2)

    pl.run_scoped(
        attention,
        pltpu.VMEM((2,) + w_qkv_hbm.shape[1:], LOW), pltpu.VMEM((breadth, rows), LOW),
        pltpu.VMEM((2, 2, rows, tile), F32), pltpu.VMEM((2, 2, rows, tile), F32),
        pltpu.VMEM((2, 3, rows, tile), LOW), pltpu.VMEM((2, rows, tile), F32), pltpu.VMEM((2, rows, tile), F32),
        pltpu.VMEM((rows, 3 * tile), F32), pltpu.VMEM((128, 2 * rows), F32), pltpu.VMEM((rows, rows), LOW),
        pltpu.VMEM((rows, rows), LOW), pltpu.VMEM((128, 2 * rows), F32), pltpu.VMEM((2, rows, tile), LOW),
        pltpu.VMEM((2, rows, tile), LOW), pltpu.VMEM((2, rows, tile), LOW), pltpu.VMEM((rows, tile), LOW),
        pltpu.VMEM((2, tile, rows), LOW), pltpu.VMEM((2, tile, rows), F32), pltpu.VMEM((tile, tile), LOW),
        pltpu.VMEM((rows, rows), F32), pltpu.VMEM((breadth // tile + 1, 2 * tile, tile), LOW),
    )
    result = load(g_hidden_ref, g_tokens_hbm, 31)
    result.start()
    scatter.second(qkv(2))
    scatter.first(qkv(1))
    scatter.second(small)
    scatter.along(out, s_out)
    scatter.along(up, s_up)
    scatter.first(small)
    scatter.first(qkv(2))
    scatter.along(qkv(1), s_qkv.at[1])
    scatter.along(qkv(0), s_qkv.at[0])
    scatter.along(qkv(2), s_qkv.at[2])
    s_small[...] = scatter.summed(small)
    for item, target in ((down, s_down), (up, s_up), (out, s_out), (small, None)):
        scatter.sent(item, target)
    for group in range(breadth // tile):
        scatter.sent(qkv(group), s_qkv.at[group])
    result.wait()


def behind_call(depth, seq, feat, vec, rpe, gvec, g_sum, weights, kept, tokens, lengths):
    rows, breadth = tokens.shape
    chips = 4 * depth
    devices = 2 * chips
    w_qkv, w_out, w_up, w_down = weights
    group = 3 * 256
    groups = w_qkv.shape[0]
    table = rpe.shape[0]
    blocks = [(w.shape[0] // devices, w.shape[1]) for w in (w_out, w_up, w_down)]
    lead = (depth, 4)
    given = [lead + (2 * block[0], block[1]) for block in blocks]
    qkv_block = (w_qkv.shape[1] // devices, group)

    def buffers(block, kind, front=()):
        if kind == LOW:
            part, leaving = (2 * block[0], block[1] // 2), (block[0], block[1] // 2)
        else:
            part, leaving = block, (8, 128)
        numbers = [lead, (2, depth), (depth,), (depth - 1,)]
        return [pltpu.VMEM(front + number + part, kind) for number in numbers] + [pltpu.VMEM(front + leaving, F32)]

    slots = depth - 1 + 1 + 2 + 2
    scratch = [pltpu.VMEM((groups,) + lead + (2 * qkv_block[0], group), LOW)]
    scratch += [pltpu.VMEM(dims, LOW) for dims in given]
    scratch += [pltpu.VMEM(lead + (2, PIECE, 128), F32)]
    for block in blocks:
        scratch += buffers(block, LOW)
    scratch += buffers(qkv_block, LOW, (groups,)) + buffers((PIECE, 128), F32)
    scratch += [
        pltpu.VMEM((rows, breadth), F32), pltpu.VMEM((rows, breadth), F32), pltpu.VMEM((rows, breadth), LOW),
        pltpu.VMEM(vec.shape, F32), pltpu.VMEM((table, 128), F32), pltpu.VMEM((groups, rows, group), LOW),
        pltpu.SemaphoreType.DMA((7, slots)), pltpu.SemaphoreType.DMA((7, slots)), pltpu.SemaphoreType.DMA((32,)),
    ]
    return pl.pallas_call(
        functools.partial(behind_kernel, depth, lengths),
        out_shape=(
            shape((rows, breadth), F32), shape((groups,) + qkv_block, F32),
        ) + tuple(shape(block, F32) for block in blocks) + (shape((PIECE, 128), F32),),
        in_specs=[SCALARS] + vmem(5) + [ANYWHERE] * (4 + len(kept) + 1),
        out_specs=(ANYWHERE,) + tuple(vmem(5)),
        scratch_shapes=scratch,
        compiler_params=pltpu.CompilerParams(
            collective_id=1, has_side_effects=True, vmem_limit_bytes=62 * MIB
        ),
        name="behind",
    )(seq, feat, vec, rpe, gvec, g_sum, *weights, *kept, tokens)


def emit_kernel(count, lengths, *refs):
    big, small, refs = refs[:count], refs[count], refs[count + 1 :]
    outs, refs = refs[:count], refs[count:]
    pieces, held, sems = refs[: len(lengths) + 1], refs[len(lengths) + 1 : -1], refs[-1]
    inward, owners = [], []
    for index in range(count):
        if len(big[index].shape) == 3:
            groups, _, breadth = big[index].shape
            tile = breadth // 3
            for group in range(groups):
                for part in range(3):
                    start = part * breadth + group * tile
                    source = big[index].at[group, :, part * tile : part * tile + tile]
                    inward.append((source, held[index].at[:, start : start + tile]))
                    owners.append(index)
        else:
            inward.append((big[index], held[index]))
            owners.append(index)
    inward = [
        pltpu.make_async_copy(source, target, sems.at[0, index]) for index, (source, target) in enumerate(inward)
    ]
    outward = [pltpu.make_async_copy(held[index], outs[index], sems.at[1, index]) for index in range(count)]
    for copy in inward:
        copy.start()
    for row, length in enumerate(lengths):
        pieces[row][...] = small[row : row + 1, 0:length]
    table = pieces[-1]
    for part in range(table.shape[0] // 128):
        row = len(lengths) + part
        table[128 * part : 128 * part + 128] = small[row : row + 1, :].reshape(128)
    for index in range(count):
        for owner, copy in zip(owners, inward):
            if owner == index:
                copy.wait()
        outward[index].start()
    for copy in outward:
        copy.wait()


def emit_call(arrays, small, lengths, table):
    shapes = [
        (array.shape[1], array.shape[0] * array.shape[2]) if len(array.shape) == 3 else array.shape for array in arrays
    ]
    result = pl.pallas_call(
        functools.partial(emit_kernel, len(arrays), lengths),
        out_shape=tuple(shape(dims, array.dtype) for dims, array in zip(shapes, arrays))
        + tuple(shape((1, length), F32) for length in lengths) + (shape((table,), F32),),
        in_specs=[ANYWHERE] * len(arrays) + vmem(1),
        out_specs=(ANYWHERE,) * len(arrays) + tuple(vmem(len(lengths) + 1)),
        scratch_shapes=[pltpu.VMEM(dims, array.dtype) for dims, array in zip(shapes, arrays)]
        + [pltpu.SemaphoreType.DMA((2, len(arrays) + 8))],
        compiler_params=pltpu.CompilerParams(vmem_limit_bytes=60 * MIB),
        name="emit",
    )(*arrays, small)
    return result[: len(arrays)], [piece.reshape(-1) for piece in result[len(arrays) :]]


def plain_gather(value):
    return lax.all_gather(value.astype(LOW), "dp", axis=0, tiled=True)


def plain_scatter(value):
    return lax.psum_scatter(value.astype(F32), "dp", scatter_dimension=0, tiled=True)


def body(
    depth, tokens, cotangent, seq_lengths, random_feat, w_qkv, b_qkv, w_out, b_out, ln1_gain, ln1_bias,
    w_up, b_up, w_down, b_down, ln2_gain, ln2_bias, rpe_table,
):
    vectors = (b_qkv, b_up, b_out, ln1_gain, ln1_bias, b_down, ln2_gain, ln2_bias)
    matrices = (w_qkv, w_out, w_up, w_down)
    lengths = tuple(piece.shape[0] for piece in vectors)
    if depth:
        pieces = [piece.reshape(1, -1) for piece in vectors] + [rpe_table]
        result = ahead_call(depth, seq_lengths, tokens, cotangent, random_feat, matrices, pieces)
        out, gvec, vec, rpe = result[:4]
        g_sum, weights, kept = result[4], result[5:9], result[9:]
        g_tokens, s_qkv, s_out, s_up, s_down, small = behind_call(
            depth, seq_lengths, random_feat, vec, rpe, gvec, g_sum, weights, kept, tokens, lengths
        )
        arrays, pieces = emit_call(
            (out, g_tokens, s_qkv, s_out, s_up, s_down), small, lengths, rpe_table.shape[0]
        )
        out, g_tokens, s_qkv, s_out, s_up, s_down = arrays
    else:
        full_vectors = [plain_gather(piece).astype(F32) for piece in vectors]
        longest = max(piece.shape[0] for piece in full_vectors)
        vec = jnp.stack([jnp.pad(piece, (0, longest - piece.shape[0])) for piece in full_vectors])
        rpe = plain_gather(rpe_table).astype(F32).reshape(-1, 128)
        full_qkv, full_out, full_up, full_down = [plain_gather(piece) for piece in matrices]
        scaled, phi, low, den, ctx, ctx_low = forward_call(seq_lengths, tokens, random_feat, full_qkv, vec, rpe)
        out, g_hidden, g_ctx, d_out, d_up, d_down, gvec_one = middle_call(
            seq_lengths, tokens, cotangent, ctx_low, vec, full_out, full_up, full_down
        )
        g_tokens, d_qkv, gvec_two, grpe = backward_call(
            seq_lengths, tokens, random_feat, full_qkv, rpe, scaled, phi, low, den, ctx, g_ctx, g_hidden, vec
        )
        gvec = gvec_one + gvec_two
        s_qkv, s_out, s_up, s_down = [plain_scatter(grad) for grad in (d_qkv, d_out, d_up, d_down)]
        devices = lax.axis_size("dp")
        pieces = [plain_scatter(gvec[row, : length * devices]) for row, length in enumerate(lengths)]
        pieces.append(plain_scatter(grpe.reshape(-1)))
    p_qkv, p_up, p_out, p_gain_one, p_bias_one, p_down, p_gain_two, p_bias_two, p_rpe = pieces
    return (
        out, g_tokens, s_qkv, p_qkv, s_out, p_out, p_gain_one, p_bias_one, s_up, p_up, s_down, p_down,
        p_gain_two, p_bias_two, p_rpe,
    )


def solution(mesh):
    wide, flat = P("dp", None), P("dp")
    devices = mesh.shape["dp"]
    depth = devices // 8 if devices == 32 else 0
    in_specs = (
        wide, wide, wide, P(), wide, flat, wide, flat, flat, flat, wide, flat, wide, flat, flat, flat, flat,
    )
    out_specs = (
        wide, wide, wide, flat, wide, flat, flat, flat, wide, flat, wide, flat, flat, flat, flat,
    )
    return jax.shard_map(
        functools.partial(body, depth), mesh=mesh, in_specs=in_specs, out_specs=out_specs, check_vma=False
    )
```

```python
import functools

import jax
import jax.numpy as jnp
from jax import lax
from jax.experimental import pallas as pl
from jax.experimental.pallas import tpu as pltpu
from jax.sharding import PartitionSpec as P

EPSILON = 1e-05
F32 = jnp.float32
LOW = jnp.bfloat16
MESH = pl.DeviceIdType.MESH
MIB = 2**20


def mm(first_op, second_op, first_dim=1, second_dim=0):
    return lax.dot_general(
        first_op,
        second_op,
        (((first_dim,), (second_dim,)), ((), ())),
        preferred_element_type=F32,
    )


def mm2(value, weight, weight_dim=0):
    high = value.astype(LOW)
    rest = (value - high.astype(F32)).astype(LOW)
    return mm(high, weight, 1, weight_dim) + mm(rest, weight, 1, weight_dim)


def iota(shape, dim):
    return lax.broadcasted_iota(jnp.int32, shape, dim)


def cols(index, width):
    return pl.ds(pl.multiple_of(index * width, width), width)


def build_tables(seq_ref, feat_ref, mask_ref, block_ref, ones_ref):
    rows = mask_ref.shape[0]
    first_end = seq_ref[0, 0]
    second_end = first_end + seq_ref[0, 1]

    def segment(place):
        return (place >= first_end).astype(jnp.int32) + (place >= second_end).astype(jnp.int32)

    across = segment(iota((128, rows), 1))
    for start in range(0, rows, 128):
        down = segment(iota((128, rows), 0) + start)
        mask_ref[start : start + 128, :] = jnp.where(down == across, 1.0, 0.0)
    head_size = feat_ref.shape[1]
    breadth = ones_ref.shape[0]
    group = breadth // head_size
    bits = head_size.bit_length() - 1
    owner_row = lax.shift_right_logical(iota((breadth, breadth), 0), bits)
    owner_col = lax.shift_right_logical(iota((breadth, breadth), 1), bits)
    same = owner_row == owner_col
    ones_ref[...] = jnp.where(same, 1.0, 0.0).astype(LOW)
    for index in range(feat_ref.shape[0] // group):
        rows_of = []
        for inner in range(group):
            piece = feat_ref[index * group + inner].astype(F32)
            rows_of.append(jnp.concatenate([piece] * group, axis=1))
        full = jnp.concatenate(rows_of, axis=0)
        block_ref[index] = jnp.where(same, full, 0.0).astype(LOW)


def project(tokens_ref, w_ref, vec_ref, scaled_ref, phi_ref, low_ref, block_ref, ones_ref):
    breadth = tokens_ref.shape[1]
    tile = ones_ref.shape[0]
    per_part = breadth // tile
    scale = 64 ** (-0.25)

    def features(step, carry):
        where = cols(step, tile)
        acc = mm(tokens_ref[...], w_ref[:, where]) + vec_ref[0:1, where]
        scaled = acc * scale
        scaled_ref[:, where] = scaled
        block = block_ref[lax.rem(step, per_part)]
        mapped = mm2(scaled, block)
        squared = mm2(scaled * scaled, ones_ref[...])
        phi = jnp.exp(mapped - 0.5 * squared) * 0.125
        phi_ref[:, where] = phi
        low_ref[:, where] = phi.astype(LOW)
        return carry

    lax.fori_loop(0, 2 * per_part, features, 0)

    def plain(step, carry):
        where = cols(step + 2 * per_part, tile)
        acc = mm(tokens_ref[...], w_ref[:, where]) + vec_ref[0:1, where]
        low_ref[:, where] = acc.astype(LOW)
        return carry

    lax.fori_loop(0, per_part, plain, 0)


def coefficients(rpe_ref, head, coef_ref):
    flip = (iota((128, 128), 0) + iota((128, 128), 1) == 127).astype(F32).astype(LOW)
    raw = rpe_ref[pl.ds(pl.multiple_of(head * 8, 8), 8), :].astype(LOW)
    table = jnp.exp(mm(raw, flip))
    wide = jnp.concatenate(
        [jnp.broadcast_to(table[7 - k : 8 - k, :], (128, 128)) for k in range(8)], axis=1
    )
    coef_ref[...] = pltpu.roll(wide, 1024 - 127, axis=1, stride=1, stride_axis=0)


def attend(low_ref, rpe_ref, mask_ref, den_ref, ctx_ref, ctx_low_ref, coef_ref, key_ref):
    rows, breadth = ctx_ref.shape

    def pair_step(pair, carry):
        q_at = cols(pair, 128)
        k_at = pl.ds(pl.multiple_of(pair * 128 + breadth, 128), 128)
        v_at = pl.ds(pl.multiple_of(pair * 128 + 2 * breadth, 128), 128)
        lane = iota((128, 128), 1)
        for side in range(2):
            coefficients(rpe_ref, pair * 2 + side, coef_ref)
            mine = lane >= 64 if side else lane < 64
            keep_half(low_ref, k_at, key_ref, side)
            for block in range(rows // 128):
                at = slice(block * 128, block * 128 + 128)
                kernel = mm(low_ref[at, q_at], key_ref[...], 1, 1)
                lead = 128 * (rows // 128 - 1 - block)
                scores = kernel * (coef_ref[:, lead : lead + rows] * mask_ref[at, :])
                total = jnp.sum(scores, axis=1, keepdims=True)
                context = mm(scores.astype(LOW), low_ref[:, v_at]) * (1.0 / total)
                total = jnp.broadcast_to(total, (128, 128))
                if side == 0:
                    den_ref[at, q_at] = total
                    ctx_ref[at, q_at] = context
                else:
                    den_ref[at, q_at] = jnp.where(mine, total, den_ref[at, q_at])
                    context = jnp.where(mine, context, ctx_ref[at, q_at])
                    ctx_ref[at, q_at] = context
                    ctx_low_ref[at, q_at] = context.astype(LOW)
        return carry

    lax.fori_loop(0, breadth // 128, pair_step, 0)


def keep_half(low_ref, where, out_ref, side):
    rows = low_ref.shape[0]
    lane = iota((rows, 128), 1)
    mine = lane >= 64 if side else lane < 64
    out_ref[...] = jnp.where(mine, low_ref[:, where].astype(F32), 0.0).astype(LOW)


def forward_kernel(
    seq_ref, tokens_ref, feat_ref, w_ref, vec_ref, rpe_ref,
    scaled_ref, phi_ref, low_ref, den_ref, ctx_ref, ctx_low_ref,
    mask_ref, block_ref, ones_ref, coef_ref, key_ref,
):
    build_tables(seq_ref, feat_ref, mask_ref, block_ref, ones_ref)
    project(tokens_ref, w_ref, vec_ref, scaled_ref, phi_ref, low_ref, block_ref, ones_ref)
    attend(low_ref, rpe_ref, mask_ref, den_ref, ctx_ref, ctx_low_ref, coef_ref, key_ref)


def norm(value):
    centred = value - jnp.mean(value, axis=-1, keepdims=True)
    inverse = lax.rsqrt(jnp.mean(centred * centred, axis=-1, keepdims=True) + EPSILON)
    return centred * inverse, inverse


def norm_back(grad, xhat, inverse, gain):
    scaled = grad * gain
    mean = jnp.mean(scaled, axis=-1, keepdims=True)
    along = jnp.mean(scaled * xhat, axis=-1, keepdims=True)
    return inverse * (scaled - mean - xhat * along)


def add_to(ref, row, value):
    ref[row : row + 1, 0 : value.shape[1]] += value


def column_sum(value):
    return jnp.sum(value, axis=0, keepdims=True)


def middle_kernel(
    seq_ref, tokens_ref, cot_ref, ctx_low_ref, vec_ref, w_out_ref, w_up_ref, w_down_ref,
    out_ref, g_hidden_ref, g_ctx_ref, d_out_ref, d_up_ref, d_down_ref, gvec_ref,
    wide_ref, normed_ref, normed_low_ref, xhat_ref, inverse_ref, act_ref, slope_ref, g_sum_ref,
    g_low_ref, g_up_ref, flip_ref,
):
    rows, breadth = tokens_ref.shape
    hidden = w_up_ref.shape[1]
    height, tile = 128, 256
    blocks, tiles = rows // height, breadth // tile
    valid_rows = seq_ref[0, 0] + seq_ref[0, 1]
    gvec_ref[...] = jnp.zeros_like(gvec_ref)
    gain_one, bias_one = vec_ref[3:4, :breadth], vec_ref[4:5, :breadth]
    gain_two, bias_two = vec_ref[6:7, :breadth], vec_ref[7:8, :breadth]

    def rows_at(step):
        return pl.ds(pl.multiple_of(step * height, height), height)

    def loop(count, step):
        def run(index, carry):
            step(index)
            return carry

        lax.fori_loop(0, count, run, 0)

    def attended_step(step):
        where = cols(step, tile)
        wide_ref[:, where] = mm(ctx_low_ref[...], w_out_ref[:, where]) + vec_ref[2:3, where]

    loop(tiles, attended_step)

    def first_norm(step):
        at = rows_at(step)
        xhat, inverse = norm(tokens_ref[at, :].astype(F32) + wide_ref[at, :])
        xhat_ref[at, :] = xhat
        inverse_ref[at, :] = jnp.broadcast_to(inverse, (height, 128))
        normed = xhat * gain_one + bias_one
        normed_ref[at, :] = normed
        normed_low_ref[at, :] = normed.astype(LOW)

    loop(blocks, first_norm)

    def upward_step(step):
        where = cols(step, tile)
        upward = mm(normed_low_ref[...], w_up_ref[:, where]) + vec_ref[1:2, where]
        phi = 0.5 + 0.5 * lax.erf(upward * 0.5**0.5)
        density = jnp.exp(-0.5 * upward * upward) * 0.3989422804014327
        act_ref[:, where] = (upward * phi).astype(LOW)
        slope_ref[:, where] = phi + upward * density

    loop(hidden // tile, upward_step)

    def downward_step(step):
        where = cols(step, tile)
        wide_ref[:, where] = mm(act_ref[...], w_down_ref[:, where]) + vec_ref[5:6, where]

    loop(tiles, downward_step)

    def second_norm(step):
        at = rows_at(step)
        xhat, inverse = norm(normed_ref[at, :] + wide_ref[at, :])
        out_ref[at, :] = (xhat * gain_two + bias_two).astype(LOW)
        place = iota((height, breadth), 0) + step * height
        grad = jnp.where(place < valid_rows, cot_ref[at, :].astype(F32), 0.0)
        add_to(gvec_ref, 6, column_sum(grad * xhat))
        add_to(gvec_ref, 7, column_sum(grad))
        g_sum = norm_back(grad, xhat, inverse, gain_two)
        add_to(gvec_ref, 5, column_sum(g_sum))
        g_sum_ref[at, :] = g_sum
        g_low_ref[at, :] = g_sum.astype(LOW)

    loop(blocks, second_norm)
    flip_ref[...] = jnp.transpose(normed_low_ref[...])

    def down_step(step):
        where = cols(step, tile)
        g_upward = mm(g_low_ref[...], w_down_ref[where, :], 1, 1) * slope_ref[:, where]
        gvec_ref[1:2, where] = column_sum(g_upward)
        g_upward = g_upward.astype(LOW)
        g_up_ref[:, where] = g_upward
        d_down_ref[where, :] = mm(act_ref[:, where], g_low_ref[...], 0, 0).astype(LOW)
        d_up_ref[:, where] = mm(flip_ref[...], g_upward).astype(LOW)

    loop(hidden // tile, down_step)

    def up_back(step):
        where = cols(step, tile)
        wide_ref[:, where] = mm(g_up_ref[...], w_up_ref[where, :], 1, 1) + g_sum_ref[:, where]

    loop(tiles, up_back)

    def first_back(step):
        at = rows_at(step)
        g_normed = wide_ref[at, :]
        xhat = xhat_ref[at, :]
        add_to(gvec_ref, 3, column_sum(g_normed * xhat))
        add_to(gvec_ref, 4, column_sum(g_normed))
        g_hidden = norm_back(g_normed, xhat, inverse_ref[at, 0:1], gain_one)
        add_to(gvec_ref, 2, column_sum(g_hidden))
        g_hidden_ref[at, :] = g_hidden
        g_low_ref[at, :] = g_hidden.astype(LOW)

    loop(blocks, first_back)

    def out_back(step):
        where = cols(step, tile)
        g_ctx_ref[:, where] = mm(g_low_ref[...], w_out_ref[where, :], 1, 1)
        d_out_ref[where, :] = mm(ctx_low_ref[:, where], g_low_ref[...], 0, 0).astype(LOW)

    loop(tiles, out_back)


def plain_diagonals(diag_ref, out_ref, head):
    value = diag_ref[...]
    height = value.shape[0]
    while height > 1:
        height //= 2
        value = value[height:] + pltpu.roll(value[:height], height, axis=1)
    for k in range(8):
        out_ref[pl.ds(head * 8 + 7 - k, 1), :] = value[:, 128 * k : 128 * k + 128]


def attend_back(
    low_ref, rpe_ref, mask_ref, den_ref, ctx_ref, g_ctx_ref,
    g_feat_ref, g_low_ref, gvec_ref, grpe_ref,
    coef_ref, scores_ref, gk_ref, diag_ref, query_ref, key_ref, value_ref, num_ref,
):
    rows, breadth = ctx_ref.shape

    def pair_step(pair, carry):
        q_at = cols(pair, 128)
        k_at = pl.ds(pl.multiple_of(pair * 128 + breadth, 128), 128)
        v_at = pl.ds(pl.multiple_of(pair * 128 + 2 * breadth, 128), 128)
        lane = iota((128, 128), 1)
        ones = jnp.ones((128, 128), LOW)
        for side in range(2):
            coefficients(rpe_ref, pair * 2 + side, coef_ref)
            mine = lane >= 64 if side else lane < 64
            other = 0 if side else 64
            keep_half(low_ref, q_at, query_ref, side)
            keep_half(low_ref, k_at, key_ref, side)
            keep_half(low_ref, v_at, value_ref, side)
            diag_ref[...] = jnp.zeros_like(diag_ref)
            is_high, is_rest = lane == other, lane == other + 1
            extra = jnp.where(jnp.logical_or(is_high, is_rest), 1.0, 0.0)
            for block in range(rows // 128):
                at = slice(block * 128, block * 128 + 128)
                value_ref[at, :] = (value_ref[at, :].astype(F32) + extra).astype(LOW)
            for block in range(rows // 128):
                at = slice(block * 128, block * 128 + 128)
                kernel = mm(low_ref[at, q_at], key_ref[...], 1, 1)
                g_num = jnp.where(mine, g_ctx_ref[at, q_at] * (1.0 / den_ref[at, q_at]), 0.0)
                g_den = -mm2(g_num * ctx_ref[at, q_at], ones)
                num_ref[at, :] = g_num.astype(LOW)
                high = g_den.astype(LOW).astype(F32)
                extended = jnp.where(is_high, high, jnp.where(is_rest, g_den - high, g_num))
                g_scores = mm(extended.astype(LOW), value_ref[...], 1, 1)
                lead = 128 * (rows // 128 - 1 - block)
                weight = coef_ref[:, lead : lead + rows] * mask_ref[at, :]
                scores = kernel * weight
                g_kernel = (g_scores * weight).astype(LOW)
                diag_ref[:, lead : lead + rows] += g_scores * scores
                scores_ref[at, :] = scores.astype(LOW)
                gk_ref[at, :] = g_kernel
                g_query = mm(g_kernel, key_ref[...])
                if side:
                    g_query = g_query + g_feat_ref[at, q_at]
                g_feat_ref[at, q_at] = g_query
            g_key = mm(gk_ref[...], query_ref[...], 0, 0)
            g_value = mm(scores_ref[...], num_ref[...], 0, 0)
            if side:
                g_key = g_key + g_feat_ref[:, k_at]
                g_value = g_value + g_feat_ref[:, v_at]
            g_feat_ref[:, k_at] = g_key
            g_feat_ref[:, v_at] = g_value
            plain_diagonals(diag_ref, grpe_ref, pair * 2 + side)
        g_value = g_feat_ref[:, v_at]
        gvec_ref[0:1, v_at] = column_sum(g_value)
        g_low_ref[:, v_at] = g_value.astype(LOW)
        return carry

    lax.fori_loop(0, breadth // 128, pair_step, 0)
    flip = (jnp.where(iota((128, 128), 0) + iota((128, 128), 1) == 127, 1.0, 0.0)).astype(LOW)
    grpe_ref[...] = mm2(grpe_ref[...], flip)


def project_back(
    tokens_ref, w_ref, g_hidden_ref, phi_ref, scaled_ref, block_ref, ones_ref,
    g_feat_ref, g_low_ref, gvec_ref, g_tokens_ref, d_qkv_ref, flip_ref,
):
    breadth = tokens_ref.shape[1]
    tile = ones_ref.shape[0]
    per_part = breadth // tile
    scale = 64 ** (-0.25)

    def features(step, carry):
        where = cols(step, tile)
        upward = g_feat_ref[:, where] * phi_ref[:, where]
        total = mm2(upward, ones_ref[...])
        grad = mm2(upward, block_ref[lax.rem(step, per_part)], 1) - scaled_ref[:, where] * total
        grad = grad * scale
        gvec_ref[0:1, where] = column_sum(grad)
        g_low_ref[:, where] = grad.astype(LOW)
        return carry

    lax.fori_loop(0, 2 * per_part, features, 0)
    flip_ref[...] = jnp.transpose(tokens_ref[...])

    def weights(step, carry):
        where = cols(step, tile)
        d_qkv_ref[:, where] = mm(flip_ref[...], g_low_ref[:, where]).astype(LOW)
        return carry

    lax.fori_loop(0, 3 * per_part, weights, 0)

    def inputs(step, carry):
        where = cols(step, tile)
        g_tokens_ref[:, where] = mm(g_low_ref[...], w_ref[where, :], 1, 1) + g_hidden_ref[:, where]
        return carry

    lax.fori_loop(0, per_part, inputs, 0)


def backward_kernel(
    seq_ref, tokens_ref, feat_ref, w_ref, rpe_ref, scaled_ref, phi_ref, low_ref, den_ref, ctx_ref,
    g_ctx_ref, g_hidden_ref,
    g_tokens_ref, d_qkv_ref, gvec_ref, grpe_ref,
    mask_ref, block_ref, ones_ref, coef_ref, g_feat_ref, g_low_ref, scores_ref, gk_ref, diag_ref,
    query_ref, key_ref, value_ref, num_ref, flip_ref,
):
    build_tables(seq_ref, feat_ref, mask_ref, block_ref, ones_ref)
    gvec_ref[...] = jnp.zeros_like(gvec_ref)
    attend_back(
        low_ref, rpe_ref, mask_ref, den_ref, ctx_ref, g_ctx_ref, g_feat_ref, g_low_ref, gvec_ref, grpe_ref,
        coef_ref, scores_ref, gk_ref, diag_ref, query_ref, key_ref, value_ref, num_ref,
    )
    project_back(
        tokens_ref, w_ref, g_hidden_ref, phi_ref, scaled_ref, block_ref, ones_ref,
        g_feat_ref, g_low_ref, gvec_ref, g_tokens_ref, d_qkv_ref, flip_ref,
    )


def vmem(count):
    return [pl.BlockSpec(memory_space=pltpu.VMEM)] * count


def shape(dims, kind):
    return jax.ShapeDtypeStruct(dims, kind)


SCALARS = pl.BlockSpec(memory_space=pltpu.SMEM)


def forward_call(seq, tokens, feat, w_qkv, vec, rpe):
    rows, breadth = tokens.shape
    span = 2 * rows
    return pl.pallas_call(
        forward_kernel,
        out_shape=(
            shape((rows, 2 * breadth), F32), shape((rows, 2 * breadth), F32), shape((rows, 3 * breadth), LOW),
            shape((rows, breadth), F32), shape((rows, breadth), F32), shape((rows, breadth), LOW),
        ),
        in_specs=[SCALARS] + vmem(5),
        out_specs=tuple(vmem(6)),
        scratch_shapes=[
            pltpu.VMEM((rows, rows), F32), pltpu.VMEM((breadth // 256, 256, 256), LOW),
            pltpu.VMEM((256, 256), LOW), pltpu.VMEM((128, span), F32), pltpu.VMEM((rows, 128), LOW),
        ],
        compiler_params=pltpu.CompilerParams(vmem_limit_bytes=60 * MIB),
        name="attend",
    )(seq, tokens, feat, w_qkv, vec, rpe)


def middle_call(seq, tokens, cotangent, ctx_low, vec, w_out, w_up, w_down):
    rows, breadth = tokens.shape
    hidden = w_up.shape[1]
    return pl.pallas_call(
        middle_kernel,
        out_shape=(
            shape((rows, breadth), LOW), shape((rows, breadth), F32), shape((rows, breadth), F32),
            shape(w_out.shape, LOW), shape(w_up.shape, LOW), shape(w_down.shape, LOW), shape(vec.shape, F32),
        ),
        in_specs=[SCALARS] + vmem(7),
        out_specs=tuple(vmem(7)),
        scratch_shapes=[
            pltpu.VMEM((rows, breadth), F32), pltpu.VMEM((rows, breadth), F32), pltpu.VMEM((rows, breadth), LOW),
            pltpu.VMEM((rows, breadth), F32), pltpu.VMEM((rows, 128), F32), pltpu.VMEM((rows, hidden), LOW),
            pltpu.VMEM((rows, hidden), F32), pltpu.VMEM((rows, breadth), F32), pltpu.VMEM((rows, breadth), LOW),
            pltpu.VMEM((rows, hidden), LOW), pltpu.VMEM((breadth, rows), LOW),
        ],
        compiler_params=pltpu.CompilerParams(vmem_limit_bytes=60 * MIB),
        name="feed_forward",
    )(seq, tokens, cotangent, ctx_low, vec, w_out, w_up, w_down)


def backward_call(seq, tokens, feat, w_qkv, rpe, scaled, phi, low, den, ctx, g_ctx, g_hidden, vec):
    rows, breadth = tokens.shape
    span = 2 * rows
    return pl.pallas_call(
        backward_kernel,
        out_shape=(
            shape((rows, breadth), F32), shape(w_qkv.shape, LOW), shape(vec.shape, F32), shape(rpe.shape, F32),
        ),
        in_specs=[SCALARS] + vmem(11),
        out_specs=tuple(vmem(4)),
        scratch_shapes=[
            pltpu.VMEM((rows, rows), F32), pltpu.VMEM((breadth // 256, 256, 256), LOW),
            pltpu.VMEM((256, 256), LOW), pltpu.VMEM((128, span), F32), pltpu.VMEM((rows, 3 * breadth), F32),
            pltpu.VMEM((rows, 3 * breadth), LOW), pltpu.VMEM((rows, rows), LOW), pltpu.VMEM((rows, rows), LOW),
            pltpu.VMEM((128, span), F32), pltpu.VMEM((rows, 128), LOW), pltpu.VMEM((rows, 128), LOW),
            pltpu.VMEM((rows, 128), LOW), pltpu.VMEM((rows, 128), LOW), pltpu.VMEM((breadth, rows), LOW),
        ],
        compiler_params=pltpu.CompilerParams(vmem_limit_bytes=60 * MIB),
        name="attend_back",
    )(seq, tokens, feat, w_qkv, rpe, scaled, phi, low, den, ctx, g_ctx, g_hidden)


PIECE = 16
BLOCK_ROWS = 256


def place():
    me = lax.axis_index("dp")
    core = lax.rem(me, 2)
    x = lax.rem(me // 2, 2)
    y = lax.rem(me // 4, 2)
    z = me // 8
    first = x * (1 - core) + y * core
    second = y * (1 - core) + x * core
    return core, z, first, second


class Plane:
    def __init__(self, depth):
        self.depth = depth
        self.core, self.z, self.first, self.second = place()
        self.chip = self.at(self.z, self.first, self.second)
        self.sibling = self.chip * 2 + 1 - self.core
        self.over_first = self.device(self.z, 1 - self.first, self.second)
        self.over_second = self.device(self.z, self.first, 1 - self.second)

    def at(self, z, first, second):
        return 4 * z + first * (1 + self.core) + second * (2 - self.core)

    def device(self, z, first, second):
        return 2 * self.at(z, first, second) + self.core

    def spot(self, first, second):
        return first * (1 + self.core) + second * (2 - self.core)

    def ahead(self, distance):
        return lax.rem(self.z + distance, self.depth)

    def behind(self, distance):
        return lax.rem(self.z + self.depth - distance, self.depth)

    def greet(self):
        barrier = pltpu.get_barrier_semaphore()
        others = [self.sibling, self.over_first, self.over_second]
        others += [self.device(self.ahead(d), self.first, self.second) for d in range(1, self.depth)]
        for other in others:
            pl.semaphore_signal(barrier, inc=1, device_id=(other,), device_id_type=MESH)
        pl.semaphore_wait(barrier, len(others))


def remote(source, target, sems, item, slot, device):
    return pltpu.make_async_remote_copy(
        src_ref=source, dst_ref=target, send_sem=sems[0].at[item, slot], recv_sem=sems[1].at[item, slot],
        device_id=(device,), device_id_type=MESH,
    )


def each(count, step):
    def run(index, carry):
        step(index)
        return carry

    lax.fori_loop(0, count, run, 0)


def span(start, stop, step):
    def run(index, carry):
        step(index)
        return carry

    lax.fori_loop(start, stop, run, 0)


def half(ref, zs, spot, core):
    if len(ref.shape) == 5:
        return ref.at[zs, spot, core]
    breadth = ref.shape[3] // 2
    return ref.at[zs, spot, :, pl.ds(pl.multiple_of(core * breadth, 128), breadth)]


ALL = slice(None)


class Gather:
    def __init__(self, plane, full, sems):
        self.plane, self.full, self.sems = plane, full, sems
        self.here = plane.spot(plane.first, plane.second)
        self.across = plane.spot(1 - plane.first, plane.second)
        self.first_slot = plane.depth - 1
        self.second_slot = self.first_slot + 1
        self.core_slot = self.second_slot + 2

    def copy(self, item, zs, spot, slot, device, core=None):
        part = half(self.full[item], zs, spot, self.plane.core if core is None else core)
        return remote(part, part, self.sems, item, slot, device)

    def to_depth(self, item, distance):
        plane = self.plane
        target = plane.device(plane.ahead(distance), plane.first, plane.second)
        return self.copy(item, plane.z, self.here, distance - 1, target)

    def to_first(self, item):
        return self.copy(item, ALL, self.here, self.first_slot, self.plane.over_first)

    def to_second(self, item, first):
        spot = self.plane.spot(first, self.plane.second)
        return self.copy(item, ALL, spot, self.second_slot + first, self.plane.over_second)

    def to_core(self, item, spot):
        return self.copy(item, ALL, spot, self.core_slot + spot, self.plane.sibling)

    def begin(self, item):
        for distance in range(1, self.plane.depth):
            self.to_depth(item, distance).start()

    def over_depth(self, item):
        plane = self.plane
        for distance in range(1, plane.depth):
            self.copy(item, plane.behind(distance), self.here, distance - 1, plane.sibling).wait_recv()
        self.to_first(item).start()
        self.to_second(item, plane.first).start()
        self.to_core(item, self.here).start()

    def over_first(self, item):
        plane = self.plane
        self.copy(item, ALL, self.across, self.first_slot, plane.over_first).wait_recv()
        self.to_second(item, 1 - plane.first).start()
        self.to_core(item, self.across).start()

    def over_second(self, item):
        plane = self.plane
        for first in (plane.first, 1 - plane.first):
            spot = plane.spot(first, 1 - plane.second)
            self.copy(item, ALL, spot, self.second_slot + first, plane.over_second).wait_recv()
            self.to_core(item, spot).start()

    def over_core(self, item):
        plane = self.plane
        for spot in range(4):
            self.copy(item, ALL, spot, self.core_slot + spot, plane.sibling, 1 - plane.core).wait_recv()

    def sent(self, item):
        plane = self.plane
        for distance in range(1, plane.depth):
            self.to_depth(item, distance).wait_send()
        self.to_first(item).wait_send()
        for first in range(2):
            self.to_second(item, first).wait_send()
        for spot in range(4):
            self.to_core(item, spot).wait_send()


def one_hot(length, breadth):
    factor = (1 << 20) // length + 1
    col = iota((128, breadth), 1)
    owner = lax.shift_right_logical(col * factor, 20)
    return jnp.where(iota((128, breadth), 0) == col - owner * length, 1.0, 0.0).astype(LOW)


def owned(devices, length, breadth):
    factor = (1 << 20) // length + 1
    col = iota((devices, breadth), 1)
    return lax.shift_right_logical(col * factor, 20) == iota((devices, breadth), 0)


def pack_small(piece_refs, small_ref):
    small_ref[...] = jnp.zeros_like(small_ref)
    for row, piece in enumerate(piece_refs[:-1]):
        small_ref[row : row + 1, 0 : piece.shape[1]] = piece[...].astype(LOW).astype(F32)
    table = piece_refs[-1]
    for part in range(table.shape[0] // 128):
        row = len(piece_refs) - 1 + part
        value = table[128 * part : 128 * part + 128].reshape(1, 128)
        small_ref[row : row + 1, :] = value.astype(LOW).astype(F32)


def unpack_small(all_ref, lengths, table_rows, vec_ref, rpe_ref):
    devices = all_ref.shape[0] // PIECE
    vec_ref[...] = jnp.zeros_like(vec_ref)
    for row, length in enumerate(lengths):
        breadth = length * devices
        picked = all_ref[pl.ds(row, devices, stride=PIECE), :].astype(LOW)
        spread = jnp.where(owned(devices, length, breadth), mm(picked, one_hot(length, breadth)), 0.0)
        vec_ref[row : row + 1, 0:breadth] = column_sum(spread)
    for part in range(table_rows):
        rpe_ref[pl.ds(part, devices, stride=table_rows), :] = all_ref[
            pl.ds(len(lengths) + part, devices, stride=PIECE), :
        ]


ANYWHERE = pl.BlockSpec(memory_space=pl.ANY)


class Saver:
    def __init__(self, sources, targets, sems):
        self.copies = [
            pltpu.make_async_copy(source, target, sems.at[index])
            for index, (source, target) in enumerate(zip(sources, targets))
        ]

    def start(self, *indices):
        for index in indices:
            self.copies[index].start()

    def finish(self):
        for copy in self.copies:
            copy.wait()


def norm_forward(tokens_ref, wide_ref, vec_ref, xhat_ref, inverse_ref, normed_ref, normed_low_ref):
    rows, breadth = tokens_ref.shape
    gain, bias = vec_ref[3:4, :breadth], vec_ref[4:5, :breadth]

    def step(index):
        at = pl.ds(pl.multiple_of(index * 128, 128), 128)
        xhat, inverse = norm(tokens_ref[at, :].astype(F32) + wide_ref[at, :])
        xhat_ref[at, :] = xhat
        inverse_ref[at, :] = jnp.broadcast_to(inverse, (128, 128))
        normed = xhat * gain + bias
        normed_ref[at, :] = normed
        normed_low_ref[at, :] = normed.astype(LOW)

    each(rows // 128, step)


def norm_result(seq_ref, normed_ref, wide_ref, vec_ref, cot_ref, out_ref, g_sum_ref, gvec_ref):
    rows, breadth = normed_ref.shape
    gain, bias = vec_ref[6:7, :breadth], vec_ref[7:8, :breadth]
    valid_rows = seq_ref[0, 0] + seq_ref[0, 1]
    gvec_ref[...] = jnp.zeros_like(gvec_ref)

    def step(index):
        at = pl.ds(pl.multiple_of(index * 128, 128), 128)
        xhat, inverse = norm(normed_ref[at, :] + wide_ref[at, :])
        out_ref[at, :] = (xhat * gain + bias).astype(LOW)
        spot = iota((128, breadth), 0) + index * 128
        grad = jnp.where(spot < valid_rows, cot_ref[at, :].astype(F32), 0.0)
        add_to(gvec_ref, 6, column_sum(grad * xhat))
        add_to(gvec_ref, 7, column_sum(grad))
        g_sum = norm_back(grad, xhat, inverse, gain)
        add_to(gvec_ref, 5, column_sum(g_sum))
        g_sum_ref[at, :] = g_sum

    each(rows // 128, step)


def attend_pair(pair, q_at, k_at, v_at, low_ref, rpe_ref, mask_ref, den_ref, ctx_ref, ctx_low_ref, coef_ref, key_ref, score_ref, serve):
    rows = mask_ref.shape[0]
    tall = BLOCK_ROWS
    lower = iota((tall, 128), 1) < 64
    here = cols(pair, 128)
    for side in range(2):
        serve(pair, side)
        coefficients(rpe_ref, pair * 2 + side, coef_ref)
        keep_half(low_ref, k_at, key_ref, side)
        for block in range(rows // tall):
            at = slice(block * tall, block * tall + tall)
            kernel = mm(low_ref[at, q_at], key_ref[...], 1, 1)
            totals = []
            for part in range(tall // 128):
                start = block * tall + part * 128
                lead = rows - 128 - start
                weight = coef_ref[:, lead : lead + rows] * mask_ref[start : start + 128, :]
                scores = kernel[part * 128 : part * 128 + 128] * weight
                totals.append(jnp.sum(scores, axis=1, keepdims=True))
                score_ref[start : start + 128, :] = scores.astype(LOW)
            total = jnp.broadcast_to(jnp.concatenate(totals, axis=0), (tall, 128))
            context = mm(score_ref[at, :], low_ref[:, v_at]) * (1.0 / total)
            if side == 0:
                den_ref[at, here] = total
                ctx_ref[at, here] = context
            else:
                den_ref[at, here] = jnp.where(lower, den_ref[at, here], total)
                context = jnp.where(lower, ctx_ref[at, here], context)
                ctx_ref[at, here] = context
                ctx_low_ref[at, here] = context.astype(LOW)


def upward_tile(normed_low_ref, w, bias, act_ref, slope_ref, where):
    upward = mm(normed_low_ref[...], w[...]) + bias
    phi = 0.5 + 0.5 * lax.erf(upward * 0.5**0.5)
    density = jnp.exp(-0.5 * upward * upward) * 0.3989422804014327
    act_ref[:, where] = (upward * phi).astype(LOW)
    slope_ref[:, where] = phi + upward * density


def build_stack(feat_ref, stack_ref):
    tile = stack_ref.shape[2]
    head_size = feat_ref.shape[1]
    group = tile // head_size
    bits = head_size.bit_length() - 1
    same = lax.shift_right_logical(iota((tile, tile), 0), bits) == lax.shift_right_logical(iota((tile, tile), 1), bits)
    half = jnp.where(same, -0.5, 0.0).astype(LOW)
    for index in range(stack_ref.shape[0]):
        rows_of = []
        for inner in range(group):
            piece = feat_ref[index * group + inner].astype(F32)
            rows_of.append(jnp.concatenate([piece] * group, axis=1))
        full = jnp.where(same, jnp.concatenate(rows_of, axis=0), 0.0).astype(LOW)
        for part, value in enumerate((full, full, half, half)):
            stack_ref[index, part * tile : part * tile + tile, :] = value


def two_parts(value):
    high = value.astype(LOW)
    return [high, (value - high.astype(F32)).astype(LOW)]


def segment_mask(seq_ref, mask_ref):
    rows = mask_ref.shape[0]
    first_end = seq_ref[0, 0]
    second_end = first_end + seq_ref[0, 1]

    def segment(place):
        return (place >= first_end).astype(jnp.int32) + (place >= second_end).astype(jnp.int32)

    across = segment(iota((128, rows), 1))
    for start in range(0, rows, 128):
        down = segment(iota((128, rows), 0) + start)
        mask_ref[start : start + 128, :] = jnp.where(down == across, 1.0, 0.0)


def ahead_kernel(depth, pieces, *refs):
    seq_ref, tokens_ref, cot_ref, feat_ref, refs = refs[0], refs[1], refs[2], refs[3], refs[4:]
    matrices, refs = refs[:4], refs[4:]
    piece_refs, refs = refs[:pieces], refs[pieces:]
    out_ref, gvec_ref, vec_ref, rpe_ref, wide_ref, refs = refs[:5] + (refs[5:],)
    weights_hbm, kept_hbm, refs = refs[:4], refs[4:15], refs[15:]
    w_qkv, w_out, w_up, w_down, refs = refs[:4] + (refs[4:],)
    kept, refs = refs[:11], refs[11:]
    peers, refs = refs[:4], refs[4:]
    small_ref, all_ref, mask_ref, stack_ref, coef_ref, key_ref, score_ref, normed_ref = refs[:8]
    send, recv, peer_send, peer_recv, save_sem = refs[8:]
    scaled_ref, phi_ref, low_ref, den_ref, ctx_ref, ctx_low_ref = kept[:6]
    normed_low_ref, xhat_ref, inverse_ref, act_ref, slope_ref = kept[6:]
    rows, breadth = tokens_ref.shape
    groups, tile = w_qkv.shape[0], stack_ref.shape[2]
    up_tile, down_tile = w_up.shape[4], w_down.shape[4]

    plane = Plane(depth)
    core = plane.core
    pack_small(piece_refs, small_ref)
    thirds = range(groups)
    full = [all_ref] + [w_qkv.at[g] for g in thirds] + [w_out]
    full += [w_up.at[g] for g in thirds] + [w_down.at[g] for g in thirds]
    gather = Gather(plane, full, (send, recv))
    all_ref[plane.z, gather.here, core] = small_ref[...]
    plane.greet()
    swaps = [
        remote(matrix, peer, (peer_send, peer_recv), 0, index, plane.sibling)
        for index, (matrix, peer) in enumerate(zip(matrices, peers))
    ]
    for swap in swaps:
        swap.start()

    def assemble(item, matrix, starts, breadth_of):
        mine, other = matrices[matrix], peers[matrix]
        offset = core * (len(starts) * breadth_of)
        for number, start in enumerate(starts):
            at = pl.ds(pl.multiple_of(start, 128), breadth_of)
            own, peer = mine[:, at], other[:, at]
            both = jnp.concatenate([jnp.where(core == 0, own, peer), jnp.where(core == 0, peer, own)], axis=0)
            to = pl.ds(pl.multiple_of(offset + number * breadth_of, 128), breadth_of)
            full[item][plane.z, gather.here, :, to] = both.astype(LOW)

    def assemble_qkv(group):
        starts = []
        for number in range(3):
            place_of = 3 * core + number
            starts.append((place_of // 2) * breadth + group * tile + lax.rem(place_of, 2) * 128)
        assemble(1 + group, 0, starts, 128)

    flat_qkv = w_qkv.reshape(groups, breadth, 3 * tile)
    flat_out = w_out.reshape(breadth, breadth)
    flat_up = w_up.reshape(groups, breadth, up_tile)
    flat_down = w_down.reshape(groups, w_down.shape[1] * w_down.shape[2] * w_down.shape[3], down_tile)
    sources = [flat_qkv.at[g] for g in thirds] + [flat_out] + [flat_up.at[g] for g in thirds]
    sources += [flat_down.at[g] for g in thirds]
    targets = [weights_hbm[0].at[g] for g in thirds] + [weights_hbm[1]]
    targets += [weights_hbm[2].at[:, g * up_tile : g * up_tile + up_tile] for g in thirds]
    targets += [weights_hbm[3].at[:, g * down_tile : g * down_tile + down_tile] for g in thirds]
    saver = Saver(sources + list(kept), targets + list(kept_hbm), save_sem)
    first_kept = len(targets)

    def keep(*indices):
        saver.start(*[first_kept + index for index in indices])

    begin, along, first, second = gather.begin, gather.over_depth, gather.over_first, gather.over_second

    def whole(item):
        gather.over_core(item)
        if item:
            saver.start(item - 1)

    plan = {
        ("head", 1): ((second, 2), (along, 5)),
        ("head", 3): ((first, 4), (begin, 8), (whole, 2), (along, 6), (begin, 7)),
        ("project", 1): ((first, 5), (second, 3)),
        ("head", 5): ((second, 4),),
        ("project", 2): (
            (along, 7), (second, 5), (whole, 3), (begin, 9), (first, 6), (along, 8), (first, 7), (whole, 4),
        ),
        ("head", 8): ((whole, 5), (second, 6), (first, 8), (begin, 10)),
        ("head", 11): ((along, 9), (second, 7)),
        ("up", 0): ((second, 8), (first, 9), (whole, 6)),
        ("up", 2): ((first, 10), (whole, 8)),
        ("down", 0): ((second, 9),),
        ("down", 1): ((whole, 9), (second, 10)),
        ("down", 2): ((whole, 10),),
    }

    def serve(kind, index):
        for (work, number), steps in plan.items():
            if work == kind:

                @pl.when(index == number)
                def _(steps=steps):
                    for step, item in steps:
                        step(item)

    begin(0)
    swaps[0].wait_recv()
    assemble_qkv(0)
    begin(1)
    assemble_qkv(1)
    assemble_qkv(2)
    for swap in swaps[1:]:
        swap.wait_recv()
    assemble(4, 1, [core * (breadth // 2)], breadth // 2)
    for group in thirds:
        assemble(5 + group, 2, [group * up_tile + core * (up_tile // 2)], up_tile // 2)
        assemble(8 + group, 3, [group * down_tile + core * (down_tile // 2)], down_tile // 2)
    along(0)
    begin(2)
    segment_mask(seq_ref, mask_ref)
    first(0)
    along(1)
    second(0)
    along(2)
    begin(3)
    whole(0)
    begin(4)
    build_stack(feat_ref, stack_ref)
    first(1)
    along(3)
    first(2)
    begin(5)
    second(1)
    lengths = [piece.shape[1] for piece in piece_refs[:-1]]
    flat_all = all_ref.reshape(8 * depth * PIECE, 128)
    unpack_small(flat_all, lengths, piece_refs[-1].shape[0] // 128, vec_ref, rpe_ref)
    along(4)
    begin(6)
    whole(1)
    first(3)
    scale = 64 ** (-0.25)

    def serve_pair(pair, side):
        for (work, number), steps in plan.items():
            if work == "head" and number % 2 == side:

                @pl.when(pair == number // 2)
                def _(steps=steps):
                    for step, item in steps:
                        step(item)

    def group_step(group):
        serve("project", group)
        wide_ref[...] = mm(tokens_ref[...], flat_qkv[group])
        for part in range(3):
            where = pl.ds(pl.multiple_of(part * breadth + group * tile, tile), tile)
            value = wide_ref[:, part * tile : part * tile + tile] + vec_ref[0:1, where]
            if part < 2:
                scaled = value * scale
                scaled_ref[:, where] = scaled
                operand = jnp.concatenate(two_parts(scaled) + two_parts(scaled * scaled), axis=1)
                value = jnp.exp(mm(operand, stack_ref[group])) * 0.125
                phi_ref[:, where] = value
            low_ref[:, where] = value.astype(LOW)

        def pair_step(inner):
            pair = 2 * group + inner
            attend_pair(
                pair, cols(pair, 128), pl.ds(pl.multiple_of(pair * 128 + breadth, 128), 128),
                pl.ds(pl.multiple_of(pair * 128 + 2 * breadth, 128), 128),
                low_ref, rpe_ref, mask_ref, den_ref, ctx_ref, ctx_low_ref, coef_ref, key_ref, score_ref, serve_pair,
            )

        each(2, pair_step)

    each(groups, group_step)
    keep(0, 1, 2, 3, 4, 5)
    along(10)
    whole(7)
    wide_ref[...] = mm(ctx_low_ref[...], flat_out[...]) + vec_ref[2:3, :breadth]
    norm_forward(tokens_ref, wide_ref, vec_ref, xhat_ref, inverse_ref, normed_ref, normed_low_ref)
    keep(6, 7, 8)

    def upward_step(index):
        serve("up", index)
        where = cols(index, up_tile)
        upward_tile(normed_low_ref, flat_up.at[index], vec_ref[1:2, where], act_ref, slope_ref, where)

    each(groups, upward_step)
    keep(9, 10)

    def downward_step(index):
        serve("down", index)
        where = cols(index, down_tile)
        wide_ref[:, where] = mm(act_ref[...], flat_down[index]) + vec_ref[5:6, where]

    each(groups, downward_step)
    norm_result(seq_ref, normed_ref, wide_ref, vec_ref, cot_ref, out_ref, wide_ref, gvec_ref)
    for item in range(len(full)):
        gather.sent(item)
    for swap in swaps:
        swap.wait_send()
    saver.finish()


def ahead_call(depth, seq, tokens, cotangent, feat, matrices, pieces):
    rows, breadth = tokens.shape
    span_length = 2 * rows
    devices = 8 * depth
    groups, tile = 3, 256
    slots = depth - 1 + 1 + 2 + 4
    longest = max(piece.shape[1] for piece in pieces[:-1]) * devices
    table = pieces[-1].shape[0] * devices // 128
    w_qkv, w_out, w_up, w_down = matrices
    hidden = w_up.shape[1]
    lead = (depth, 4)
    full = [
        (groups,) + lead + (2 * w_qkv.shape[0], 3 * tile), lead + (2 * w_out.shape[0], breadth),
        (groups,) + lead + (2 * w_up.shape[0], hidden // groups),
        (groups,) + lead + (2 * w_down.shape[0], breadth // groups),
    ]
    saved = [(groups, breadth, 3 * tile), (breadth, breadth), (devices * w_up.shape[0], hidden), (devices * w_down.shape[0], breadth)]
    kept = [
        ((rows, 2 * breadth), F32), ((rows, 2 * breadth), F32), ((rows, 3 * breadth), LOW),
        ((rows, breadth), F32), ((rows, breadth), F32), ((rows, breadth), LOW),
        ((rows, breadth), LOW), ((rows, breadth), F32), ((rows, 128), F32), ((rows, hidden), LOW),
        ((rows, hidden), F32),
    ]
    items = 2 + 3 * groups
    return pl.pallas_call(
        functools.partial(ahead_kernel, depth, len(pieces)),
        out_shape=(
            shape((rows, breadth), LOW), shape((len(pieces) - 1, longest), F32),
            shape((len(pieces) - 1, longest), F32), shape((table, 128), F32), shape((rows, breadth), F32),
        )
        + tuple(shape(dims, LOW) for dims in saved)
        + tuple(shape(dims, kind) for dims, kind in kept),
        in_specs=[SCALARS] + vmem(3 + len(matrices) + len(pieces)),
        out_specs=tuple(vmem(5)) + (ANYWHERE,) * len(saved + kept),
        scratch_shapes=[pltpu.VMEM(dims, LOW) for dims in full]
        + [pltpu.VMEM(dims, kind) for dims, kind in kept]
        + [pltpu.VMEM(matrix.shape, F32) for matrix in matrices]
        + [
            pltpu.VMEM((PIECE, 128), F32), pltpu.VMEM((depth, 4, 2, PIECE, 128), F32),
            pltpu.VMEM((rows, rows), F32), pltpu.VMEM((groups, 4 * tile, tile), LOW),
            pltpu.VMEM((128, span_length), F32), pltpu.VMEM((rows, 128), LOW), pltpu.VMEM((rows, rows), LOW),
            pltpu.VMEM((rows, breadth), F32),
            pltpu.SemaphoreType.DMA((items, slots)), pltpu.SemaphoreType.DMA((items, slots)),
            pltpu.SemaphoreType.DMA((1, 4)), pltpu.SemaphoreType.DMA((1, 4)), pltpu.SemaphoreType.DMA((items - 1 + len(kept),)),
        ],
        compiler_params=pltpu.CompilerParams(
            collective_id=0, has_side_effects=True, vmem_limit_bytes=60 * MIB
        ),
        name="ahead",
    )(seq, tokens, cotangent, feat, *matrices, *pieces)


def prepare_back(group, slot, low_ref, den_ref, ctx_ref, g_ctx_ref, swap_ref, ext_ref, key_ref, val_ref, num_ref, flip_ref):
    rows = g_ctx_ref.shape[0]
    breadth = swap_ref.shape[0]
    where = cols(group, breadth)
    lane = jnp.bitwise_and(iota((128, breadth), 1), 127)
    lower = lane < 64

    def step(index):
        at = pl.ds(pl.multiple_of(index * 128, 128), 128)
        g_num = g_ctx_ref[at, where] * (1.0 / den_ref[slot, at, :])
        g_den = -mm2(g_num * ctx_ref[slot, at, :], swap_ref[...])
        high = g_den.astype(LOW).astype(F32)
        rest = g_den - high
        key = low_ref[slot, 1, at, :].astype(F32)
        value = low_ref[slot, 2, at, :].astype(F32)
        for side in range(2):
            mine = jnp.logical_not(lower) if side else lower
            other = 0 if side else 64
            is_high, is_rest = lane == other, lane == other + 1
            extended = jnp.where(mine, g_num, jnp.where(is_high, high, jnp.where(is_rest, rest, 0.0)))
            ext_ref[side, at, :] = extended.astype(LOW)
            key_ref[side, at, :] = jnp.where(mine, key, 0.0).astype(LOW)
            ones = jnp.where(jnp.logical_or(is_high, is_rest), 1.0, 0.0)
            val_ref[side, at, :] = jnp.where(mine, value, ones).astype(LOW)
        num_ref[at, :] = g_num.astype(LOW)

    each(rows // 128, step)
    flip_ref[0] = jnp.transpose(low_ref[slot, 0])
    flip_ref[1] = jnp.transpose(num_ref[...])


def attend_back_pair(
    pair, inner, slot, low_ref, rpe_ref, mask_ref, g_feat_ref, grpe_ref, coef_ref, scores_ref, gk_ref, diag_ref,
    ext_ref, key_ref, val_ref, flip_ref, turn_ref, serve,
):
    rows = mask_ref.shape[0]
    tall = BLOCK_ROWS
    here = cols(inner, 128)
    lower = iota((tall, 128), 1) < 64
    for side in range(2):
        serve(pair, side)
        coefficients(rpe_ref, pair * 2 + side, coef_ref)
        diag_ref[...] = jnp.zeros_like(diag_ref)
        for block in range(rows // tall):
            at = slice(block * tall, block * tall + tall)
            kernel = mm(low_ref[slot, 0, at, here], key_ref[side, :, here], 1, 1)
            g_scores = mm(ext_ref[side, at, here], val_ref[side, :, here], 1, 1)
            for part in range(tall // 128):
                start = block * tall + part * 128
                lead = rows - 128 - start
                inside = slice(part * 128, part * 128 + 128)
                weight = coef_ref[:, lead : lead + rows] * mask_ref[start : start + 128, :]
                scores = kernel[inside] * weight
                diag_ref[:, lead : lead + rows] += g_scores[inside] * scores
                scores_ref[start : start + 128, :] = scores.astype(LOW)
                gk_ref[start : start + 128, :] = (g_scores[inside] * weight).astype(LOW)
            g_query = mm(gk_ref[at, :], low_ref[slot, 1, :, here])
            if side:
                g_query = jnp.where(lower, g_feat_ref[at, here], g_query)
            g_feat_ref[at, here] = g_query
        head_rows = pl.ds(pl.multiple_of(inner * 128 + side * 64, 64), 64)
        turn_ref[0, head_rows, :] = mm(flip_ref[0, head_rows, :], gk_ref[...])
        turn_ref[1, head_rows, :] = mm(flip_ref[1, head_rows, :], scores_ref[...])
        diagonals(diag_ref, grpe_ref, pair * 2 + side)


def diagonals(diag_ref, out_ref, head):
    flip = jnp.where(iota((128, 128), 0) + iota((128, 128), 1) == 127, 1.0, 0.0).astype(LOW)
    value = diag_ref[...]
    high = value.astype(LOW)
    rest = (value - high.astype(F32)).astype(LOW)
    value = pltpu.roll(mm(flip, high) + mm(flip, rest), 0, axis=1, stride=1, stride_axis=0)
    sums = jnp.sum(value, axis=0, keepdims=True)
    for k in range(8):
        out_ref[pl.ds(head * 8 + 7 - k, 1), :] = sums[:, 128 * k : 128 * k + 128]


class Item:
    def __init__(self, given, buffers, row):
        self.given = given
        self.from_core, self.from_second, self.from_first, self.from_depth, self.leaving = buffers
        self.row = row


class Scatter:
    def __init__(self, plane, sems):
        self.plane, self.sems = plane, sems
        self.here = plane.spot(plane.first, plane.second)
        self.across = plane.spot(1 - plane.first, plane.second)
        self.first_slot = plane.depth - 1
        self.second_slot = self.first_slot + 1
        self.core_slot = self.second_slot + 2
        self.last_slot = self.core_slot + 1

    def with_core(self, item):
        return remote(
            half(item.given, ALL, ALL, 1 - self.plane.core), item.from_core, self.sems, item.row, self.core_slot,
            self.plane.sibling,
        )

    def begin(self, item):
        self.with_core(item).start()

    def to_second(self, item, first):
        spot = self.plane.spot(first, 1 - self.plane.second)
        return remote(
            half(item.given, ALL, spot, self.plane.core), item.from_second.at[first], self.sems, item.row,
            self.second_slot + first, self.plane.over_second,
        )

    def to_first(self, item):
        return remote(
            half(item.given, ALL, self.across, self.plane.core), item.from_first, self.sems, item.row,
            self.first_slot, self.plane.over_first,
        )

    def to_depth(self, item, distance):
        plane = self.plane
        z = plane.ahead(distance)
        return remote(
            half(item.given, z, self.here, plane.core), item.from_depth.at[distance - 1], self.sems, item.row,
            distance - 1, plane.device(z, plane.first, plane.second),
        )

    def join(self, item, spot, piece):
        def step(z):
            target = half(item.given, z, spot, self.plane.core)
            target[...] = target[...] + piece(z)

        each(self.plane.depth, step)

    def core(self, item):
        plane = self.plane
        self.with_core(item).wait_recv()
        for first in range(2):
            spot = plane.spot(first, 1 - plane.second)
            self.join(item, spot, lambda z, spot=spot: item.from_core[z, spot])
            self.to_second(item, first).start()
        for first in range(2):
            spot = plane.spot(first, plane.second)
            self.join(item, spot, lambda z, spot=spot: item.from_core[z, spot])

    def second(self, item):
        plane = self.plane
        away = 1 - plane.first
        self.to_second(item, away).wait_recv()
        self.join(item, self.across, lambda z: item.from_second[away, z])
        self.to_first(item).start()
        self.to_second(item, plane.first).wait_recv()
        self.join(item, self.here, lambda z: item.from_second[plane.first, z])

    def first(self, item):
        self.to_first(item).wait_recv()
        self.join(item, self.here, lambda z: item.from_first[z])
        for distance in range(1, self.plane.depth):
            self.to_depth(item, distance).start()

    def summed(self, item):
        plane = self.plane
        for distance in range(1, plane.depth):
            self.to_depth(item, distance).wait_recv()
        value = half(item.given, plane.z, self.here, plane.core)[...].astype(F32)
        for distance in range(1, plane.depth):
            value = value + item.from_depth[distance - 1].astype(F32)
        return value

    def columns(self, item, core):
        breadth = item.leaving.shape[1]
        return pl.ds(pl.multiple_of(core * breadth, 128), breadth)

    def last(self, item, target):
        core = self.plane.core
        return remote(
            item.leaving, target.at[:, self.columns(item, core)], self.sems, item.row, self.last_slot,
            self.plane.sibling,
        )

    def along(self, item, target):
        core = self.plane.core
        value = self.summed(item)
        height = value.shape[0] // 2
        upper, lower = value[:height], value[height:]
        target[:, self.columns(item, core)] = jnp.where(core == 0, upper, lower)
        item.leaving[...] = jnp.where(core == 0, lower, upper)
        self.last(item, target).start()

    def sent(self, item, target=None):
        self.with_core(item).wait_send()
        for first in range(2):
            self.to_second(item, first).wait_send()
        self.to_first(item).wait_send()
        for distance in range(1, self.plane.depth):
            self.to_depth(item, distance).wait_send()
        if target is not None:
            core = self.plane.core
            self.last(item, target).wait_send()
            arrived = target.at[:, self.columns(item, 1 - core)]
            remote(
                item.leaving, arrived, self.sems, item.row, self.last_slot, self.plane.sibling
            ).wait_recv()


def pack_grads(gvec_ref, lengths, grpe_ref, flat_ref):
    devices = flat_ref.shape[0] // PIECE
    table_rows = grpe_ref.shape[0] // devices
    flat_ref[...] = jnp.zeros_like(flat_ref)
    for row, length in enumerate(lengths):
        breadth = length * devices
        value = gvec_ref[row : row + 1, 0:breadth]
        spread = jnp.where(owned(devices, length, breadth), jnp.broadcast_to(value, (devices, breadth)), 0.0)
        flat_ref[pl.ds(row, devices, stride=PIECE), :] = mm2(spread, one_hot(length, breadth), 1)
    for part in range(table_rows):
        flat_ref[pl.ds(len(lengths) + part, devices, stride=PIECE), :] = grpe_ref[
            pl.ds(part, devices, stride=table_rows), :
        ]


def build_back(feat_ref, stack_ref):
    tile = stack_ref.shape[2]
    head_size = feat_ref.shape[1]
    group = tile // head_size
    bits = head_size.bit_length() - 1
    same = lax.shift_right_logical(iota((tile, tile), 0), bits) == lax.shift_right_logical(iota((tile, tile), 1), bits)
    last = stack_ref.shape[0] - 1
    for index in range(last):
        rows_of = []
        for inner in range(group):
            piece = jnp.transpose(feat_ref[index * group + inner].astype(F32))
            rows_of.append(jnp.concatenate([piece] * group, axis=1))
        full = jnp.where(same, jnp.concatenate(rows_of, axis=0), 0.0).astype(LOW)
        for part in range(2):
            stack_ref[index, part * tile : part * tile + tile, :] = full
    for part in range(2):
        stack_ref[last, part * tile : part * tile + tile, :] = jnp.where(same, 1.0, 0.0).astype(LOW)


def build_swap(swap_ref):
    tile = swap_ref.shape[0]
    down = lax.shift_right_logical(iota((tile, tile), 0), 6)
    across = lax.shift_right_logical(iota((tile, tile), 1), 6)
    swap_ref[...] = jnp.where(jnp.bitwise_xor(down, 1) == across, 1.0, 0.0).astype(LOW)


def behind_kernel(depth, lengths, *refs):
    seq_ref, feat_ref, vec_ref, rpe_ref, gvec_in_ref, g_sum_ref, refs = refs[:6] + (refs[6:],)
    w_qkv_hbm, w_out_hbm, w_up_hbm, w_down_hbm, refs = refs[:4] + (refs[4:],)
    scaled_hbm, phi_hbm, low_hbm, den_hbm, ctx_hbm, ctx_low_hbm, refs = refs[:6] + (refs[6:],)
    normed_low_hbm, xhat_hbm, inverse_hbm, act_hbm, slope_hbm, tokens_hbm, refs = refs[:6] + (refs[6:],)
    g_tokens_hbm, s_qkv, s_out, s_up, s_down, s_small, refs = refs[:6] + (refs[6:],)
    d_qkv, d_out, d_up, d_down, d_small, refs = refs[:5] + (refs[5:],)
    buffers, refs = [refs[5 * index : 5 * index + 5] for index in range(5)], refs[25:]
    g_hidden_ref, g_ctx_ref, g_low_ref, gvec_ref, grpe_ref, g_qkv_ref, refs = refs[:6] + (refs[6:],)
    send, recv, load_sem = refs
    rows, breadth = g_sum_ref.shape
    hidden = w_up_hbm.shape[1]
    tile, height = 256, 128
    wide = min(768, breadth)
    plane = Plane(depth)
    scatter = Scatter(plane, (send, recv))
    down, up, out = [
        Item(given, buffers[index], 2 - index)
        for given, index in ((d_down, 2), (d_up, 1), (d_out, 0))
    ]
    small = Item(d_small, buffers[4], 3)
    flat_down, flat_up, flat_out, flat_qkv = d_down.reshape(hidden, breadth), d_up.reshape(breadth, hidden), (
        d_out.reshape(breadth, breadth)
    ), d_qkv.reshape(breadth // tile, breadth, 3 * tile)
    flat_small = d_small.reshape(8 * depth * PIECE, 128)

    def qkv(group):
        return Item(d_qkv.at[group], [buffer.at[group] for buffer in buffers[3]], 4 + group)

    def load(source, target, index):
        return pltpu.make_async_copy(source, target, load_sem.at[index])

    def feed_forward(
        w_out_ref, w_up_ref, w_down_ref, act_ref, slope_ref, normed_low_ref, flip_ref,
        inverse_ref, ctx_low_ref,
    ):
        chunk = slope_ref.shape[2]
        chunks = hidden // chunk
        pending = {}

        def columns(index):
            return slice(index * chunk, index * chunk + chunk)

        acts = [
            load(act_hbm.at[:, columns(index)], act_ref.at[:, columns(index)], 2 * chunks + index)
            for index in range(chunks)
        ]

        def fetch(index):
            at = columns(index)
            pending[index] = [
                load(w_down_hbm.at[at, :], w_down_ref.at[at, :], 2 * index),
                load(slope_hbm.at[:, at], slope_ref.at[index % 2], 2 * index + 1),
            ]
            for copy in pending[index]:
                copy.start()

        for copy in acts:
            copy.start()
        fetch(0)
        fetch(1)
        base = 3 * chunks
        later = [
            load(normed_low_hbm, normed_low_ref, base), load(w_up_hbm, w_up_ref, base + 1),
            load(xhat_hbm, g_hidden_ref, base + 2), load(inverse_hbm, inverse_ref, base + 3),
            load(w_out_hbm, w_out_ref, base + 4), load(ctx_low_hbm, ctx_low_ref, base + 5),
        ]
        g_low_ref[...] = g_sum_ref[...].astype(LOW)
        gvec_ref[...] = gvec_in_ref[...]
        plane.greet()
        for index in range(chunks):
            acts[index].wait()

            at = columns(index)
            flat_down[at, :] = mm(act_ref[:, at], g_low_ref[...], 0, 0).astype(LOW)
        scatter.begin(down)
        for index in range(chunks):
            for copy in pending[index]:
                copy.wait()
            if index == 2:
                scatter.core(down)

            at = columns(index)
            g_upward = mm(g_low_ref[...], w_down_ref[at, :], 1, 1) * slope_ref[index % 2]
            gvec_ref[1:2, at] = column_sum(g_upward)
            act_ref[:, at] = g_upward.astype(LOW)
            if index + 2 < chunks:
                fetch(index + 2)
            if index == 0:
                for copy in later:
                    copy.start()
        for copy in later:
            copy.wait()
        flip_ref[...] = jnp.transpose(normed_low_ref[...])

        def up_step(step):
            where = cols(step, wide)
            flat_up[:, where] = mm(flip_ref[...], act_ref[:, where]).astype(LOW)

        each(hidden // wide, up_step)
        scatter.begin(up)

        g_sum_ref[...] = mm(act_ref[...], w_up_ref[...], 1, 1) + g_sum_ref[...]
        gain_one = vec_ref[3:4, :breadth]

        def first_back(step):
            at = pl.ds(pl.multiple_of(step * height, height), height)
            g_normed = g_sum_ref[at, :]
            xhat = g_hidden_ref[at, :]
            add_to(gvec_ref, 3, column_sum(g_normed * xhat))
            add_to(gvec_ref, 4, column_sum(g_normed))
            g_hidden = norm_back(g_normed, xhat, inverse_ref[at, 0:1], gain_one)
            add_to(gvec_ref, 2, column_sum(g_hidden))
            g_hidden_ref[at, :] = g_hidden
            g_low_ref[at, :] = g_hidden.astype(LOW)

        each(rows // height, first_back)

        flat_out[...] = mm(ctx_low_ref[...], g_low_ref[...], 0, 0).astype(LOW)
        scatter.begin(out)
        scatter.core(up)
        scatter.second(down)
        g_ctx_ref[...] = mm(g_low_ref[...], w_out_ref[...], 1, 1)

    chunk = min(768, hidden)
    pl.run_scoped(
        feed_forward,
        pltpu.VMEM(w_out_hbm.shape, LOW), pltpu.VMEM(w_up_hbm.shape, LOW), pltpu.VMEM(w_down_hbm.shape, LOW),
        pltpu.VMEM((rows, hidden), LOW), pltpu.VMEM((2, rows, chunk), F32),
        pltpu.VMEM((rows, breadth), LOW), pltpu.VMEM((breadth, rows), LOW),
        pltpu.VMEM((rows, 128), F32), pltpu.VMEM((rows, breadth), LOW),
    )

    calls = {
        4: (lambda: scatter.core(out), lambda: scatter.first(down)),
        7: (lambda: scatter.second(up),),
        9: (lambda: scatter.core(qkv(0)), lambda: scatter.first(up)),
        11: (lambda: scatter.second(out), lambda: scatter.core(qkv(1))),
    }

    def serve(pair, side):
        for head, steps in calls.items():
            if head % 2 == side:

                @pl.when(pair == head // 2)
                def _(steps=steps):
                    for step in steps:
                        step()

    def attention(
        w_qkv_ref, flip_ref, scaled_ref, phi_ref, low_ref, den_ref, ctx_ref, g_feat_ref, coef_ref,
        scores_ref, gk_ref, diag_ref, ext_ref, key_ref, val_ref, num_ref, turn_low_ref, turn_ref, swap_ref, mask_ref, stack_ref,
    ):
        groups = breadth // tile

        def part(ref, at, number):
            return ref.at[:, pl.ds(pl.multiple_of(at * tile + number * breadth, tile), tile)]

        def loads(group):
            slot = lax.rem(group, 2)
            copies = []
            for number in range(3):
                copies.append((part(low_hbm, group, number), low_ref.at[slot, number]))
            copies.append((part(den_hbm, group, 0), den_ref.at[slot]))
            copies.append((part(ctx_hbm, group, 0), ctx_ref.at[slot]))
            for number in range(2):
                copies.append((part(scaled_hbm, group, number), scaled_ref.at[slot, number]))
                copies.append((part(phi_hbm, group, number), phi_ref.at[slot, number]))
            return [
                load(source, target, slot * 9 + index) for index, (source, target) in enumerate(copies)
            ]

        base = 18
        tokens_copy = load(tokens_hbm, g_low_ref, base)

        def weights(group):
            return load(w_qkv_hbm.at[group], w_qkv_ref.at[group % 2], base + 1 + group)

        for copy in loads(0):
            copy.start()
        for copy in (tokens_copy, weights(0), weights(1)):
            copy.start()
        segment_mask(seq_ref, mask_ref)
        build_back(feat_ref, stack_ref)
        tokens_copy.wait()
        flip_ref[...] = jnp.transpose(g_low_ref[...])
        build_swap(swap_ref)
        scale = 64 ** (-0.25)

        def group_step(group):
            slot = lax.rem(group, 2)
            for copy in loads(group):
                copy.wait()

            @pl.when(group + 1 < groups)
            def _():
                for copy in loads(group + 1):
                    copy.start()

            prepare_back(
                group, slot, low_ref, den_ref, ctx_ref, g_ctx_ref, swap_ref, ext_ref, key_ref, val_ref, num_ref,
                turn_low_ref,
            )

            def pair_step(inner):
                pair = 2 * group + inner
                attend_back_pair(
                    pair, inner, slot, low_ref, rpe_ref, mask_ref, g_feat_ref, grpe_ref, coef_ref, scores_ref,
                    gk_ref, diag_ref, ext_ref, key_ref, val_ref, turn_low_ref, turn_ref, serve,
                )

            each(2, pair_step)

            g_feat_ref[:, tile : 2 * tile] = jnp.transpose(turn_ref[0])
            g_feat_ref[:, 2 * tile : 3 * tile] = jnp.transpose(turn_ref[1])
            for number in range(3):
                at = slice(number * tile, number * tile + tile)
                where = pl.ds(pl.multiple_of(group * tile + number * breadth, tile), tile)
                grad = g_feat_ref[:, at]
                if number < 2:
                    upward = jnp.concatenate(two_parts(grad * phi_ref[slot, number]), axis=1)
                    total = mm(upward, stack_ref[groups])
                    grad = mm(upward, stack_ref[group]) - scaled_ref[slot, number] * total
                    grad = grad * scale
                gvec_ref[0:1, where] = column_sum(grad)
                g_qkv_ref[group, :, at] = grad.astype(LOW)
            flat_qkv[group] = mm(flip_ref[...], g_qkv_ref[group]).astype(LOW)
            scatter.begin(qkv(group))

        each(groups, group_step)
        scatter.second(qkv(0))
        scatter.core(qkv(2))
        scatter.along(down, s_down)
        scatter.first(out)
        scatter.first(qkv(0))
        flip = jnp.where(iota((128, 128), 0) + iota((128, 128), 1) == 127, 1.0, 0.0).astype(LOW)
        grpe_ref[...] = mm2(grpe_ref[...], flip)
        pack_grads(gvec_ref, lengths, grpe_ref, flat_small)
        scatter.begin(small)
        scatter.second(qkv(1))

        def inputs(group):
            weights(group).wait()
            g_hidden_ref[...] += mm(g_qkv_ref[group], w_qkv_ref[group % 2], 1, 1)
            if group + 2 < groups:
                weights(group + 2).start()

        inputs(0)
        inputs(1)
        scatter.core(small)
        inputs(2)

    pl.run_scoped(
        attention,
        pltpu.VMEM((2,) + w_qkv_hbm.shape[1:], LOW), pltpu.VMEM((breadth, rows), LOW),
        pltpu.VMEM((2, 2, rows, tile), F32), pltpu.VMEM((2, 2, rows, tile), F32),
        pltpu.VMEM((2, 3, rows, tile), LOW), pltpu.VMEM((2, rows, tile), F32), pltpu.VMEM((2, rows, tile), F32),
        pltpu.VMEM((rows, 3 * tile), F32), pltpu.VMEM((128, 2 * rows), F32), pltpu.VMEM((rows, rows), LOW),
        pltpu.VMEM((rows, rows), LOW), pltpu.VMEM((128, 2 * rows), F32), pltpu.VMEM((2, rows, tile), LOW),
        pltpu.VMEM((2, rows, tile), LOW), pltpu.VMEM((2, rows, tile), LOW), pltpu.VMEM((rows, tile), LOW),
        pltpu.VMEM((2, tile, rows), LOW), pltpu.VMEM((2, tile, rows), F32), pltpu.VMEM((tile, tile), LOW),
        pltpu.VMEM((rows, rows), F32), pltpu.VMEM((breadth // tile + 1, 2 * tile, tile), LOW),
    )
    result = load(g_hidden_ref, g_tokens_hbm, 31)
    result.start()
    scatter.second(qkv(2))
    scatter.first(qkv(1))
    scatter.second(small)
    scatter.along(out, s_out)
    scatter.along(up, s_up)
    scatter.first(small)
    scatter.first(qkv(2))
    scatter.along(qkv(1), s_qkv.at[1])
    scatter.along(qkv(0), s_qkv.at[0])
    scatter.along(qkv(2), s_qkv.at[2])
    s_small[...] = scatter.summed(small)
    for item, target in ((down, s_down), (up, s_up), (out, s_out), (small, None)):
        scatter.sent(item, target)
    for group in range(breadth // tile):
        scatter.sent(qkv(group), s_qkv.at[group])
    result.wait()


def behind_call(depth, seq, feat, vec, rpe, gvec, g_sum, weights, kept, tokens, lengths):
    rows, breadth = tokens.shape
    chips = 4 * depth
    devices = 2 * chips
    w_qkv, w_out, w_up, w_down = weights
    group = 3 * 256
    groups = w_qkv.shape[0]
    table = rpe.shape[0]
    blocks = [(w.shape[0] // devices, w.shape[1]) for w in (w_out, w_up, w_down)]
    lead = (depth, 4)
    given = [lead + (2 * block[0], block[1]) for block in blocks]
    qkv_block = (w_qkv.shape[1] // devices, group)

    def buffers(block, kind, front=()):
        if kind == LOW:
            part, leaving = (2 * block[0], block[1] // 2), (block[0], block[1] // 2)
        else:
            part, leaving = block, (8, 128)
        numbers = [lead, (2, depth), (depth,), (depth - 1,)]
        return [pltpu.VMEM(front + number + part, kind) for number in numbers] + [pltpu.VMEM(front + leaving, F32)]

    slots = depth - 1 + 1 + 2 + 2
    scratch = [pltpu.VMEM((groups,) + lead + (2 * qkv_block[0], group), LOW)]
    scratch += [pltpu.VMEM(dims, LOW) for dims in given]
    scratch += [pltpu.VMEM(lead + (2, PIECE, 128), F32)]
    for block in blocks:
        scratch += buffers(block, LOW)
    scratch += buffers(qkv_block, LOW, (groups,)) + buffers((PIECE, 128), F32)
    scratch += [
        pltpu.VMEM((rows, breadth), F32), pltpu.VMEM((rows, breadth), F32), pltpu.VMEM((rows, breadth), LOW),
        pltpu.VMEM(vec.shape, F32), pltpu.VMEM((table, 128), F32), pltpu.VMEM((groups, rows, group), LOW),
        pltpu.SemaphoreType.DMA((7, slots)), pltpu.SemaphoreType.DMA((7, slots)), pltpu.SemaphoreType.DMA((32,)),
    ]
    return pl.pallas_call(
        functools.partial(behind_kernel, depth, lengths),
        out_shape=(
            shape((rows, breadth), F32), shape((groups,) + qkv_block, F32),
        ) + tuple(shape(block, F32) for block in blocks) + (shape((PIECE, 128), F32),),
        in_specs=[SCALARS] + vmem(5) + [ANYWHERE] * (4 + len(kept) + 1),
        out_specs=(ANYWHERE,) + tuple(vmem(5)),
        scratch_shapes=scratch,
        compiler_params=pltpu.CompilerParams(
            collective_id=1, has_side_effects=True, vmem_limit_bytes=62 * MIB
        ),
        name="behind",
    )(seq, feat, vec, rpe, gvec, g_sum, *weights, *kept, tokens)


def emit_kernel(count, lengths, *refs):
    big, small_hbm, refs = refs[:count], refs[count], refs[count + 1 :]
    outs, refs = refs[:count], refs[count:]
    number = len(lengths) + 1
    targets, refs = refs[:number], refs[number:]
    held, pieces, small, sems, piece_sems = refs[:count], refs[count : count + number], refs[-3], refs[-2], refs[-1]
    arrive = pltpu.make_async_copy(small_hbm, small, piece_sems.at[number])
    arrive.start()
    leave = [
        pltpu.make_async_copy(piece, target, piece_sems.at[index])
        for index, (piece, target) in enumerate(zip(pieces, targets))
    ]
    inward, owners = [], []
    for index in range(count):
        if len(big[index].shape) == 3:
            groups, _, breadth = big[index].shape
            tile = breadth // 3
            for group in range(groups):
                for part in range(3):
                    start = part * breadth + group * tile
                    source = big[index].at[group, :, part * tile : part * tile + tile]
                    inward.append((source, held[index].at[:, start : start + tile]))
                    owners.append(index)
        else:
            inward.append((big[index], held[index]))
            owners.append(index)
    inward = [
        pltpu.make_async_copy(source, target, sems.at[0, index]) for index, (source, target) in enumerate(inward)
    ]
    outward = [pltpu.make_async_copy(held[index], outs[index], sems.at[1, index]) for index in range(count)]
    for copy in inward:
        copy.start()
    arrive.wait()
    for row, length in enumerate(lengths):
        pieces[row][...] = small[row : row + 1, 0:length]
    table = pieces[-1]
    for part in range(table.shape[0] // 128):
        row = len(lengths) + part
        table[128 * part : 128 * part + 128] = small[row : row + 1, :].reshape(128)
    for copy in leave:
        copy.start()
    for index in range(count):
        for owner, copy in zip(owners, inward):
            if owner == index:
                copy.wait()
        outward[index].start()
    for copy in outward + leave:
        copy.wait()


def emit_call(arrays, small, lengths, table):
    shapes = [
        (array.shape[1], array.shape[0] * array.shape[2]) if len(array.shape) == 3 else array.shape for array in arrays
    ]
    result = pl.pallas_call(
        functools.partial(emit_kernel, len(arrays), lengths),
        out_shape=tuple(shape(dims, array.dtype) for dims, array in zip(shapes, arrays))
        + tuple(shape((1, length), F32) for length in lengths) + (shape((table,), F32),),
        in_specs=[ANYWHERE] * (len(arrays) + 1),
        out_specs=(ANYWHERE,) * (len(arrays) + len(lengths) + 1),
        scratch_shapes=[pltpu.VMEM(dims, array.dtype) for dims, array in zip(shapes, arrays)]
        + [pltpu.VMEM((1, length), F32) for length in lengths]
        + [
            pltpu.VMEM((table,), F32), pltpu.VMEM(small.shape, F32), pltpu.SemaphoreType.DMA((2, len(arrays) + 8)),
            pltpu.SemaphoreType.DMA((len(lengths) + 2,)),
        ],
        compiler_params=pltpu.CompilerParams(vmem_limit_bytes=60 * MIB),
        name="emit",
    )(*arrays, small)
    return result[: len(arrays)], [piece.reshape(-1) for piece in result[len(arrays) :]]


def plain_gather(value):
    return lax.all_gather(value.astype(LOW), "dp", axis=0, tiled=True)


def plain_scatter(value):
    return lax.psum_scatter(value.astype(F32), "dp", scatter_dimension=0, tiled=True)


def body(
    depth, tokens, cotangent, seq_lengths, random_feat, w_qkv, b_qkv, w_out, b_out, ln1_gain, ln1_bias,
    w_up, b_up, w_down, b_down, ln2_gain, ln2_bias, rpe_table,
):
    vectors = (b_qkv, b_up, b_out, ln1_gain, ln1_bias, b_down, ln2_gain, ln2_bias)
    matrices = (w_qkv, w_out, w_up, w_down)
    lengths = tuple(piece.shape[0] for piece in vectors)
    if depth:
        pieces = [piece.reshape(1, -1) for piece in vectors] + [rpe_table]
        result = ahead_call(depth, seq_lengths, tokens, cotangent, random_feat, matrices, pieces)
        out, gvec, vec, rpe = result[:4]
        g_sum, weights, kept = result[4], result[5:9], result[9:]
        g_tokens, s_qkv, s_out, s_up, s_down, small = behind_call(
            depth, seq_lengths, random_feat, vec, rpe, gvec, g_sum, weights, kept, tokens, lengths
        )
        arrays, pieces = emit_call(
            (out, g_tokens, s_qkv, s_out, s_up, s_down), small, lengths, rpe_table.shape[0]
        )
        out, g_tokens, s_qkv, s_out, s_up, s_down = arrays
    else:
        full_vectors = [plain_gather(piece).astype(F32) for piece in vectors]
        longest = max(piece.shape[0] for piece in full_vectors)
        vec = jnp.stack([jnp.pad(piece, (0, longest - piece.shape[0])) for piece in full_vectors])
        rpe = plain_gather(rpe_table).astype(F32).reshape(-1, 128)
        full_qkv, full_out, full_up, full_down = [plain_gather(piece) for piece in matrices]
        scaled, phi, low, den, ctx, ctx_low = forward_call(seq_lengths, tokens, random_feat, full_qkv, vec, rpe)
        out, g_hidden, g_ctx, d_out, d_up, d_down, gvec_one = middle_call(
            seq_lengths, tokens, cotangent, ctx_low, vec, full_out, full_up, full_down
        )
        g_tokens, d_qkv, gvec_two, grpe = backward_call(
            seq_lengths, tokens, random_feat, full_qkv, rpe, scaled, phi, low, den, ctx, g_ctx, g_hidden, vec
        )
        gvec = gvec_one + gvec_two
        s_qkv, s_out, s_up, s_down = [plain_scatter(grad) for grad in (d_qkv, d_out, d_up, d_down)]
        devices = lax.axis_size("dp")
        pieces = [plain_scatter(gvec[row, : length * devices]) for row, length in enumerate(lengths)]
        pieces.append(plain_scatter(grpe.reshape(-1)))
    p_qkv, p_up, p_out, p_gain_one, p_bias_one, p_down, p_gain_two, p_bias_two, p_rpe = pieces
    return (
        out, g_tokens, s_qkv, p_qkv, s_out, p_out, p_gain_one, p_bias_one, s_up, p_up, s_down, p_down,
        p_gain_two, p_bias_two, p_rpe,
    )


def solution(mesh):
    wide, flat = P("dp", None), P("dp")
    devices = mesh.shape["dp"]
    depth = devices // 8 if devices == 32 else 0
    in_specs = (
        wide, wide, wide, P(), wide, flat, wide, flat, flat, flat, wide, flat, wide, flat, flat, flat, flat,
    )
    out_specs = (
        wide, wide, wide, flat, wide, flat, flat, flat, wide, flat, wide, flat, flat, flat, flat,
    )
    return jax.shard_map(
        functools.partial(body, depth), mesh=mesh, in_specs=in_specs, out_specs=out_specs, check_vma=False
    )
```

```python
import functools

import jax
import jax.numpy as jnp
from jax import lax
from jax.experimental import pallas as pl
from jax.experimental.pallas import tpu as pltpu
from jax.sharding import PartitionSpec as P

EPSILON = 1e-05
F32 = jnp.float32
LOW = jnp.bfloat16
MESH = pl.DeviceIdType.MESH
MIB = 2**20


def mm(first_op, second_op, first_dim=1, second_dim=0):
    return lax.dot_general(
        first_op,
        second_op,
        (((first_dim,), (second_dim,)), ((), ())),
        preferred_element_type=F32,
    )


def mm2(value, weight, weight_dim=0):
    high = value.astype(LOW)
    rest = (value - high.astype(F32)).astype(LOW)
    return mm(high, weight, 1, weight_dim) + mm(rest, weight, 1, weight_dim)


def iota(shape, dim):
    return lax.broadcasted_iota(jnp.int32, shape, dim)


def cols(index, width):
    return pl.ds(pl.multiple_of(index * width, width), width)


def build_tables(seq_ref, feat_ref, mask_ref, block_ref, ones_ref):
    rows = mask_ref.shape[0]
    first_end = seq_ref[0, 0]
    second_end = first_end + seq_ref[0, 1]

    def segment(place):
        return (place >= first_end).astype(jnp.int32) + (place >= second_end).astype(jnp.int32)

    across = segment(iota((128, rows), 1))
    for start in range(0, rows, 128):
        down = segment(iota((128, rows), 0) + start)
        mask_ref[start : start + 128, :] = jnp.where(down == across, 1.0, 0.0)
    head_size = feat_ref.shape[1]
    breadth = ones_ref.shape[0]
    group = breadth // head_size
    bits = head_size.bit_length() - 1
    owner_row = lax.shift_right_logical(iota((breadth, breadth), 0), bits)
    owner_col = lax.shift_right_logical(iota((breadth, breadth), 1), bits)
    same = owner_row == owner_col
    ones_ref[...] = jnp.where(same, 1.0, 0.0).astype(LOW)
    for index in range(feat_ref.shape[0] // group):
        rows_of = []
        for inner in range(group):
            piece = feat_ref[index * group + inner].astype(F32)
            rows_of.append(jnp.concatenate([piece] * group, axis=1))
        full = jnp.concatenate(rows_of, axis=0)
        block_ref[index] = jnp.where(same, full, 0.0).astype(LOW)


def project(tokens_ref, w_ref, vec_ref, scaled_ref, phi_ref, low_ref, block_ref, ones_ref):
    breadth = tokens_ref.shape[1]
    tile = ones_ref.shape[0]
    per_part = breadth // tile
    scale = 64 ** (-0.25)

    def features(step, carry):
        where = cols(step, tile)
        acc = mm(tokens_ref[...], w_ref[:, where]) + vec_ref[0:1, where]
        scaled = acc * scale
        scaled_ref[:, where] = scaled
        block = block_ref[lax.rem(step, per_part)]
        mapped = mm2(scaled, block)
        squared = mm2(scaled * scaled, ones_ref[...])
        phi = jnp.exp(mapped - 0.5 * squared) * 0.125
        phi_ref[:, where] = phi
        low_ref[:, where] = phi.astype(LOW)
        return carry

    lax.fori_loop(0, 2 * per_part, features, 0)

    def plain(step, carry):
        where = cols(step + 2 * per_part, tile)
        acc = mm(tokens_ref[...], w_ref[:, where]) + vec_ref[0:1, where]
        low_ref[:, where] = acc.astype(LOW)
        return carry

    lax.fori_loop(0, per_part, plain, 0)


def coefficients(rpe_ref, head, coef_ref):
    flip = (iota((128, 128), 0) + iota((128, 128), 1) == 127).astype(F32).astype(LOW)
    raw = rpe_ref[pl.ds(pl.multiple_of(head * 8, 8), 8), :].astype(LOW)
    table = jnp.exp(mm(raw, flip))
    wide = jnp.concatenate(
        [jnp.broadcast_to(table[7 - k : 8 - k, :], (128, 128)) for k in range(8)], axis=1
    )
    coef_ref[...] = pltpu.roll(wide, 1024 - 127, axis=1, stride=1, stride_axis=0)


def attend(low_ref, rpe_ref, mask_ref, den_ref, ctx_ref, ctx_low_ref, coef_ref, key_ref):
    rows, breadth = ctx_ref.shape

    def pair_step(pair, carry):
        q_at = cols(pair, 128)
        k_at = pl.ds(pl.multiple_of(pair * 128 + breadth, 128), 128)
        v_at = pl.ds(pl.multiple_of(pair * 128 + 2 * breadth, 128), 128)
        lane = iota((128, 128), 1)
        for side in range(2):
            coefficients(rpe_ref, pair * 2 + side, coef_ref)
            mine = lane >= 64 if side else lane < 64
            keep_half(low_ref, k_at, key_ref, side)
            for block in range(rows // 128):
                at = slice(block * 128, block * 128 + 128)
                kernel = mm(low_ref[at, q_at], key_ref[...], 1, 1)
                lead = 128 * (rows // 128 - 1 - block)
                scores = kernel * (coef_ref[:, lead : lead + rows] * mask_ref[at, :])
                total = jnp.sum(scores, axis=1, keepdims=True)
                context = mm(scores.astype(LOW), low_ref[:, v_at]) * (1.0 / total)
                total = jnp.broadcast_to(total, (128, 128))
                if side == 0:
                    den_ref[at, q_at] = total
                    ctx_ref[at, q_at] = context
                else:
                    den_ref[at, q_at] = jnp.where(mine, total, den_ref[at, q_at])
                    context = jnp.where(mine, context, ctx_ref[at, q_at])
                    ctx_ref[at, q_at] = context
                    ctx_low_ref[at, q_at] = context.astype(LOW)
        return carry

    lax.fori_loop(0, breadth // 128, pair_step, 0)


def keep_half(low_ref, where, out_ref, side):
    rows = low_ref.shape[0]
    lane = iota((rows, 128), 1)
    mine = lane >= 64 if side else lane < 64
    out_ref[...] = jnp.where(mine, low_ref[:, where].astype(F32), 0.0).astype(LOW)


def forward_kernel(
    seq_ref, tokens_ref, feat_ref, w_ref, vec_ref, rpe_ref,
    scaled_ref, phi_ref, low_ref, den_ref, ctx_ref, ctx_low_ref,
    mask_ref, block_ref, ones_ref, coef_ref, key_ref,
):
    build_tables(seq_ref, feat_ref, mask_ref, block_ref, ones_ref)
    project(tokens_ref, w_ref, vec_ref, scaled_ref, phi_ref, low_ref, block_ref, ones_ref)
    attend(low_ref, rpe_ref, mask_ref, den_ref, ctx_ref, ctx_low_ref, coef_ref, key_ref)


def norm(value):
    centred = value - jnp.mean(value, axis=-1, keepdims=True)
    inverse = lax.rsqrt(jnp.mean(centred * centred, axis=-1, keepdims=True) + EPSILON)
    return centred * inverse, inverse


def norm_back(grad, xhat, inverse, gain):
    scaled = grad * gain
    mean = jnp.mean(scaled, axis=-1, keepdims=True)
    along = jnp.mean(scaled * xhat, axis=-1, keepdims=True)
    return inverse * (scaled - mean - xhat * along)


def add_to(ref, row, value):
    ref[row : row + 1, 0 : value.shape[1]] += value


def column_sum(value):
    return jnp.sum(value, axis=0, keepdims=True)


def middle_kernel(
    seq_ref, tokens_ref, cot_ref, ctx_low_ref, vec_ref, w_out_ref, w_up_ref, w_down_ref,
    out_ref, g_hidden_ref, g_ctx_ref, d_out_ref, d_up_ref, d_down_ref, gvec_ref,
    wide_ref, normed_ref, normed_low_ref, xhat_ref, inverse_ref, act_ref, slope_ref, g_sum_ref,
    g_low_ref, g_up_ref, flip_ref,
):
    rows, breadth = tokens_ref.shape
    hidden = w_up_ref.shape[1]
    height, tile = 128, 256
    blocks, tiles = rows // height, breadth // tile
    valid_rows = seq_ref[0, 0] + seq_ref[0, 1]
    gvec_ref[...] = jnp.zeros_like(gvec_ref)
    gain_one, bias_one = vec_ref[3:4, :breadth], vec_ref[4:5, :breadth]
    gain_two, bias_two = vec_ref[6:7, :breadth], vec_ref[7:8, :breadth]

    def rows_at(step):
        return pl.ds(pl.multiple_of(step * height, height), height)

    def loop(count, step):
        def run(index, carry):
            step(index)
            return carry

        lax.fori_loop(0, count, run, 0)

    def attended_step(step):
        where = cols(step, tile)
        wide_ref[:, where] = mm(ctx_low_ref[...], w_out_ref[:, where]) + vec_ref[2:3, where]

    loop(tiles, attended_step)

    def first_norm(step):
        at = rows_at(step)
        xhat, inverse = norm(tokens_ref[at, :].astype(F32) + wide_ref[at, :])
        xhat_ref[at, :] = xhat
        inverse_ref[at, :] = jnp.broadcast_to(inverse, (height, 128))
        normed = xhat * gain_one + bias_one
        normed_ref[at, :] = normed
        normed_low_ref[at, :] = normed.astype(LOW)

    loop(blocks, first_norm)

    def upward_step(step):
        where = cols(step, tile)
        upward = mm(normed_low_ref[...], w_up_ref[:, where]) + vec_ref[1:2, where]
        phi = 0.5 + 0.5 * lax.erf(upward * 0.5**0.5)
        density = jnp.exp(-0.5 * upward * upward) * 0.3989422804014327
        act_ref[:, where] = (upward * phi).astype(LOW)
        slope_ref[:, where] = phi + upward * density

    loop(hidden // tile, upward_step)

    def downward_step(step):
        where = cols(step, tile)
        wide_ref[:, where] = mm(act_ref[...], w_down_ref[:, where]) + vec_ref[5:6, where]

    loop(tiles, downward_step)

    def second_norm(step):
        at = rows_at(step)
        xhat, inverse = norm(normed_ref[at, :] + wide_ref[at, :])
        out_ref[at, :] = (xhat * gain_two + bias_two).astype(LOW)
        place = iota((height, breadth), 0) + step * height
        grad = jnp.where(place < valid_rows, cot_ref[at, :].astype(F32), 0.0)
        add_to(gvec_ref, 6, column_sum(grad * xhat))
        add_to(gvec_ref, 7, column_sum(grad))
        g_sum = norm_back(grad, xhat, inverse, gain_two)
        add_to(gvec_ref, 5, column_sum(g_sum))
        g_sum_ref[at, :] = g_sum
        g_low_ref[at, :] = g_sum.astype(LOW)

    loop(blocks, second_norm)
    flip_ref[...] = jnp.transpose(normed_low_ref[...])

    def down_step(step):
        where = cols(step, tile)
        g_upward = mm(g_low_ref[...], w_down_ref[where, :], 1, 1) * slope_ref[:, where]
        gvec_ref[1:2, where] = column_sum(g_upward)
        g_upward = g_upward.astype(LOW)
        g_up_ref[:, where] = g_upward
        d_down_ref[where, :] = mm(act_ref[:, where], g_low_ref[...], 0, 0).astype(LOW)
        d_up_ref[:, where] = mm(flip_ref[...], g_upward).astype(LOW)

    loop(hidden // tile, down_step)

    def up_back(step):
        where = cols(step, tile)
        wide_ref[:, where] = mm(g_up_ref[...], w_up_ref[where, :], 1, 1) + g_sum_ref[:, where]

    loop(tiles, up_back)

    def first_back(step):
        at = rows_at(step)
        g_normed = wide_ref[at, :]
        xhat = xhat_ref[at, :]
        add_to(gvec_ref, 3, column_sum(g_normed * xhat))
        add_to(gvec_ref, 4, column_sum(g_normed))
        g_hidden = norm_back(g_normed, xhat, inverse_ref[at, 0:1], gain_one)
        add_to(gvec_ref, 2, column_sum(g_hidden))
        g_hidden_ref[at, :] = g_hidden
        g_low_ref[at, :] = g_hidden.astype(LOW)

    loop(blocks, first_back)

    def out_back(step):
        where = cols(step, tile)
        g_ctx_ref[:, where] = mm(g_low_ref[...], w_out_ref[where, :], 1, 1)
        d_out_ref[where, :] = mm(ctx_low_ref[:, where], g_low_ref[...], 0, 0).astype(LOW)

    loop(tiles, out_back)


def plain_diagonals(diag_ref, out_ref, head):
    value = diag_ref[...]
    height = value.shape[0]
    while height > 1:
        height //= 2
        value = value[height:] + pltpu.roll(value[:height], height, axis=1)
    for k in range(8):
        out_ref[pl.ds(head * 8 + 7 - k, 1), :] = value[:, 128 * k : 128 * k + 128]


def attend_back(
    low_ref, rpe_ref, mask_ref, den_ref, ctx_ref, g_ctx_ref,
    g_feat_ref, g_low_ref, gvec_ref, grpe_ref,
    coef_ref, scores_ref, gk_ref, diag_ref, query_ref, key_ref, value_ref, num_ref,
):
    rows, breadth = ctx_ref.shape

    def pair_step(pair, carry):
        q_at = cols(pair, 128)
        k_at = pl.ds(pl.multiple_of(pair * 128 + breadth, 128), 128)
        v_at = pl.ds(pl.multiple_of(pair * 128 + 2 * breadth, 128), 128)
        lane = iota((128, 128), 1)
        ones = jnp.ones((128, 128), LOW)
        for side in range(2):
            coefficients(rpe_ref, pair * 2 + side, coef_ref)
            mine = lane >= 64 if side else lane < 64
            other = 0 if side else 64
            keep_half(low_ref, q_at, query_ref, side)
            keep_half(low_ref, k_at, key_ref, side)
            keep_half(low_ref, v_at, value_ref, side)
            diag_ref[...] = jnp.zeros_like(diag_ref)
            is_high, is_rest = lane == other, lane == other + 1
            extra = jnp.where(jnp.logical_or(is_high, is_rest), 1.0, 0.0)
            for block in range(rows // 128):
                at = slice(block * 128, block * 128 + 128)
                value_ref[at, :] = (value_ref[at, :].astype(F32) + extra).astype(LOW)
            for block in range(rows // 128):
                at = slice(block * 128, block * 128 + 128)
                kernel = mm(low_ref[at, q_at], key_ref[...], 1, 1)
                g_num = jnp.where(mine, g_ctx_ref[at, q_at] * (1.0 / den_ref[at, q_at]), 0.0)
                g_den = -mm2(g_num * ctx_ref[at, q_at], ones)
                num_ref[at, :] = g_num.astype(LOW)
                high = g_den.astype(LOW).astype(F32)
                extended = jnp.where(is_high, high, jnp.where(is_rest, g_den - high, g_num))
                g_scores = mm(extended.astype(LOW), value_ref[...], 1, 1)
                lead = 128 * (rows // 128 - 1 - block)
                weight = coef_ref[:, lead : lead + rows] * mask_ref[at, :]
                scores = kernel * weight
                g_kernel = (g_scores * weight).astype(LOW)
                diag_ref[:, lead : lead + rows] += g_scores * scores
                scores_ref[at, :] = scores.astype(LOW)
                gk_ref[at, :] = g_kernel
                g_query = mm(g_kernel, key_ref[...])
                if side:
                    g_query = g_query + g_feat_ref[at, q_at]
                g_feat_ref[at, q_at] = g_query
            g_key = mm(gk_ref[...], query_ref[...], 0, 0)
            g_value = mm(scores_ref[...], num_ref[...], 0, 0)
            if side:
                g_key = g_key + g_feat_ref[:, k_at]
                g_value = g_value + g_feat_ref[:, v_at]
            g_feat_ref[:, k_at] = g_key
            g_feat_ref[:, v_at] = g_value
            plain_diagonals(diag_ref, grpe_ref, pair * 2 + side)
        g_value = g_feat_ref[:, v_at]
        gvec_ref[0:1, v_at] = column_sum(g_value)
        g_low_ref[:, v_at] = g_value.astype(LOW)
        return carry

    lax.fori_loop(0, breadth // 128, pair_step, 0)
    flip = (jnp.where(iota((128, 128), 0) + iota((128, 128), 1) == 127, 1.0, 0.0)).astype(LOW)
    grpe_ref[...] = mm2(grpe_ref[...], flip)


def project_back(
    tokens_ref, w_ref, g_hidden_ref, phi_ref, scaled_ref, block_ref, ones_ref,
    g_feat_ref, g_low_ref, gvec_ref, g_tokens_ref, d_qkv_ref, flip_ref,
):
    breadth = tokens_ref.shape[1]
    tile = ones_ref.shape[0]
    per_part = breadth // tile
    scale = 64 ** (-0.25)

    def features(step, carry):
        where = cols(step, tile)
        upward = g_feat_ref[:, where] * phi_ref[:, where]
        total = mm2(upward, ones_ref[...])
        grad = mm2(upward, block_ref[lax.rem(step, per_part)], 1) - scaled_ref[:, where] * total
        grad = grad * scale
        gvec_ref[0:1, where] = column_sum(grad)
        g_low_ref[:, where] = grad.astype(LOW)
        return carry

    lax.fori_loop(0, 2 * per_part, features, 0)
    flip_ref[...] = jnp.transpose(tokens_ref[...])

    def weights(step, carry):
        where = cols(step, tile)
        d_qkv_ref[:, where] = mm(flip_ref[...], g_low_ref[:, where]).astype(LOW)
        return carry

    lax.fori_loop(0, 3 * per_part, weights, 0)

    def inputs(step, carry):
        where = cols(step, tile)
        g_tokens_ref[:, where] = mm(g_low_ref[...], w_ref[where, :], 1, 1) + g_hidden_ref[:, where]
        return carry

    lax.fori_loop(0, per_part, inputs, 0)


def backward_kernel(
    seq_ref, tokens_ref, feat_ref, w_ref, rpe_ref, scaled_ref, phi_ref, low_ref, den_ref, ctx_ref,
    g_ctx_ref, g_hidden_ref,
    g_tokens_ref, d_qkv_ref, gvec_ref, grpe_ref,
    mask_ref, block_ref, ones_ref, coef_ref, g_feat_ref, g_low_ref, scores_ref, gk_ref, diag_ref,
    query_ref, key_ref, value_ref, num_ref, flip_ref,
):
    build_tables(seq_ref, feat_ref, mask_ref, block_ref, ones_ref)
    gvec_ref[...] = jnp.zeros_like(gvec_ref)
    attend_back(
        low_ref, rpe_ref, mask_ref, den_ref, ctx_ref, g_ctx_ref, g_feat_ref, g_low_ref, gvec_ref, grpe_ref,
        coef_ref, scores_ref, gk_ref, diag_ref, query_ref, key_ref, value_ref, num_ref,
    )
    project_back(
        tokens_ref, w_ref, g_hidden_ref, phi_ref, scaled_ref, block_ref, ones_ref,
        g_feat_ref, g_low_ref, gvec_ref, g_tokens_ref, d_qkv_ref, flip_ref,
    )


def vmem(count):
    return [pl.BlockSpec(memory_space=pltpu.VMEM)] * count


def shape(dims, kind):
    return jax.ShapeDtypeStruct(dims, kind)


SCALARS = pl.BlockSpec(memory_space=pltpu.SMEM)


def forward_call(seq, tokens, feat, w_qkv, vec, rpe):
    rows, breadth = tokens.shape
    span = 2 * rows
    return pl.pallas_call(
        forward_kernel,
        out_shape=(
            shape((rows, 2 * breadth), F32), shape((rows, 2 * breadth), F32), shape((rows, 3 * breadth), LOW),
            shape((rows, breadth), F32), shape((rows, breadth), F32), shape((rows, breadth), LOW),
        ),
        in_specs=[SCALARS] + vmem(5),
        out_specs=tuple(vmem(6)),
        scratch_shapes=[
            pltpu.VMEM((rows, rows), F32), pltpu.VMEM((breadth // 256, 256, 256), LOW),
            pltpu.VMEM((256, 256), LOW), pltpu.VMEM((128, span), F32), pltpu.VMEM((rows, 128), LOW),
        ],
        compiler_params=pltpu.CompilerParams(vmem_limit_bytes=60 * MIB),
        name="attend",
    )(seq, tokens, feat, w_qkv, vec, rpe)


def middle_call(seq, tokens, cotangent, ctx_low, vec, w_out, w_up, w_down):
    rows, breadth = tokens.shape
    hidden = w_up.shape[1]
    return pl.pallas_call(
        middle_kernel,
        out_shape=(
            shape((rows, breadth), LOW), shape((rows, breadth), F32), shape((rows, breadth), F32),
            shape(w_out.shape, LOW), shape(w_up.shape, LOW), shape(w_down.shape, LOW), shape(vec.shape, F32),
        ),
        in_specs=[SCALARS] + vmem(7),
        out_specs=tuple(vmem(7)),
        scratch_shapes=[
            pltpu.VMEM((rows, breadth), F32), pltpu.VMEM((rows, breadth), F32), pltpu.VMEM((rows, breadth), LOW),
            pltpu.VMEM((rows, breadth), F32), pltpu.VMEM((rows, 128), F32), pltpu.VMEM((rows, hidden), LOW),
            pltpu.VMEM((rows, hidden), F32), pltpu.VMEM((rows, breadth), F32), pltpu.VMEM((rows, breadth), LOW),
            pltpu.VMEM((rows, hidden), LOW), pltpu.VMEM((breadth, rows), LOW),
        ],
        compiler_params=pltpu.CompilerParams(vmem_limit_bytes=60 * MIB),
        name="feed_forward",
    )(seq, tokens, cotangent, ctx_low, vec, w_out, w_up, w_down)


def backward_call(seq, tokens, feat, w_qkv, rpe, scaled, phi, low, den, ctx, g_ctx, g_hidden, vec):
    rows, breadth = tokens.shape
    span = 2 * rows
    return pl.pallas_call(
        backward_kernel,
        out_shape=(
            shape((rows, breadth), F32), shape(w_qkv.shape, LOW), shape(vec.shape, F32), shape(rpe.shape, F32),
        ),
        in_specs=[SCALARS] + vmem(11),
        out_specs=tuple(vmem(4)),
        scratch_shapes=[
            pltpu.VMEM((rows, rows), F32), pltpu.VMEM((breadth // 256, 256, 256), LOW),
            pltpu.VMEM((256, 256), LOW), pltpu.VMEM((128, span), F32), pltpu.VMEM((rows, 3 * breadth), F32),
            pltpu.VMEM((rows, 3 * breadth), LOW), pltpu.VMEM((rows, rows), LOW), pltpu.VMEM((rows, rows), LOW),
            pltpu.VMEM((128, span), F32), pltpu.VMEM((rows, 128), LOW), pltpu.VMEM((rows, 128), LOW),
            pltpu.VMEM((rows, 128), LOW), pltpu.VMEM((rows, 128), LOW), pltpu.VMEM((breadth, rows), LOW),
        ],
        compiler_params=pltpu.CompilerParams(vmem_limit_bytes=60 * MIB),
        name="attend_back",
    )(seq, tokens, feat, w_qkv, rpe, scaled, phi, low, den, ctx, g_ctx, g_hidden)


PIECE = 16
BLOCK_ROWS = 256


def place():
    me = lax.axis_index("dp")
    core = lax.rem(me, 2)
    x = lax.rem(me // 2, 2)
    y = lax.rem(me // 4, 2)
    z = me // 8
    first = x * (1 - core) + y * core
    second = y * (1 - core) + x * core
    return core, z, first, second


class Plane:
    def __init__(self, depth):
        self.depth = depth
        self.core, self.z, self.first, self.second = place()
        self.chip = self.at(self.z, self.first, self.second)
        self.sibling = self.chip * 2 + 1 - self.core
        self.over_first = self.device(self.z, 1 - self.first, self.second)
        self.over_second = self.device(self.z, self.first, 1 - self.second)

    def at(self, z, first, second):
        return 4 * z + first * (1 + self.core) + second * (2 - self.core)

    def device(self, z, first, second):
        return 2 * self.at(z, first, second) + self.core

    def spot(self, first, second):
        return first * (1 + self.core) + second * (2 - self.core)

    def ahead(self, distance):
        return lax.rem(self.z + distance, self.depth)

    def behind(self, distance):
        return lax.rem(self.z + self.depth - distance, self.depth)

    def greet(self):
        barrier = pltpu.get_barrier_semaphore()
        others = [self.sibling, self.over_first, self.over_second]
        others += [self.device(self.ahead(d), self.first, self.second) for d in range(1, self.depth)]
        for other in others:
            pl.semaphore_signal(barrier, inc=1, device_id=(other,), device_id_type=MESH)
        pl.semaphore_wait(barrier, len(others))


def remote(source, target, sems, item, slot, device):
    return pltpu.make_async_remote_copy(
        src_ref=source, dst_ref=target, send_sem=sems[0].at[item, slot], recv_sem=sems[1].at[item, slot],
        device_id=(device,), device_id_type=MESH,
    )


def each(count, step):
    def run(index, carry):
        step(index)
        return carry

    lax.fori_loop(0, count, run, 0)


def span(start, stop, step):
    def run(index, carry):
        step(index)
        return carry

    lax.fori_loop(start, stop, run, 0)


def half(ref, zs, spot, core):
    if len(ref.shape) == 5:
        return ref.at[zs, spot, core]
    breadth = ref.shape[3] // 2
    return ref.at[zs, spot, :, pl.ds(pl.multiple_of(core * breadth, 128), breadth)]


ALL = slice(None)


class Gather:
    def __init__(self, plane, full, sems):
        self.plane, self.full, self.sems = plane, full, sems
        self.here = plane.spot(plane.first, plane.second)
        self.across = plane.spot(1 - plane.first, plane.second)
        self.first_slot = plane.depth - 1
        self.second_slot = self.first_slot + 1
        self.core_slot = self.second_slot + 2

    def copy(self, item, zs, spot, slot, device, core=None):
        part = half(self.full[item], zs, spot, self.plane.core if core is None else core)
        return remote(part, part, self.sems, item, slot, device)

    def to_depth(self, item, distance):
        plane = self.plane
        target = plane.device(plane.ahead(distance), plane.first, plane.second)
        return self.copy(item, plane.z, self.here, distance - 1, target)

    def to_first(self, item):
        return self.copy(item, ALL, self.here, self.first_slot, self.plane.over_first)

    def to_second(self, item, first):
        spot = self.plane.spot(first, self.plane.second)
        return self.copy(item, ALL, spot, self.second_slot + first, self.plane.over_second)

    def to_core(self, item, spot):
        return self.copy(item, ALL, spot, self.core_slot + spot, self.plane.sibling)

    def begin(self, item):
        for distance in range(1, self.plane.depth):
            self.to_depth(item, distance).start()

    def over_depth(self, item):
        plane = self.plane
        for distance in range(1, plane.depth):
            self.copy(item, plane.behind(distance), self.here, distance - 1, plane.sibling).wait_recv()
        self.to_first(item).start()
        self.to_second(item, plane.first).start()
        self.to_core(item, self.here).start()

    def over_first(self, item):
        plane = self.plane
        self.copy(item, ALL, self.across, self.first_slot, plane.over_first).wait_recv()
        self.to_second(item, 1 - plane.first).start()
        self.to_core(item, self.across).start()

    def over_second(self, item):
        plane = self.plane
        for first in (plane.first, 1 - plane.first):
            spot = plane.spot(first, 1 - plane.second)
            self.copy(item, ALL, spot, self.second_slot + first, plane.over_second).wait_recv()
            self.to_core(item, spot).start()

    def over_core(self, item):
        plane = self.plane
        for spot in range(4):
            self.copy(item, ALL, spot, self.core_slot + spot, plane.sibling, 1 - plane.core).wait_recv()

    def sent(self, item):
        plane = self.plane
        for distance in range(1, plane.depth):
            self.to_depth(item, distance).wait_send()
        self.to_first(item).wait_send()
        for first in range(2):
            self.to_second(item, first).wait_send()
        for spot in range(4):
            self.to_core(item, spot).wait_send()


def one_hot(length, breadth):
    factor = (1 << 20) // length + 1
    col = iota((128, breadth), 1)
    owner = lax.shift_right_logical(col * factor, 20)
    return jnp.where(iota((128, breadth), 0) == col - owner * length, 1.0, 0.0).astype(LOW)


def owned(devices, length, breadth):
    factor = (1 << 20) // length + 1
    col = iota((devices, breadth), 1)
    return lax.shift_right_logical(col * factor, 20) == iota((devices, breadth), 0)


def pack_small(piece_refs, small_ref):
    small_ref[...] = jnp.zeros_like(small_ref)
    for row, piece in enumerate(piece_refs[:-1]):
        small_ref[row : row + 1, 0 : piece.shape[1]] = piece[...].astype(LOW).astype(F32)
    table = piece_refs[-1]
    for part in range(table.shape[0] // 128):
        row = len(piece_refs) - 1 + part
        value = table[128 * part : 128 * part + 128].reshape(1, 128)
        small_ref[row : row + 1, :] = value.astype(LOW).astype(F32)


def unpack_small(all_ref, lengths, table_rows, vec_ref, rpe_ref):
    devices = all_ref.shape[0] // PIECE
    vec_ref[...] = jnp.zeros_like(vec_ref)
    for row, length in enumerate(lengths):
        breadth = length * devices
        picked = all_ref[pl.ds(row, devices, stride=PIECE), :].astype(LOW)
        spread = jnp.where(owned(devices, length, breadth), mm(picked, one_hot(length, breadth)), 0.0)
        vec_ref[row : row + 1, 0:breadth] = column_sum(spread)
    for part in range(table_rows):
        rpe_ref[pl.ds(part, devices, stride=table_rows), :] = all_ref[
            pl.ds(len(lengths) + part, devices, stride=PIECE), :
        ]


ANYWHERE = pl.BlockSpec(memory_space=pl.ANY)


class Saver:
    def __init__(self, sources, targets, sems):
        self.copies = [
            pltpu.make_async_copy(source, target, sems.at[index])
            for index, (source, target) in enumerate(zip(sources, targets))
        ]

    def start(self, *indices):
        for index in indices:
            self.copies[index].start()

    def finish(self):
        for copy in self.copies:
            copy.wait()


def norm_forward(tokens_ref, wide_ref, vec_ref, xhat_ref, inverse_ref, normed_ref, normed_low_ref):
    rows, breadth = tokens_ref.shape
    gain, bias = vec_ref[3:4, :breadth], vec_ref[4:5, :breadth]

    def step(index):
        at = pl.ds(pl.multiple_of(index * 128, 128), 128)
        xhat, inverse = norm(tokens_ref[at, :].astype(F32) + wide_ref[at, :])
        xhat_ref[at, :] = xhat
        inverse_ref[at, :] = jnp.broadcast_to(inverse, (128, 128))
        normed = xhat * gain + bias
        normed_ref[at, :] = normed
        normed_low_ref[at, :] = normed.astype(LOW)

    each(rows // 128, step)


def norm_result(seq_ref, normed_ref, wide_ref, vec_ref, cot_ref, out_ref, g_sum_ref, gvec_ref):
    rows, breadth = normed_ref.shape
    gain, bias = vec_ref[6:7, :breadth], vec_ref[7:8, :breadth]
    valid_rows = seq_ref[0, 0] + seq_ref[0, 1]
    gvec_ref[...] = jnp.zeros_like(gvec_ref)

    def step(index):
        at = pl.ds(pl.multiple_of(index * 128, 128), 128)
        xhat, inverse = norm(normed_ref[at, :] + wide_ref[at, :])
        out_ref[at, :] = (xhat * gain + bias).astype(LOW)
        spot = iota((128, breadth), 0) + index * 128
        grad = jnp.where(spot < valid_rows, cot_ref[at, :].astype(F32), 0.0)
        add_to(gvec_ref, 6, column_sum(grad * xhat))
        add_to(gvec_ref, 7, column_sum(grad))
        g_sum = norm_back(grad, xhat, inverse, gain)
        add_to(gvec_ref, 5, column_sum(g_sum))
        g_sum_ref[at, :] = g_sum

    each(rows // 128, step)


def attend_pair(pair, q_at, k_at, v_at, low_ref, rpe_ref, mask_ref, den_ref, ctx_ref, ctx_low_ref, coef_ref, key_ref, score_ref, serve):
    rows = mask_ref.shape[0]
    tall = BLOCK_ROWS
    lower = iota((tall, 128), 1) < 64
    here = cols(pair, 128)
    for side in range(2):
        serve(pair, side)
        coefficients(rpe_ref, pair * 2 + side, coef_ref)
        keep_half(low_ref, k_at, key_ref, side)
        for block in range(rows // tall):
            at = slice(block * tall, block * tall + tall)
            kernel = mm(low_ref[at, q_at], key_ref[...], 1, 1)
            totals = []
            for part in range(tall // 128):
                start = block * tall + part * 128
                lead = rows - 128 - start
                weight = coef_ref[:, lead : lead + rows] * mask_ref[start : start + 128, :]
                scores = kernel[part * 128 : part * 128 + 128] * weight
                totals.append(jnp.sum(scores, axis=1, keepdims=True))
                score_ref[start : start + 128, :] = scores.astype(LOW)
            total = jnp.broadcast_to(jnp.concatenate(totals, axis=0), (tall, 128))
            context = mm(score_ref[at, :], low_ref[:, v_at]) * (1.0 / total)
            if side == 0:
                den_ref[at, here] = total
                ctx_ref[at, here] = context
            else:
                den_ref[at, here] = jnp.where(lower, den_ref[at, here], total)
                context = jnp.where(lower, ctx_ref[at, here], context)
                ctx_ref[at, here] = context
                ctx_low_ref[at, here] = context.astype(LOW)


def upward_tile(normed_low_ref, w, bias, act_ref, slope_ref, where):
    upward = mm(normed_low_ref[...], w[...]) + bias
    phi = 0.5 + 0.5 * lax.erf(upward * 0.5**0.5)
    density = jnp.exp(-0.5 * upward * upward) * 0.3989422804014327
    act_ref[:, where] = (upward * phi).astype(LOW)
    slope_ref[:, where] = phi + upward * density


def build_stack(feat_ref, stack_ref):
    tile = stack_ref.shape[2]
    head_size = feat_ref.shape[1]
    group = tile // head_size
    bits = head_size.bit_length() - 1
    same = lax.shift_right_logical(iota((tile, tile), 0), bits) == lax.shift_right_logical(iota((tile, tile), 1), bits)
    half = jnp.where(same, -0.5, 0.0).astype(LOW)
    for index in range(stack_ref.shape[0]):
        rows_of = []
        for inner in range(group):
            piece = feat_ref[index * group + inner].astype(F32)
            rows_of.append(jnp.concatenate([piece] * group, axis=1))
        full = jnp.where(same, jnp.concatenate(rows_of, axis=0), 0.0).astype(LOW)
        for part, value in enumerate((full, full, half, half)):
            stack_ref[index, part * tile : part * tile + tile, :] = value


def two_parts(value):
    high = value.astype(LOW)
    return [high, (value - high.astype(F32)).astype(LOW)]


def segment_mask(seq_ref, mask_ref):
    rows = mask_ref.shape[0]
    first_end = seq_ref[0, 0]
    second_end = first_end + seq_ref[0, 1]

    def segment(place):
        return (place >= first_end).astype(jnp.int32) + (place >= second_end).astype(jnp.int32)

    across = segment(iota((128, rows), 1))
    for start in range(0, rows, 128):
        down = segment(iota((128, rows), 0) + start)
        mask_ref[start : start + 128, :] = jnp.where(down == across, 1.0, 0.0)


def ahead_kernel(depth, pieces, *refs):
    seq_ref, tokens_ref, cot_ref, feat_ref, refs = refs[0], refs[1], refs[2], refs[3], refs[4:]
    matrices, refs = refs[:4], refs[4:]
    piece_refs, refs = refs[:pieces], refs[pieces:]
    out_ref, gvec_ref, vec_ref, rpe_ref, wide_ref, refs = refs[:5] + (refs[5:],)
    weights_hbm, kept_hbm, refs = refs[:4], refs[4:15], refs[15:]
    w_qkv, w_out, w_up, w_down, refs = refs[:4] + (refs[4:],)
    kept, refs = refs[:11], refs[11:]
    peers, refs = refs[:4], refs[4:]
    small_ref, all_ref, mask_ref, stack_ref, coef_ref, key_ref, score_ref, normed_ref = refs[:8]
    send, recv, peer_send, peer_recv, save_sem = refs[8:]
    scaled_ref, phi_ref, low_ref, den_ref, ctx_ref, ctx_low_ref = kept[:6]
    normed_low_ref, xhat_ref, inverse_ref, act_ref, slope_ref = kept[6:]
    rows, breadth = tokens_ref.shape
    groups, tile = w_qkv.shape[0], stack_ref.shape[2]
    up_tile, down_tile = w_up.shape[4], w_down.shape[4]

    plane = Plane(depth)
    core = plane.core
    pack_small(piece_refs, small_ref)
    thirds = range(groups)
    full = [all_ref] + [w_qkv.at[g] for g in thirds] + [w_out]
    full += [w_up.at[g] for g in thirds] + [w_down.at[g] for g in thirds]
    gather = Gather(plane, full, (send, recv))
    all_ref[plane.z, gather.here, core] = small_ref[...]
    plane.greet()
    swaps = [
        remote(matrix, peer, (peer_send, peer_recv), 0, index, plane.sibling)
        for index, (matrix, peer) in enumerate(zip(matrices, peers))
    ]
    for swap in swaps:
        swap.start()

    def assemble(item, matrix, starts, breadth_of):
        mine, other = matrices[matrix], peers[matrix]
        offset = core * (len(starts) * breadth_of)
        for number, start in enumerate(starts):
            at = pl.ds(pl.multiple_of(start, 128), breadth_of)
            own, peer = mine[:, at], other[:, at]
            both = jnp.concatenate([jnp.where(core == 0, own, peer), jnp.where(core == 0, peer, own)], axis=0)
            to = pl.ds(pl.multiple_of(offset + number * breadth_of, 128), breadth_of)
            full[item][plane.z, gather.here, :, to] = both.astype(LOW)

    def assemble_qkv(group):
        starts = []
        for number in range(3):
            place_of = 3 * core + number
            starts.append((place_of // 2) * breadth + group * tile + lax.rem(place_of, 2) * 128)
        assemble(1 + group, 0, starts, 128)

    flat_qkv = w_qkv.reshape(groups, breadth, 3 * tile)
    flat_out = w_out.reshape(breadth, breadth)
    flat_up = w_up.reshape(groups, breadth, up_tile)
    flat_down = w_down.reshape(groups, w_down.shape[1] * w_down.shape[2] * w_down.shape[3], down_tile)
    sources = [flat_qkv.at[g] for g in thirds] + [flat_out] + [flat_up.at[g] for g in thirds]
    sources += [flat_down.at[g] for g in thirds]
    targets = [weights_hbm[0].at[g] for g in thirds] + [weights_hbm[1]]
    targets += [weights_hbm[2].at[:, g * up_tile : g * up_tile + up_tile] for g in thirds]
    targets += [weights_hbm[3].at[:, g * down_tile : g * down_tile + down_tile] for g in thirds]
    saver = Saver(sources + list(kept), targets + list(kept_hbm), save_sem)
    first_kept = len(targets)

    def keep(*indices):
        saver.start(*[first_kept + index for index in indices])

    begin, along, first, second = gather.begin, gather.over_depth, gather.over_first, gather.over_second

    def whole(item):
        gather.over_core(item)
        if item:
            saver.start(item - 1)

    plan = {
        ("head", 1): ((second, 2), (along, 5)),
        ("head", 3): ((first, 4), (begin, 8), (whole, 2), (along, 6), (begin, 7)),
        ("project", 1): ((first, 5), (second, 3)),
        ("head", 5): ((second, 4),),
        ("project", 2): (
            (along, 7), (second, 5), (whole, 3), (begin, 9), (first, 6), (along, 8), (first, 7), (whole, 4),
        ),
        ("head", 8): ((whole, 5), (second, 6), (first, 8), (begin, 10)),
        ("head", 11): ((along, 9), (second, 7)),
        ("up", 0): ((second, 8), (first, 9), (whole, 6)),
        ("up", 2): ((first, 10), (whole, 8)),
        ("down", 0): ((second, 9),) + tuple((gather.sent, item) for item in range(6)),
        ("down", 1): ((whole, 9), (second, 10), (gather.sent, 6), (gather.sent, 7)),
        ("down", 2): ((gather.sent, 8), (gather.sent, 9), (whole, 10)),
    }

    def serve(kind, index):
        for (work, number), steps in plan.items():
            if work == kind:

                @pl.when(index == number)
                def _(steps=steps):
                    for step, item in steps:
                        step(item)

    begin(0)
    swaps[0].wait_recv()
    assemble_qkv(0)
    begin(1)
    assemble_qkv(1)
    assemble_qkv(2)
    for swap in swaps[1:]:
        swap.wait_recv()
    for swap in swaps:
        swap.wait_send()
    assemble(4, 1, [core * (breadth // 2)], breadth // 2)
    for group in thirds:
        assemble(5 + group, 2, [group * up_tile + core * (up_tile // 2)], up_tile // 2)
        assemble(8 + group, 3, [group * down_tile + core * (down_tile // 2)], down_tile // 2)
    along(0)
    begin(2)
    segment_mask(seq_ref, mask_ref)
    first(0)
    along(1)
    second(0)
    along(2)
    begin(3)
    whole(0)
    begin(4)
    build_stack(feat_ref, stack_ref)
    first(1)
    along(3)
    first(2)
    begin(5)
    second(1)
    lengths = [piece.shape[1] for piece in piece_refs[:-1]]
    flat_all = all_ref.reshape(8 * depth * PIECE, 128)
    unpack_small(flat_all, lengths, piece_refs[-1].shape[0] // 128, vec_ref, rpe_ref)
    along(4)
    begin(6)
    whole(1)
    first(3)
    scale = 64 ** (-0.25)

    def serve_pair(pair, side):
        for (work, number), steps in plan.items():
            if work == "head" and number % 2 == side:

                @pl.when(pair == number // 2)
                def _(steps=steps):
                    for step, item in steps:
                        step(item)

    def group_step(group):
        serve("project", group)
        wide_ref[...] = mm(tokens_ref[...], flat_qkv[group])
        for part in range(3):
            where = pl.ds(pl.multiple_of(part * breadth + group * tile, tile), tile)
            value = wide_ref[:, part * tile : part * tile + tile] + vec_ref[0:1, where]
            if part < 2:
                scaled = value * scale
                scaled_ref[:, where] = scaled
                operand = jnp.concatenate(two_parts(scaled) + two_parts(scaled * scaled), axis=1)
                value = jnp.exp(mm(operand, stack_ref[group])) * 0.125
                phi_ref[:, where] = value
            low_ref[:, where] = value.astype(LOW)

        def pair_step(inner):
            pair = 2 * group + inner
            attend_pair(
                pair, cols(pair, 128), pl.ds(pl.multiple_of(pair * 128 + breadth, 128), 128),
                pl.ds(pl.multiple_of(pair * 128 + 2 * breadth, 128), 128),
                low_ref, rpe_ref, mask_ref, den_ref, ctx_ref, ctx_low_ref, coef_ref, key_ref, score_ref, serve_pair,
            )

        each(2, pair_step)

    each(groups, group_step)
    keep(0, 1, 2, 3, 4, 5)
    along(10)
    whole(7)
    wide_ref[...] = mm(ctx_low_ref[...], flat_out[...]) + vec_ref[2:3, :breadth]
    norm_forward(tokens_ref, wide_ref, vec_ref, xhat_ref, inverse_ref, normed_ref, normed_low_ref)
    keep(6, 7, 8)

    def upward_step(index):
        serve("up", index)
        where = cols(index, up_tile)
        upward_tile(normed_low_ref, flat_up.at[index], vec_ref[1:2, where], act_ref, slope_ref, where)

    each(groups, upward_step)
    keep(9, 10)

    def downward_step(index):
        serve("down", index)
        where = cols(index, down_tile)
        wide_ref[:, where] = mm(act_ref[...], flat_down[index]) + vec_ref[5:6, where]

    each(groups, downward_step)
    norm_result(seq_ref, normed_ref, wide_ref, vec_ref, cot_ref, out_ref, wide_ref, gvec_ref)
    gather.sent(len(full) - 1)
    saver.finish()


def ahead_call(depth, seq, tokens, cotangent, feat, matrices, pieces):
    rows, breadth = tokens.shape
    span_length = 2 * rows
    devices = 8 * depth
    groups, tile = 3, 256
    slots = depth - 1 + 1 + 2 + 4
    longest = max(piece.shape[1] for piece in pieces[:-1]) * devices
    table = pieces[-1].shape[0] * devices // 128
    w_qkv, w_out, w_up, w_down = matrices
    hidden = w_up.shape[1]
    lead = (depth, 4)
    full = [
        (groups,) + lead + (2 * w_qkv.shape[0], 3 * tile), lead + (2 * w_out.shape[0], breadth),
        (groups,) + lead + (2 * w_up.shape[0], hidden // groups),
        (groups,) + lead + (2 * w_down.shape[0], breadth // groups),
    ]
    saved = [(groups, breadth, 3 * tile), (breadth, breadth), (devices * w_up.shape[0], hidden), (devices * w_down.shape[0], breadth)]
    kept = [
        ((rows, 2 * breadth), F32), ((rows, 2 * breadth), F32), ((rows, 3 * breadth), LOW),
        ((rows, breadth), F32), ((rows, breadth), F32), ((rows, breadth), LOW),
        ((rows, breadth), LOW), ((rows, breadth), F32), ((rows, 128), F32), ((rows, hidden), LOW),
        ((rows, hidden), F32),
    ]
    items = 2 + 3 * groups
    return pl.pallas_call(
        functools.partial(ahead_kernel, depth, len(pieces)),
        out_shape=(
            shape((rows, breadth), LOW), shape((len(pieces) - 1, longest), F32),
            shape((len(pieces) - 1, longest), F32), shape((table, 128), F32), shape((rows, breadth), F32),
        )
        + tuple(shape(dims, LOW) for dims in saved)
        + tuple(shape(dims, kind) for dims, kind in kept),
        in_specs=[SCALARS] + vmem(3 + len(matrices) + len(pieces)),
        out_specs=tuple(vmem(5)) + (ANYWHERE,) * len(saved + kept),
        scratch_shapes=[pltpu.VMEM(dims, LOW) for dims in full]
        + [pltpu.VMEM(dims, kind) for dims, kind in kept]
        + [pltpu.VMEM(matrix.shape, F32) for matrix in matrices]
        + [
            pltpu.VMEM((PIECE, 128), F32), pltpu.VMEM((depth, 4, 2, PIECE, 128), F32),
            pltpu.VMEM((rows, rows), F32), pltpu.VMEM((groups, 4 * tile, tile), LOW),
            pltpu.VMEM((128, span_length), F32), pltpu.VMEM((rows, 128), LOW), pltpu.VMEM((rows, rows), LOW),
            pltpu.VMEM((rows, breadth), F32),
            pltpu.SemaphoreType.DMA((items, slots)), pltpu.SemaphoreType.DMA((items, slots)),
            pltpu.SemaphoreType.DMA((1, 4)), pltpu.SemaphoreType.DMA((1, 4)), pltpu.SemaphoreType.DMA((items - 1 + len(kept),)),
        ],
        compiler_params=pltpu.CompilerParams(
            collective_id=0, has_side_effects=True, vmem_limit_bytes=60 * MIB
        ),
        name="ahead",
    )(seq, tokens, cotangent, feat, *matrices, *pieces)


def prepare_back(group, slot, low_ref, den_ref, ctx_ref, g_ctx_ref, swap_ref, ext_ref, key_ref, val_ref, num_ref, flip_ref):
    rows = g_ctx_ref.shape[0]
    breadth = swap_ref.shape[0]
    where = cols(group, breadth)
    lane = jnp.bitwise_and(iota((128, breadth), 1), 127)
    lower = lane < 64

    def step(index):
        at = pl.ds(pl.multiple_of(index * 128, 128), 128)
        g_num = g_ctx_ref[at, where] * (1.0 / den_ref[slot, at, :])
        g_den = -mm2(g_num * ctx_ref[slot, at, :], swap_ref[...])
        high = g_den.astype(LOW).astype(F32)
        rest = g_den - high
        key = low_ref[slot, 1, at, :].astype(F32)
        value = low_ref[slot, 2, at, :].astype(F32)
        for side in range(2):
            mine = jnp.logical_not(lower) if side else lower
            other = 0 if side else 64
            is_high, is_rest = lane == other, lane == other + 1
            extended = jnp.where(mine, g_num, jnp.where(is_high, high, jnp.where(is_rest, rest, 0.0)))
            ext_ref[side, at, :] = extended.astype(LOW)
            key_ref[side, at, :] = jnp.where(mine, key, 0.0).astype(LOW)
            ones = jnp.where(jnp.logical_or(is_high, is_rest), 1.0, 0.0)
            val_ref[side, at, :] = jnp.where(mine, value, ones).astype(LOW)
        num_ref[at, :] = g_num.astype(LOW)

    each(rows // 128, step)
    flip_ref[0] = jnp.transpose(low_ref[slot, 0])
    flip_ref[1] = jnp.transpose(num_ref[...])


def attend_back_pair(
    pair, inner, slot, low_ref, rpe_ref, mask_ref, g_feat_ref, grpe_ref, coef_ref, scores_ref, gk_ref, diag_ref,
    ext_ref, key_ref, val_ref, flip_ref, turn_ref, serve,
):
    rows = mask_ref.shape[0]
    tall = BLOCK_ROWS
    here = cols(inner, 128)
    lower = iota((tall, 128), 1) < 64
    for side in range(2):
        serve(pair, side)
        coefficients(rpe_ref, pair * 2 + side, coef_ref)
        diag_ref[...] = jnp.zeros_like(diag_ref)
        for block in range(rows // tall):
            at = slice(block * tall, block * tall + tall)
            kernel = mm(low_ref[slot, 0, at, here], key_ref[side, :, here], 1, 1)
            g_scores = mm(ext_ref[side, at, here], val_ref[side, :, here], 1, 1)
            for part in range(tall // 128):
                start = block * tall + part * 128
                lead = rows - 128 - start
                inside = slice(part * 128, part * 128 + 128)
                weight = coef_ref[:, lead : lead + rows] * mask_ref[start : start + 128, :]
                scores = kernel[inside] * weight
                diag_ref[:, lead : lead + rows] += g_scores[inside] * scores
                scores_ref[start : start + 128, :] = scores.astype(LOW)
                gk_ref[start : start + 128, :] = (g_scores[inside] * weight).astype(LOW)
            g_query = mm(gk_ref[at, :], low_ref[slot, 1, :, here])
            if side:
                g_query = jnp.where(lower, g_feat_ref[at, here], g_query)
            g_feat_ref[at, here] = g_query
        head_rows = pl.ds(pl.multiple_of(inner * 128 + side * 64, 64), 64)
        turn_ref[0, head_rows, :] = mm(flip_ref[0, head_rows, :], gk_ref[...])
        turn_ref[1, head_rows, :] = mm(flip_ref[1, head_rows, :], scores_ref[...])
        diagonals(diag_ref, grpe_ref, pair * 2 + side)


def diagonals(diag_ref, out_ref, head):
    flip = jnp.where(iota((128, 128), 0) + iota((128, 128), 1) == 127, 1.0, 0.0).astype(LOW)
    value = diag_ref[...]
    high = value.astype(LOW)
    rest = (value - high.astype(F32)).astype(LOW)
    value = pltpu.roll(mm(flip, high) + mm(flip, rest), 0, axis=1, stride=1, stride_axis=0)
    sums = jnp.sum(value, axis=0, keepdims=True)
    for k in range(8):
        out_ref[pl.ds(head * 8 + 7 - k, 1), :] = sums[:, 128 * k : 128 * k + 128]


class Item:
    def __init__(self, given, buffers, row):
        self.given = given
        self.from_core, self.from_second, self.from_first, self.from_depth, self.leaving = buffers
        self.row = row


class Scatter:
    def __init__(self, plane, sems):
        self.plane, self.sems = plane, sems
        self.here = plane.spot(plane.first, plane.second)
        self.across = plane.spot(1 - plane.first, plane.second)
        self.first_slot = plane.depth - 1
        self.second_slot = self.first_slot + 1
        self.core_slot = self.second_slot + 2
        self.last_slot = self.core_slot + 1

    def with_core(self, item):
        return remote(
            half(item.given, ALL, ALL, 1 - self.plane.core), item.from_core, self.sems, item.row, self.core_slot,
            self.plane.sibling,
        )

    def begin(self, item):
        self.with_core(item).start()

    def to_second(self, item, first):
        spot = self.plane.spot(first, 1 - self.plane.second)
        return remote(
            half(item.given, ALL, spot, self.plane.core), item.from_second.at[first], self.sems, item.row,
            self.second_slot + first, self.plane.over_second,
        )

    def to_first(self, item):
        return remote(
            half(item.given, ALL, self.across, self.plane.core), item.from_first, self.sems, item.row,
            self.first_slot, self.plane.over_first,
        )

    def to_depth(self, item, distance):
        plane = self.plane
        z = plane.ahead(distance)
        return remote(
            half(item.given, z, self.here, plane.core), item.from_depth.at[distance - 1], self.sems, item.row,
            distance - 1, plane.device(z, plane.first, plane.second),
        )

    def join(self, item, spot, piece):
        def step(z):
            target = half(item.given, z, spot, self.plane.core)
            target[...] = target[...] + piece(z)

        each(self.plane.depth, step)

    def core(self, item):
        plane = self.plane
        self.with_core(item).wait_recv()
        for first in range(2):
            spot = plane.spot(first, 1 - plane.second)
            self.join(item, spot, lambda z, spot=spot: item.from_core[z, spot])
            self.to_second(item, first).start()
        for first in range(2):
            spot = plane.spot(first, plane.second)
            self.join(item, spot, lambda z, spot=spot: item.from_core[z, spot])

    def second(self, item):
        plane = self.plane
        away = 1 - plane.first
        self.to_second(item, away).wait_recv()
        self.join(item, self.across, lambda z: item.from_second[away, z])
        self.to_first(item).start()
        self.to_second(item, plane.first).wait_recv()
        self.join(item, self.here, lambda z: item.from_second[plane.first, z])

    def first(self, item):
        self.to_first(item).wait_recv()
        self.join(item, self.here, lambda z: item.from_first[z])
        for distance in range(1, self.plane.depth):
            self.to_depth(item, distance).start()

    def summed(self, item):
        plane = self.plane
        for distance in range(1, plane.depth):
            self.to_depth(item, distance).wait_recv()
        value = half(item.given, plane.z, self.here, plane.core)[...].astype(F32)
        for distance in range(1, plane.depth):
            value = value + item.from_depth[distance - 1].astype(F32)
        return value

    def columns(self, item, core):
        breadth = item.leaving.shape[1]
        return pl.ds(pl.multiple_of(core * breadth, 128), breadth)

    def last(self, item, target):
        core = self.plane.core
        return remote(
            item.leaving, target.at[:, self.columns(item, core)], self.sems, item.row, self.last_slot,
            self.plane.sibling,
        )

    def along(self, item, target):
        core = self.plane.core
        value = self.summed(item)
        height = value.shape[0] // 2
        upper, lower = value[:height], value[height:]
        target[:, self.columns(item, core)] = jnp.where(core == 0, upper, lower)
        item.leaving[...] = jnp.where(core == 0, lower, upper)
        self.last(item, target).start()

    def sent(self, item, target=None):
        self.with_core(item).wait_send()
        for first in range(2):
            self.to_second(item, first).wait_send()
        self.to_first(item).wait_send()
        for distance in range(1, self.plane.depth):
            self.to_depth(item, distance).wait_send()
        if target is not None:
            core = self.plane.core
            self.last(item, target).wait_send()
            arrived = target.at[:, self.columns(item, 1 - core)]
            remote(
                item.leaving, arrived, self.sems, item.row, self.last_slot, self.plane.sibling
            ).wait_recv()


def pack_grads(gvec_ref, lengths, grpe_ref, flat_ref):
    devices = flat_ref.shape[0] // PIECE
    table_rows = grpe_ref.shape[0] // devices
    flat_ref[...] = jnp.zeros_like(flat_ref)
    for row, length in enumerate(lengths):
        breadth = length * devices
        value = gvec_ref[row : row + 1, 0:breadth]
        spread = jnp.where(owned(devices, length, breadth), jnp.broadcast_to(value, (devices, breadth)), 0.0)
        flat_ref[pl.ds(row, devices, stride=PIECE), :] = mm2(spread, one_hot(length, breadth), 1)
    for part in range(table_rows):
        flat_ref[pl.ds(len(lengths) + part, devices, stride=PIECE), :] = grpe_ref[
            pl.ds(part, devices, stride=table_rows), :
        ]


def build_back(feat_ref, stack_ref):
    tile = stack_ref.shape[2]
    head_size = feat_ref.shape[1]
    group = tile // head_size
    bits = head_size.bit_length() - 1
    same = lax.shift_right_logical(iota((tile, tile), 0), bits) == lax.shift_right_logical(iota((tile, tile), 1), bits)
    last = stack_ref.shape[0] - 1
    for index in range(last):
        rows_of = []
        for inner in range(group):
            piece = jnp.transpose(feat_ref[index * group + inner].astype(F32))
            rows_of.append(jnp.concatenate([piece] * group, axis=1))
        full = jnp.where(same, jnp.concatenate(rows_of, axis=0), 0.0).astype(LOW)
        for part in range(2):
            stack_ref[index, part * tile : part * tile + tile, :] = full
    for part in range(2):
        stack_ref[last, part * tile : part * tile + tile, :] = jnp.where(same, 1.0, 0.0).astype(LOW)


def build_swap(swap_ref):
    tile = swap_ref.shape[0]
    down = lax.shift_right_logical(iota((tile, tile), 0), 6)
    across = lax.shift_right_logical(iota((tile, tile), 1), 6)
    swap_ref[...] = jnp.where(jnp.bitwise_xor(down, 1) == across, 1.0, 0.0).astype(LOW)


def behind_kernel(depth, lengths, *refs):
    seq_ref, feat_ref, vec_ref, rpe_ref, gvec_in_ref, g_sum_ref, refs = refs[:6] + (refs[6:],)
    w_qkv_hbm, w_out_hbm, w_up_hbm, w_down_hbm, refs = refs[:4] + (refs[4:],)
    scaled_hbm, phi_hbm, low_hbm, den_hbm, ctx_hbm, ctx_low_hbm, refs = refs[:6] + (refs[6:],)
    normed_low_hbm, xhat_hbm, inverse_hbm, act_hbm, slope_hbm, tokens_hbm, refs = refs[:6] + (refs[6:],)
    g_tokens_hbm, s_qkv, s_out, s_up, s_down, s_small, refs = refs[:6] + (refs[6:],)
    d_qkv, d_out, d_up, d_down, d_small, refs = refs[:5] + (refs[5:],)
    buffers, refs = [refs[5 * index : 5 * index + 5] for index in range(5)], refs[25:]
    g_hidden_ref, g_ctx_ref, g_low_ref, gvec_ref, grpe_ref, g_qkv_ref, refs = refs[:6] + (refs[6:],)
    send, recv, load_sem = refs
    rows, breadth = g_sum_ref.shape
    hidden = w_up_hbm.shape[1]
    tile, height = 256, 128
    wide = min(768, breadth)
    plane = Plane(depth)
    scatter = Scatter(plane, (send, recv))
    down, up, out = [
        Item(given, buffers[index], 2 - index)
        for given, index in ((d_down, 2), (d_up, 1), (d_out, 0))
    ]
    small = Item(d_small, buffers[4], 3)
    flat_down, flat_up, flat_out, flat_qkv = d_down.reshape(hidden, breadth), d_up.reshape(breadth, hidden), (
        d_out.reshape(breadth, breadth)
    ), d_qkv.reshape(breadth // tile, breadth, 3 * tile)
    flat_small = d_small.reshape(8 * depth * PIECE, 128)

    def qkv(group):
        return Item(d_qkv.at[group], [buffer.at[group] for buffer in buffers[3]], 4 + group)

    def load(source, target, index):
        return pltpu.make_async_copy(source, target, load_sem.at[index])

    def feed_forward(
        w_out_ref, w_up_ref, w_down_ref, act_ref, slope_ref, normed_low_ref, flip_ref,
        inverse_ref, ctx_low_ref,
    ):
        chunk = slope_ref.shape[2]
        chunks = hidden // chunk
        pending = {}

        def columns(index):
            return slice(index * chunk, index * chunk + chunk)

        acts = [
            load(act_hbm.at[:, columns(index)], act_ref.at[:, columns(index)], 2 * chunks + index)
            for index in range(chunks)
        ]

        def fetch(index):
            at = columns(index)
            pending[index] = [
                load(w_down_hbm.at[at, :], w_down_ref.at[at, :], 2 * index),
                load(slope_hbm.at[:, at], slope_ref.at[index % 2], 2 * index + 1),
            ]
            for copy in pending[index]:
                copy.start()

        for copy in acts:
            copy.start()
        fetch(0)
        fetch(1)
        base = 3 * chunks
        later = [
            load(normed_low_hbm, normed_low_ref, base), load(w_up_hbm, w_up_ref, base + 1),
            load(xhat_hbm, g_hidden_ref, base + 2), load(inverse_hbm, inverse_ref, base + 3),
            load(w_out_hbm, w_out_ref, base + 4), load(ctx_low_hbm, ctx_low_ref, base + 5),
        ]
        g_low_ref[...] = g_sum_ref[...].astype(LOW)
        gvec_ref[...] = gvec_in_ref[...]
        plane.greet()
        for index in range(chunks):
            acts[index].wait()

            at = columns(index)
            flat_down[at, :] = mm(act_ref[:, at], g_low_ref[...], 0, 0).astype(LOW)
        scatter.begin(down)
        for index in range(chunks):
            for copy in pending[index]:
                copy.wait()
            if index == 2:
                scatter.core(down)

            at = columns(index)
            g_upward = mm(g_low_ref[...], w_down_ref[at, :], 1, 1) * slope_ref[index % 2]
            gvec_ref[1:2, at] = column_sum(g_upward)
            act_ref[:, at] = g_upward.astype(LOW)
            if index + 2 < chunks:
                fetch(index + 2)
            if index == 0:
                for copy in later:
                    copy.start()
        for copy in later:
            copy.wait()
        flip_ref[...] = jnp.transpose(normed_low_ref[...])

        def up_step(step):
            where = cols(step, wide)
            flat_up[:, where] = mm(flip_ref[...], act_ref[:, where]).astype(LOW)

        each(hidden // wide, up_step)
        scatter.begin(up)

        g_sum_ref[...] = mm(act_ref[...], w_up_ref[...], 1, 1) + g_sum_ref[...]
        gain_one = vec_ref[3:4, :breadth]

        def first_back(step):
            at = pl.ds(pl.multiple_of(step * height, height), height)
            g_normed = g_sum_ref[at, :]
            xhat = g_hidden_ref[at, :]
            add_to(gvec_ref, 3, column_sum(g_normed * xhat))
            add_to(gvec_ref, 4, column_sum(g_normed))
            g_hidden = norm_back(g_normed, xhat, inverse_ref[at, 0:1], gain_one)
            add_to(gvec_ref, 2, column_sum(g_hidden))
            g_hidden_ref[at, :] = g_hidden
            g_low_ref[at, :] = g_hidden.astype(LOW)

        each(rows // height, first_back)

        flat_out[...] = mm(ctx_low_ref[...], g_low_ref[...], 0, 0).astype(LOW)
        scatter.begin(out)
        scatter.core(up)
        scatter.second(down)
        g_ctx_ref[...] = mm(g_low_ref[...], w_out_ref[...], 1, 1)

    chunk = min(768, hidden)
    pl.run_scoped(
        feed_forward,
        pltpu.VMEM(w_out_hbm.shape, LOW), pltpu.VMEM(w_up_hbm.shape, LOW), pltpu.VMEM(w_down_hbm.shape, LOW),
        pltpu.VMEM((rows, hidden), LOW), pltpu.VMEM((2, rows, chunk), F32),
        pltpu.VMEM((rows, breadth), LOW), pltpu.VMEM((breadth, rows), LOW),
        pltpu.VMEM((rows, 128), F32), pltpu.VMEM((rows, breadth), LOW),
    )

    calls = {
        4: (lambda: scatter.core(out), lambda: scatter.first(down)),
        7: (lambda: scatter.second(up),),
        9: (lambda: scatter.core(qkv(0)), lambda: scatter.first(up)),
        11: (lambda: scatter.second(out), lambda: scatter.core(qkv(1))),
    }

    def serve(pair, side):
        for head, steps in calls.items():
            if head % 2 == side:

                @pl.when(pair == head // 2)
                def _(steps=steps):
                    for step in steps:
                        step()

    def attention(
        w_qkv_ref, flip_ref, scaled_ref, phi_ref, low_ref, den_ref, ctx_ref, g_feat_ref, coef_ref,
        scores_ref, gk_ref, diag_ref, ext_ref, key_ref, val_ref, num_ref, turn_low_ref, turn_ref, swap_ref, mask_ref, stack_ref,
    ):
        groups = breadth // tile

        def part(ref, at, number):
            return ref.at[:, pl.ds(pl.multiple_of(at * tile + number * breadth, tile), tile)]

        def loads(group):
            slot = lax.rem(group, 2)
            copies = []
            for number in range(3):
                copies.append((part(low_hbm, group, number), low_ref.at[slot, number]))
            copies.append((part(den_hbm, group, 0), den_ref.at[slot]))
            copies.append((part(ctx_hbm, group, 0), ctx_ref.at[slot]))
            for number in range(2):
                copies.append((part(scaled_hbm, group, number), scaled_ref.at[slot, number]))
                copies.append((part(phi_hbm, group, number), phi_ref.at[slot, number]))
            return [
                load(source, target, slot * 9 + index) for index, (source, target) in enumerate(copies)
            ]

        base = 18
        tokens_copy = load(tokens_hbm, g_low_ref, base)

        def weights(group):
            return load(w_qkv_hbm.at[group], w_qkv_ref.at[group % 2], base + 1 + group)

        for copy in loads(0):
            copy.start()
        for copy in (tokens_copy, weights(0), weights(1)):
            copy.start()
        segment_mask(seq_ref, mask_ref)
        build_back(feat_ref, stack_ref)
        tokens_copy.wait()
        flip_ref[...] = jnp.transpose(g_low_ref[...])
        build_swap(swap_ref)
        scale = 64 ** (-0.25)

        def group_step(group):
            slot = lax.rem(group, 2)
            for copy in loads(group):
                copy.wait()

            @pl.when(group + 1 < groups)
            def _():
                for copy in loads(group + 1):
                    copy.start()

            prepare_back(
                group, slot, low_ref, den_ref, ctx_ref, g_ctx_ref, swap_ref, ext_ref, key_ref, val_ref, num_ref,
                turn_low_ref,
            )

            def pair_step(inner):
                pair = 2 * group + inner
                attend_back_pair(
                    pair, inner, slot, low_ref, rpe_ref, mask_ref, g_feat_ref, grpe_ref, coef_ref, scores_ref,
                    gk_ref, diag_ref, ext_ref, key_ref, val_ref, turn_low_ref, turn_ref, serve,
                )

            each(2, pair_step)

            g_feat_ref[:, tile : 2 * tile] = jnp.transpose(turn_ref[0])
            g_feat_ref[:, 2 * tile : 3 * tile] = jnp.transpose(turn_ref[1])
            for number in range(3):
                at = slice(number * tile, number * tile + tile)
                where = pl.ds(pl.multiple_of(group * tile + number * breadth, tile), tile)
                grad = g_feat_ref[:, at]
                if number < 2:
                    upward = jnp.concatenate(two_parts(grad * phi_ref[slot, number]), axis=1)
                    total = mm(upward, stack_ref[groups])
                    grad = mm(upward, stack_ref[group]) - scaled_ref[slot, number] * total
                    grad = grad * scale
                gvec_ref[0:1, where] = column_sum(grad)
                g_qkv_ref[group, :, at] = grad.astype(LOW)
            flat_qkv[group] = mm(flip_ref[...], g_qkv_ref[group]).astype(LOW)
            scatter.begin(qkv(group))

        each(groups, group_step)
        scatter.second(qkv(0))
        scatter.core(qkv(2))
        scatter.along(down, s_down)
        scatter.first(out)
        scatter.first(qkv(0))
        flip = jnp.where(iota((128, 128), 0) + iota((128, 128), 1) == 127, 1.0, 0.0).astype(LOW)
        grpe_ref[...] = mm2(grpe_ref[...], flip)
        pack_grads(gvec_ref, lengths, grpe_ref, flat_small)
        scatter.begin(small)
        scatter.second(qkv(1))

        def inputs(group):
            weights(group).wait()
            g_hidden_ref[...] += mm(g_qkv_ref[group], w_qkv_ref[group % 2], 1, 1)
            if group + 2 < groups:
                weights(group + 2).start()

        inputs(0)
        inputs(1)
        scatter.core(small)
        inputs(2)

    pl.run_scoped(
        attention,
        pltpu.VMEM((2,) + w_qkv_hbm.shape[1:], LOW), pltpu.VMEM((breadth, rows), LOW),
        pltpu.VMEM((2, 2, rows, tile), F32), pltpu.VMEM((2, 2, rows, tile), F32),
        pltpu.VMEM((2, 3, rows, tile), LOW), pltpu.VMEM((2, rows, tile), F32), pltpu.VMEM((2, rows, tile), F32),
        pltpu.VMEM((rows, 3 * tile), F32), pltpu.VMEM((128, 2 * rows), F32), pltpu.VMEM((rows, rows), LOW),
        pltpu.VMEM((rows, rows), LOW), pltpu.VMEM((128, 2 * rows), F32), pltpu.VMEM((2, rows, tile), LOW),
        pltpu.VMEM((2, rows, tile), LOW), pltpu.VMEM((2, rows, tile), LOW), pltpu.VMEM((rows, tile), LOW),
        pltpu.VMEM((2, tile, rows), LOW), pltpu.VMEM((2, tile, rows), F32), pltpu.VMEM((tile, tile), LOW),
        pltpu.VMEM((rows, rows), F32), pltpu.VMEM((breadth // tile + 1, 2 * tile, tile), LOW),
    )
    result = load(g_hidden_ref, g_tokens_hbm, 31)
    result.start()
    scatter.second(qkv(2))
    scatter.first(qkv(1))
    scatter.second(small)
    scatter.along(out, s_out)
    scatter.along(up, s_up)
    scatter.first(small)
    scatter.first(qkv(2))
    scatter.sent(down, s_down)
    scatter.along(qkv(1), s_qkv.at[1])
    scatter.along(qkv(0), s_qkv.at[0])
    scatter.sent(up, s_up)
    scatter.sent(out, s_out)
    scatter.along(qkv(2), s_qkv.at[2])
    s_small[...] = scatter.summed(small)
    scatter.sent(small)
    for group in range(breadth // tile):
        scatter.sent(qkv(group), s_qkv.at[group])
    result.wait()


def behind_call(depth, seq, feat, vec, rpe, gvec, g_sum, weights, kept, tokens, lengths):
    rows, breadth = tokens.shape
    chips = 4 * depth
    devices = 2 * chips
    w_qkv, w_out, w_up, w_down = weights
    group = 3 * 256
    groups = w_qkv.shape[0]
    table = rpe.shape[0]
    blocks = [(w.shape[0] // devices, w.shape[1]) for w in (w_out, w_up, w_down)]
    lead = (depth, 4)
    given = [lead + (2 * block[0], block[1]) for block in blocks]
    qkv_block = (w_qkv.shape[1] // devices, group)

    def buffers(block, kind, front=()):
        if kind == LOW:
            part, leaving = (2 * block[0], block[1] // 2), (block[0], block[1] // 2)
        else:
            part, leaving = block, (8, 128)
        numbers = [lead, (2, depth), (depth,), (depth - 1,)]
        return [pltpu.VMEM(front + number + part, kind) for number in numbers] + [pltpu.VMEM(front + leaving, F32)]

    slots = depth - 1 + 1 + 2 + 2
    scratch = [pltpu.VMEM((groups,) + lead + (2 * qkv_block[0], group), LOW)]
    scratch += [pltpu.VMEM(dims, LOW) for dims in given]
    scratch += [pltpu.VMEM(lead + (2, PIECE, 128), F32)]
    for block in blocks:
        scratch += buffers(block, LOW)
    scratch += buffers(qkv_block, LOW, (groups,)) + buffers((PIECE, 128), F32)
    scratch += [
        pltpu.VMEM((rows, breadth), F32), pltpu.VMEM((rows, breadth), F32), pltpu.VMEM((rows, breadth), LOW),
        pltpu.VMEM(vec.shape, F32), pltpu.VMEM((table, 128), F32), pltpu.VMEM((groups, rows, group), LOW),
        pltpu.SemaphoreType.DMA((7, slots)), pltpu.SemaphoreType.DMA((7, slots)), pltpu.SemaphoreType.DMA((32,)),
    ]
    return pl.pallas_call(
        functools.partial(behind_kernel, depth, lengths),
        out_shape=(
            shape((rows, breadth), F32), shape((groups,) + qkv_block, F32),
        ) + tuple(shape(block, F32) for block in blocks) + (shape((PIECE, 128), F32),),
        in_specs=[SCALARS] + vmem(5) + [ANYWHERE] * (4 + len(kept) + 1),
        out_specs=(ANYWHERE,) + tuple(vmem(5)),
        scratch_shapes=scratch,
        compiler_params=pltpu.CompilerParams(
            collective_id=1, has_side_effects=True, vmem_limit_bytes=62 * MIB
        ),
        name="behind",
    )(seq, feat, vec, rpe, gvec, g_sum, *weights, *kept, tokens)


def emit_kernel(count, lengths, *refs):
    big, small_hbm, refs = refs[:count], refs[count], refs[count + 1 :]
    outs, refs = refs[:count], refs[count:]
    number = len(lengths) + 1
    targets, refs = refs[:number], refs[number:]
    held, pieces, small, sems, piece_sems = refs[:count], refs[count : count + number], refs[-3], refs[-2], refs[-1]
    arrive = pltpu.make_async_copy(small_hbm, small, piece_sems.at[number])
    arrive.start()
    leave = [
        pltpu.make_async_copy(piece, target, piece_sems.at[index])
        for index, (piece, target) in enumerate(zip(pieces, targets))
    ]
    inward, owners = [], []
    for index in range(count):
        if len(big[index].shape) == 3:
            groups, _, breadth = big[index].shape
            tile = breadth // 3
            for group in range(groups):
                for part in range(3):
                    start = part * breadth + group * tile
                    source = big[index].at[group, :, part * tile : part * tile + tile]
                    inward.append((source, held[index].at[:, start : start + tile]))
                    owners.append(index)
        else:
            inward.append((big[index], held[index]))
            owners.append(index)
    inward = [
        pltpu.make_async_copy(source, target, sems.at[0, index]) for index, (source, target) in enumerate(inward)
    ]
    outward = [pltpu.make_async_copy(held[index], outs[index], sems.at[1, index]) for index in range(count)]
    for copy in inward:
        copy.start()
    arrive.wait()
    for row, length in enumerate(lengths):
        pieces[row][...] = small[row : row + 1, 0:length]
    table = pieces[-1]
    for part in range(table.shape[0] // 128):
        row = len(lengths) + part
        table[128 * part : 128 * part + 128] = small[row : row + 1, :].reshape(128)
    for copy in leave:
        copy.start()
    for index in range(count):
        for owner, copy in zip(owners, inward):
            if owner == index:
                copy.wait()
        outward[index].start()
    for copy in outward + leave:
        copy.wait()


def emit_call(arrays, small, lengths, table):
    shapes = [
        (array.shape[1], array.shape[0] * array.shape[2]) if len(array.shape) == 3 else array.shape for array in arrays
    ]
    result = pl.pallas_call(
        functools.partial(emit_kernel, len(arrays), lengths),
        out_shape=tuple(shape(dims, array.dtype) for dims, array in zip(shapes, arrays))
        + tuple(shape((1, length), F32) for length in lengths) + (shape((table,), F32),),
        in_specs=[ANYWHERE] * (len(arrays) + 1),
        out_specs=(ANYWHERE,) * (len(arrays) + len(lengths) + 1),
        scratch_shapes=[pltpu.VMEM(dims, array.dtype) for dims, array in zip(shapes, arrays)]
        + [pltpu.VMEM((1, length), F32) for length in lengths]
        + [
            pltpu.VMEM((table,), F32), pltpu.VMEM(small.shape, F32), pltpu.SemaphoreType.DMA((2, len(arrays) + 8)),
            pltpu.SemaphoreType.DMA((len(lengths) + 2,)),
        ],
        compiler_params=pltpu.CompilerParams(vmem_limit_bytes=60 * MIB),
        name="emit",
    )(*arrays, small)
    return result[: len(arrays)], [piece.reshape(-1) for piece in result[len(arrays) :]]


def plain_gather(value):
    return lax.all_gather(value.astype(LOW), "dp", axis=0, tiled=True)


def plain_scatter(value):
    return lax.psum_scatter(value.astype(F32), "dp", scatter_dimension=0, tiled=True)


def body(
    depth, tokens, cotangent, seq_lengths, random_feat, w_qkv, b_qkv, w_out, b_out, ln1_gain, ln1_bias,
    w_up, b_up, w_down, b_down, ln2_gain, ln2_bias, rpe_table,
):
    vectors = (b_qkv, b_up, b_out, ln1_gain, ln1_bias, b_down, ln2_gain, ln2_bias)
    matrices = (w_qkv, w_out, w_up, w_down)
    lengths = tuple(piece.shape[0] for piece in vectors)
    if depth:
        pieces = [piece.reshape(1, -1) for piece in vectors] + [rpe_table]
        result = ahead_call(depth, seq_lengths, tokens, cotangent, random_feat, matrices, pieces)
        out, gvec, vec, rpe = result[:4]
        g_sum, weights, kept = result[4], result[5:9], result[9:]
        g_tokens, s_qkv, s_out, s_up, s_down, small = behind_call(
            depth, seq_lengths, random_feat, vec, rpe, gvec, g_sum, weights, kept, tokens, lengths
        )
        arrays, pieces = emit_call(
            (out, g_tokens, s_qkv, s_out, s_up, s_down), small, lengths, rpe_table.shape[0]
        )
        out, g_tokens, s_qkv, s_out, s_up, s_down = arrays
    else:
        full_vectors = [plain_gather(piece).astype(F32) for piece in vectors]
        longest = max(piece.shape[0] for piece in full_vectors)
        vec = jnp.stack([jnp.pad(piece, (0, longest - piece.shape[0])) for piece in full_vectors])
        rpe = plain_gather(rpe_table).astype(F32).reshape(-1, 128)
        full_qkv, full_out, full_up, full_down = [plain_gather(piece) for piece in matrices]
        scaled, phi, low, den, ctx, ctx_low = forward_call(seq_lengths, tokens, random_feat, full_qkv, vec, rpe)
        out, g_hidden, g_ctx, d_out, d_up, d_down, gvec_one = middle_call(
            seq_lengths, tokens, cotangent, ctx_low, vec, full_out, full_up, full_down
        )
        g_tokens, d_qkv, gvec_two, grpe = backward_call(
            seq_lengths, tokens, random_feat, full_qkv, rpe, scaled, phi, low, den, ctx, g_ctx, g_hidden, vec
        )
        gvec = gvec_one + gvec_two
        s_qkv, s_out, s_up, s_down = [plain_scatter(grad) for grad in (d_qkv, d_out, d_up, d_down)]
        devices = lax.axis_size("dp")
        pieces = [plain_scatter(gvec[row, : length * devices]) for row, length in enumerate(lengths)]
        pieces.append(plain_scatter(grpe.reshape(-1)))
    p_qkv, p_up, p_out, p_gain_one, p_bias_one, p_down, p_gain_two, p_bias_two, p_rpe = pieces
    return (
        out, g_tokens, s_qkv, p_qkv, s_out, p_out, p_gain_one, p_bias_one, s_up, p_up, s_down, p_down,
        p_gain_two, p_bias_two, p_rpe,
    )


def solution(mesh):
    wide, flat = P("dp", None), P("dp")
    devices = mesh.shape["dp"]
    depth = devices // 8 if devices == 32 else 0
    in_specs = (
        wide, wide, wide, P(), wide, flat, wide, flat, flat, flat, wide, flat, wide, flat, flat, flat, flat,
    )
    out_specs = (
        wide, wide, wide, flat, wide, flat, flat, flat, wide, flat, wide, flat, flat, flat, flat,
    )
    return jax.shard_map(
        functools.partial(body, depth), mesh=mesh, in_specs=in_specs, out_specs=out_specs, check_vma=False
    )
```
